256 devices in a mesh: shot: 8 (over z_hi, core), brick: 32 (over y, x, z_lo).
Axes of the slice: x: 4, y: 4, z: 8 (z_hi: 4, z_lo: 2; z = z_hi * 2 + z_lo), core: 2. Of those that a mesh axis runs over, the one named last changes fastest.
Arguments:
- field_prev: float32 [8, 128, 256, 256], P('shot', 'brick'), may hold values from -6 to 6
- field_now: float32 [8, 128, 256, 256], P('shot', 'brick'), may hold values from -6 to 6
- diag_coef: float32 [3, 128, 256, 256], P(None, 'brick'), may hold values from 0.06 to 0.22
- cross_coef: float32 [3, 128, 256, 256], P(None, 'brick'), may hold values from -0.08 to 0.08
- green: bfloat16 [8, 4096, 4096], P('shot', None, 'brick'), may hold values from -0.09375 to 0.09375
- delays: int32 [8], replicated, may hold values from 0 to 8
- past: bfloat16 [8, 8, 4096], P(None, 'shot', 'brick'), may hold values from -6 to 6
- rec_cell: int32 [8, 4096], P('shot', 'brick'), may hold values from 0 to 262143
- emit_cell: int32 [8, 4096], P('shot', 'brick'), may hold values from 0 to 262143
Outputs:
- field_before: float32 [8, 128, 256, 256], P('shot', 'brick')
- field_after: float32 [8, 128, 256, 256], P('shot', 'brick')
- recorded: bfloat16 [3, 8, 4096], P(None, 'shot', 'brick')
The draws below stay inside these ranges and needn't reach their ends.
Inputs may be any that keep to these rules, and one draw needn't show every extreme that they name: `rec_cell`: entries of block b (points b * 128 to (b + 1) * 128 - 1) index cells of brick b, counted within the brick. `emit_cell`: entries of block b (points b * 128 to (b + 1) * 128 - 1) index cells of brick b, counted within the brick.
All inputs are finite; a program needn't handle non-finite values.
Results may differ from the reference program's by a relative error of at most 0.001.
Values may be sent and summed in bfloat16 or wider, within the bound.
No kernel may reach another device: no remote copies, remote signals or barrier semaphores. Data moves between devices by JAX's collectives and lax.ppermute only.
A program may use at most 64 MiB of HBM per device.

```python
import jax
import jax.numpy as jnp
from jax import lax

CX = 4
NY = 256
NZ = 256
REC_DEV = 128
EMIT_DEV = 128
HIST = 8
STEPS = 3
NX = 128
RECS = 4096
EMITS = 4096
SHOTS = 8
LAGS = 8


def set_ends(result, rng, low, largest):
    longest = result.shape.index(max(result.shape))
    spots = []
    for shift in (0, 1):
        where = [jax.random.randint(jax.random.fold_in(rng, axis), (), 0, length) for axis, length in enumerate(result.shape)]
        where[longest] = (where[longest] + shift) % result.shape[longest]
        spots.append(tuple(where))
    return result.at[spots[0]].set(low).at[spots[1]].set(largest)


def level_of(rng, dims, pieces, least, high):
    def one(dim, shards_of):
        draws = jax.random.uniform(jax.random.fold_in(jax.random.fold_in(rng, 6), dim), (shards_of,), jnp.float32, least / len(pieces), high / len(pieces))
        return jnp.repeat(jnp.exp(draws), dims[dim] // shards_of).reshape((-1,) + (1,) * (len(dims) - dim - 1))

    gain = one(*pieces[0])
    for cut in pieces[1:]:
        gain = gain * one(*cut)
    return gain


def bell_draw(rng, extent, spread, bound, pieces=(), kind=jnp.bfloat16):
    array = spread * jax.random.normal(rng, extent, jnp.float32)
    if pieces:
        array = array * level_of(rng, extent, pieces, -0.22, 0.18)
    return jnp.clip(array, -bound, bound).astype(kind)


def setup_inputs(seed: int = 0) -> dict:
    streams_of = jax.random.split(jax.random.key(seed), 10)
    return {
        "field_prev": bell_draw(streams_of[0], (SHOTS, NX, NY, NZ), 1.0, 6.0, ((0, 8), (1, 32)), jnp.float32),
        "field_now": bell_draw(streams_of[1], (SHOTS, NX, NY, NZ), 1.0, 6.0, ((0, 8), (1, 32)), jnp.float32),
        "diag_coef": jnp.clip(0.06 + 0.16 * jax.random.uniform(streams_of[2], (3, NX, NY, NZ), jnp.float32) ** level_of(streams_of[2], (3, NX, NY, NZ), ((1, 32),), -0.2, 0.2), 0.06, 0.22),
        "cross_coef": jnp.clip(jax.random.uniform(streams_of[3], (3, NX, NY, NZ), jnp.float32, -0.08, 0.08) * level_of(streams_of[3], (3, NX, NY, NZ), ((1, 32),), -0.4, 0.0), -0.08, 0.08),
        "green": bell_draw(streams_of[4], (LAGS, EMITS, RECS), RECS ** -0.5, 0.09375, ((0, 8), (2, 32))),
        "delays": set_ends(jax.random.randint(streams_of[5], (LAGS,), 0, HIST + 1), jax.random.fold_in(streams_of[5], 1), 0, HIST).astype(jnp.int32),
        "past": bell_draw(streams_of[6], (HIST, SHOTS, RECS), 1.0, 6.0, ((1, 8), (2, 32))),
        "rec_cell": set_ends(jax.random.randint(streams_of[7], (SHOTS, RECS), 0, CX * NY * NZ), jax.random.fold_in(streams_of[7], 1), 0, (CX * NY * NZ) - 1).astype(jnp.int32),
        "emit_cell": set_ends(jax.random.randint(streams_of[8], (SHOTS, EMITS), 0, CX * NY * NZ), jax.random.fold_in(streams_of[8], 1), 0, (CX * NY * NZ) - 1).astype(jnp.int32),
    }


def operate(padded, centre, diag_coef, cross_coef):
    width_x = centre.shape[1]
    width_y = centre.shape[2]
    width_z = centre.shape[3]

    def shifted(offset_x, offset_y, offset_z):
        return padded[:, 1 + offset_x:1 + offset_x + width_x, 1 + offset_y:1 + offset_y + width_y, 1 + offset_z:1 + offset_z + width_z]

    second = diag_coef[0] * (shifted(1, 0, 0) - 2.0 * centre + shifted(-1, 0, 0))
    second = second + diag_coef[1] * (shifted(0, 1, 0) - 2.0 * centre + shifted(0, -1, 0))
    second = second + diag_coef[2] * (shifted(0, 0, 1) - 2.0 * centre + shifted(0, 0, -1))
    mixed = cross_coef[0] * (shifted(1, 1, 0) - shifted(1, -1, 0) - shifted(-1, 1, 0) + shifted(-1, -1, 0))
    mixed = mixed + cross_coef[1] * (shifted(1, 0, 1) - shifted(1, 0, -1) - shifted(-1, 0, 1) + shifted(-1, 0, -1))
    mixed = mixed + cross_coef[2] * (shifted(0, 1, 1) - shifted(0, 1, -1) - shifted(0, -1, 1) + shifted(0, -1, -1))
    return second + 0.5 * mixed


def reference(field_prev, field_now, diag_coef, cross_coef, green, delays, past, rec_cell, emit_cell):
    brick_cells = CX * NY * NZ
    rec_global = ((jnp.arange(RECS) // REC_DEV) * brick_cells).astype(jnp.int32)[None, :] + rec_cell
    emit_global = ((jnp.arange(EMITS) // EMIT_DEV) * brick_cells).astype(jnp.int32)[None, :] + emit_cell
    shot_rows = jnp.arange(SHOTS).astype(jnp.int32)
    series = [past[position] for position in range(HIST)]
    earlier, current = field_prev, field_now
    recorded = []
    for moment in range(STEPS):
        flat_now = current.reshape(SHOTS, -1)
        sample = jnp.take_along_axis(flat_now, rec_global, axis=1).astype(jnp.bfloat16)
        series.append(sample)
        recorded.append(sample)
        stacked = jnp.stack(series)
        emission = jnp.zeros((SHOTS, EMITS), jnp.float32)
        for lag_index in range(LAGS):
            where_at = (HIST + moment - delays[lag_index]).astype(jnp.int32)
            chosen = lax.dynamic_index_in_dim(stacked, where_at, 0, keepdims=False)
            emission = emission + jnp.dot(chosen, green[lag_index].T, preferred_element_type=jnp.float32)
        padded = jnp.pad(current, ((0, 0), (1, 1), (1, 1), (1, 1)))
        following = 2.0 * current - earlier + operate(padded, current, diag_coef, cross_coef)
        flat_next = following.reshape(SHOTS, -1)
        flat_next = flat_next.at[shot_rows[:, None], emit_global].add(emission)
        earlier, current = current, flat_next.reshape(current.shape)
    return earlier, current, jnp.stack(recorded)
```

```python
import functools

import jax
import jax.numpy as jnp
from jax import lax
from jax.experimental import pallas as pl
from jax.experimental.pallas import tpu as pltpu
from jax.sharding import PartitionSpec as P

STEPS = 3
VMEM = pltpu.VMEM
SMEM = pltpu.SMEM


def spec(space):
    return pl.BlockSpec(memory_space=space)


def sheet_of(row, width):
    tall = jnp.transpose(jnp.broadcast_to(row, (128, 128)))
    return jnp.concatenate([tall] * (width // 128), axis=1)


def lanes_of(cells):
    column = sheet_of((cells & 255).astype(jnp.float32), 256).astype(jnp.int32)
    return lax.broadcasted_iota(jnp.int32, (128, 256), 1) == column


def gather_row(read, cell_smem, cell_vec, rows_ref):
    for j in range(128):
        rows_ref[j : j + 1, :] = read(cell_smem[0, j] >> 8)
    picked = jnp.where(lanes_of(cell_vec), rows_ref[...], 0.0)
    return jnp.sum(jnp.transpose(picked[:, :128] + picked[:, 128:]), axis=0, keepdims=True)


def plane_row(ref):
    return lambda row: ref[row >> 8, pl.ds(row & 255, 1), :]


def first_kernel(cell_smem, cell_vec, emit_vec, past_ref, field_ref, out_ref, rows_ref):
    sample = gather_row(plane_row(field_ref), cell_smem, cell_vec[...], rows_ref)
    sample = sample.astype(jnp.bfloat16).astype(jnp.float32)
    out_ref[0:8, :] = past_ref[...].astype(jnp.float32)
    out_ref[8:9, :] = sample
    out_ref[9:10, :] = cell_vec[...].astype(jnp.float32)
    out_ref[10:11, :] = emit_vec[...].astype(jnp.float32)
    out_ref[11:16, :] = jnp.zeros((5, 128), jnp.float32)


def first_message(rec_cell, emit_cell, past, field):
    return pl.pallas_call(
        first_kernel,
        out_shape=jax.ShapeDtypeStruct((16, 128), jnp.float32),
        in_specs=[spec(SMEM), spec(VMEM), spec(VMEM), spec(VMEM), spec(VMEM)],
        out_specs=spec(VMEM),
        scratch_shapes=[pltpu.VMEM((128, 256), jnp.float32)],
        cost_estimate=pl.CostEstimate(flops=1 << 20, bytes_accessed=1 << 20, transcendentals=0),
        name="first_message",
    )(rec_cell, rec_cell, emit_cell, past, field)


def match_kernel(first_ref, out_ref):
    for s in range(8):
        rec = first_ref[s, 9:10, :]
        emit = first_ref[s, 10:11, :]
        same = sheet_of(emit, 128) == jnp.broadcast_to(rec, (128, 128))
        out_ref[s * 128 : (s + 1) * 128, :] = jnp.where(same, 1.0, 0.0).astype(jnp.bfloat16)


def matches(first):
    return pl.pallas_call(
        match_kernel,
        out_shape=jax.ShapeDtypeStruct((1024, 128), jnp.bfloat16),
        in_specs=[spec(VMEM)],
        out_specs=spec(VMEM),
        cost_estimate=pl.CostEstimate(flops=1 << 20, bytes_accessed=1 << 19, transcendentals=0),
        name="matches",
    )(first)


def multiply(chosen, green_ref, out_ref):
    left = chosen.astype(jnp.bfloat16)
    for b in range(32):
        out_ref[b] = lax.dot_general(
            left,
            green_ref[b * 128 : (b + 1) * 128, :],
            (((1,), (1,)), ((), ())),
            preferred_element_type=jnp.float32,
        )


def old_samples(first_ref, where):
    return jnp.concatenate([first_ref[s, pl.ds(where, 1), :] for s in range(8)], axis=0)


def start_kernel(delay, first_ref, green_ref, out_ref):
    multiply(old_samples(first_ref, 8 - delay[0]), green_ref, out_ref)


def emission_start(delay, first, green):
    return pl.pallas_call(
        start_kernel,
        out_shape=jax.ShapeDtypeStruct((32, 8, 128), jnp.float32),
        in_specs=[spec(SMEM), spec(VMEM), spec(VMEM)],
        out_specs=spec(VMEM),
        cost_estimate=pl.CostEstimate(flops=8 << 20, bytes_accessed=1 << 20, transcendentals=0),
        name="emission_start",
    )(delay, first, green)


def samples_kernel(moment, delay, *refs):
    message_ref, match_ref, first_ref, *newer_refs, green_ref, out_ref, emitted_ref, sample_ref = refs
    total = message_ref[0, 0:8, :]
    for lag in range(1, 8):
        total = total + message_ref[lag, 0:8, :]
    emitted_ref[...] = total
    values = jnp.concatenate([message_ref[s, 8:9, :] for s in range(8)], axis=0)
    wide = jnp.concatenate([total] * 8, axis=1)
    block = lax.broadcasted_iota(jnp.int32, (8, 1024), 1) >> 7
    wide = jnp.where(block == lax.broadcasted_iota(jnp.int32, (8, 1024), 0), wide, 0.0)
    high = wide.astype(jnp.bfloat16)
    rest = wide - high.astype(jnp.float32)
    middle = rest.astype(jnp.bfloat16)
    low = (rest - middle.astype(jnp.float32)).astype(jnp.bfloat16)
    parts = jnp.concatenate([high, middle, low], axis=0)
    added = jnp.dot(parts, match_ref[...], preferred_element_type=jnp.float32)
    values = values + ((added[16:24] + added[8:16]) + added[0:8])
    sample = values.astype(jnp.bfloat16).astype(jnp.float32)
    sample_ref[...] = sample
    where = 8 + moment - delay[0]
    chosen = old_samples(first_ref, jnp.minimum(where, 8))
    for k, newer_ref in enumerate(newer_refs):
        chosen = jnp.where(where == 9 + k, newer_ref[...], chosen)
    chosen = jnp.where(where == 8 + moment, sample, chosen)
    multiply(chosen, green_ref, out_ref)


def samples_and_emission(moment, delay, message, match, first, newer, green):
    return pl.pallas_call(
        functools.partial(samples_kernel, moment),
        out_shape=(
            jax.ShapeDtypeStruct((32, 8, 128), jnp.float32),
            jax.ShapeDtypeStruct((8, 128), jnp.float32),
            jax.ShapeDtypeStruct((8, 128), jnp.float32),
        ),
        in_specs=[spec(SMEM)] + [spec(VMEM)] * (4 + len(newer)),
        out_specs=(spec(VMEM),) * 3,
        cost_estimate=pl.CostEstimate(flops=8 << 20, bytes_accessed=1 << 20, transcendentals=0),
        name="samples",
    )(delay, message, match, first, *newer, green)


def stencil_kernel(
    take, cell_smem, cell_vec, field_ref, prev_ref, low_ref, high_ref, diag_ref, cross_ref, out_ref, *rest
):
    chunk = 32
    lane = lax.broadcasted_iota(jnp.int32, (chunk, 256), 1)
    sub = lax.broadcasted_iota(jnp.int32, (chunk, 256), 0)
    last = lane == 255
    first = lane == 0

    def right(a):
        return jnp.where(last, 0.0, pltpu.roll(a, 255, 1))

    def left(a):
        return jnp.where(first, 0.0, pltpu.roll(a, 1, 1))

    for x in range(4):

        def load(dx, a, b):
            if x + dx < 0:
                return low_ref[a:b, :]
            if x + dx > 3:
                return high_ref[a:b, :]
            return field_ref[x + dx, a:b, :]

        for k in range(256 // chunk):
            a = k * chunk
            b = a + chunk

            def up(dx):
                if b < 256:
                    return load(dx, a + 1, b + 1)
                whole = load(dx, a, b)
                return jnp.where(sub == chunk - 1, 0.0, pltpu.roll(whole, chunk - 1, 0))

            def down(dx):
                if a > 0:
                    return load(dx, a - 1, b - 1)
                whole = load(dx, a, b)
                return jnp.where(sub == 0, 0.0, pltpu.roll(whole, 1, 0))

            mid = load(0, a, b)
            ahead = load(1, a, b)
            behind = load(-1, a, b)
            mid_up, mid_down = up(0), down(0)
            twice = 2.0 * mid
            slope_x = ahead - behind
            slope_y = mid_up - mid_down
            mixed = cross_ref[0, x, a:b, :] * ((up(1) - up(-1)) - (down(1) - down(-1)))
            mixed = mixed + cross_ref[1, x, a:b, :] * (right(slope_x) - left(slope_x))
            mixed = mixed + cross_ref[2, x, a:b, :] * (right(slope_y) - left(slope_y))
            second = diag_ref[0, x, a:b, :] * (ahead - twice + behind)
            second = second + diag_ref[1, x, a:b, :] * (mid_up - twice + mid_down)
            second = second + diag_ref[2, x, a:b, :] * (right(mid) - twice + left(mid))
            out_ref[x, a:b, :] = (twice - prev_ref[x, a:b, :]) + (second + 0.5 * mixed)
    if take:
        value_ref, rows_ref = rest
        value_ref[...] = gather_row(plane_row(out_ref), cell_smem, cell_vec[...], rows_ref)


def stencil(take, rec_cell, field, prev, low, high, diag, cross):
    out_shape = [jax.ShapeDtypeStruct((4, 256, 256), jnp.float32)]
    scratch = []
    if take:
        out_shape.append(jax.ShapeDtypeStruct((1, 128), jnp.float32))
        scratch.append(pltpu.VMEM((128, 256), jnp.float32))
    return pl.pallas_call(
        functools.partial(stencil_kernel, take),
        out_shape=tuple(out_shape),
        in_specs=[spec(SMEM)] + [spec(VMEM)] * 7,
        out_specs=(spec(VMEM),) * len(out_shape),
        scratch_shapes=scratch,
        cost_estimate=pl.CostEstimate(flops=16 << 20, bytes_accessed=10 << 20, transcendentals=0),
        name="stencil",
    )(rec_cell, rec_cell, field, prev, low, high, diag, cross)


def scatter_kernel(cell_smem, cell_vec, value_ref, field_ref, out_ref, rows_ref):
    out_ref[...] = field_ref[...]
    value = value_ref[...]
    rows_ref[...] = jnp.where(lanes_of(cell_vec[...]), sheet_of(value, 256), 0.0)
    for j in range(128):
        row = cell_smem[0, j] >> 8
        at = (row >> 8, pl.ds(row & 255, 1), slice(None))
        out_ref[at] = out_ref[at] + rows_ref[j : j + 1, :]


def scatter(emit_cell, value, field):
    return pl.pallas_call(
        scatter_kernel,
        out_shape=jax.ShapeDtypeStruct((4, 256, 256), jnp.float32),
        in_specs=[spec(SMEM)] + [spec(VMEM)] * 3,
        out_specs=spec(VMEM),
        scratch_shapes=[pltpu.VMEM((128, 256), jnp.float32)],
        cost_estimate=pl.CostEstimate(flops=1 << 20, bytes_accessed=2 << 20, transcendentals=0),
        name="scatter",
    )(emit_cell, emit_cell, value, field)


def spread_kernel(parts_ref, value_ref, out_ref):
    sums = [parts_ref[b] for b in range(4)]
    for b in range(4, 32):
        sums[b % 4] = sums[b % 4] + parts_ref[b]
    total = (sums[0] + sums[1]) + (sums[2] + sums[3])
    for s in range(8):
        out_ref[s, 0:8, :] = total
        out_ref[s, 8:16, :] = jnp.broadcast_to(value_ref[...], (8, 128))


def spread(parts, value):
    return pl.pallas_call(
        spread_kernel,
        out_shape=jax.ShapeDtypeStruct((8, 16, 128), jnp.float32),
        in_specs=[spec(VMEM)] * 2,
        out_specs=spec(VMEM),
        cost_estimate=pl.CostEstimate(flops=1 << 15, bytes_accessed=1 << 18, transcendentals=0),
        name="spread",
    )(parts, value)


def exchange(array, axis):
    return lax.all_to_all(array, axis, 0, 0, tiled=True)


def halos(field):
    size = lax.axis_size("brick")
    up = [(i, i + 1) for i in range(size - 1)]
    down = [(i + 1, i) for i in range(size - 1)]
    return lax.ppermute(field[3], "brick", up), lax.ppermute(field[0], "brick", down)


def on_device(field_prev, field_now, diag, cross, green, delays, past, rec_cell, emit_cell):
    rank = lax.axis_index("shot")
    delay = lax.dynamic_slice_in_dim(delays, rank, 1)
    earlier, current, green, past = field_prev[0], field_now[0], green[0], past[:, 0]

    message = first_message(rec_cell, emit_cell, past, current)
    first = exchange(jnp.broadcast_to(message[None], (8, 16, 128)), "shot")
    low, high = halos(current)
    following, value = stencil(True, rec_cell, current, earlier, low, high, diag, cross)
    parts = exchange(emission_start(delay, first, green), "brick")
    match = matches(first)

    samples = []
    for moment in (1, 2):
        answer = exchange(spread(parts, value), "shot")
        partial, emitted, sample = samples_and_emission(moment, delay, answer, match, first, samples, green)
        samples.append(sample)
        parts = exchange(partial, "brick")
        mine = lax.dynamic_slice_in_dim(emitted, rank, 1)
        earlier, current = current, scatter(emit_cell, mine, following)
        low, high = halos(current)
        if moment == 1:
            following, value = stencil(True, rec_cell, current, earlier, low, high, diag, cross)
        else:
            (following,) = stencil(False, rec_cell, current, earlier, low, high, diag, cross)
    final = exchange(jnp.sum(parts, axis=0), "shot")
    after = scatter(emit_cell, jnp.sum(final, axis=0, keepdims=True), following)
    recorded = [message[8:9]] + [lax.dynamic_slice_in_dim(s, rank, 1) for s in samples]
    recorded = jnp.stack([r.astype(jnp.bfloat16) for r in recorded])
    return current[None], after[None], recorded


def solution(mesh):
    return jax.shard_map(
        on_device,
        mesh=mesh,
        in_specs=(
            P("shot", "brick", None, None),
            P("shot", "brick", None, None),
            P(None, "brick", None, None),
            P(None, "brick", None, None),
            P("shot", None, "brick"),
            P(),
            P(None, "shot", "brick"),
            P("shot", "brick"),
            P("shot", "brick"),
        ),
        out_specs=(
            P("shot", "brick", None, None),
            P("shot", "brick", None, None),
            P(None, "shot", "brick"),
        ),
        check_vma=False,
    )
```

```python
import functools

import jax
import jax.numpy as jnp
from jax import lax
from jax.experimental import pallas as pl
from jax.experimental.pallas import tpu as pltpu
from jax.sharding import PartitionSpec as P


VMEM = pltpu.VMEM
SMEM = pltpu.SMEM
HBM = pltpu.HBM
DMA = pltpu.SemaphoreType.DMA
f32 = jnp.float32


def spec(space):
    return pl.BlockSpec(memory_space=space)


def near(array):
    return pltpu.with_memory_space_constraint(array, pltpu.MemorySpace.VMEM)


def distant(array):
    return pltpu.with_memory_space_constraint(array, pltpu.MemorySpace.HBM)


def call(kernel, out_shape, work, scalars=(), arrays=(), far=(), free=(), scratch=(), aliases=None, room=2):
    flops, moved = work
    return pl.pallas_call(
        kernel,
        out_shape=out_shape,
        in_specs=[spec(SMEM)] * len(scalars) + [spec(VMEM)] * len(arrays) + [spec(HBM)] * len(far) + [spec(pl.ANY)] * len(free),
        out_specs=jax.tree.map(lambda _: spec(VMEM), out_shape),
        scratch_shapes=list(scratch),
        input_output_aliases=aliases or {},
        cost_estimate=pl.CostEstimate(flops=flops, bytes_accessed=moved, transcendentals=0),
        compiler_params=pltpu.CompilerParams(vmem_limit_bytes=room << 20),
    )(*scalars, *[near(a) for a in arrays], *[distant(a) for a in far], *free)


def sheet_of(row, width):
    tall = jnp.transpose(jnp.broadcast_to(row, (128, 128)))
    return jnp.concatenate([tall] * (width // 128), axis=1)


def lanes_of(cells):
    column = sheet_of((cells & 255).astype(f32), 256).astype(jnp.int32)
    return lax.broadcasted_iota(jnp.int32, (128, 256), 1) == column


def gather_row(field_ref, cell_smem, cell_vec, rows_ref):
    for j in range(128):
        row = cell_smem[0, j] >> 8
        rows_ref[j : j + 1, :] = field_ref[row >> 8, pl.ds(row & 255, 1), :]
    picked = jnp.where(lanes_of(cell_vec), rows_ref[...], 0.0)
    return jnp.sum(jnp.transpose(picked[:, :128] + picked[:, 128:]), axis=0, keepdims=True)


def copies(pairs, sems):
    started = [pltpu.make_async_copy(a, b, sems.at[k]) for k, (a, b) in enumerate(pairs)]
    for copy in started:
        copy.start()
    return started


def first_kernel(
    rank,
    delays,
    cell_smem,
    field_any,
    past_any,
    rec_any,
    emit_any,
    out_ref,
    field_ref,
    first_ref,
    last_ref,
    rec_ref,
    emit_ref,
    own_ref,
    delay_ref,
    rows_ref,
    past_ref,
    sems,
):
    pairs = [(field_any, field_ref), (past_any, past_ref), (rec_any, rec_ref), (emit_any, emit_ref)]
    pairs += [(field_any.at[0], first_ref), (field_any.at[3], last_ref)]
    started = copies(pairs, sems)
    own = lax.broadcasted_iota(jnp.int32, (8, 128), 0) == rank[0]
    own_ref[...] = jnp.where(own, 1.0, 0.0)
    delay_ref[...] = jnp.full((8, 128), delays[rank[0]], jnp.int32)
    for copy in started:
        copy.wait()
    sample = gather_row(field_ref, cell_smem, rec_ref[...], rows_ref)
    out_ref[0, 0:8, :] = past_ref[...].astype(f32)
    out_ref[0, 8:9, :] = sample.astype(jnp.bfloat16).astype(f32)
    out_ref[0, 9:10, :] = rec_ref[...].astype(f32)
    out_ref[0, 10:11, :] = emit_ref[...].astype(f32)
    out_ref[0, 11:16, :] = jnp.zeros((5, 128), f32)
    for s in range(1, 8):
        out_ref[s] = out_ref[0]


def first_message(rank, delays, rec_cell, emit_cell, past, field):
    plane = VMEM((256, 256), f32)
    row = VMEM((1, 128), jnp.int32)
    return call(
        first_kernel,
        (
            VMEM((8, 16, 128), f32),
            VMEM((4, 256, 256), f32),
            plane,
            plane,
            row,
            row,
            VMEM((8, 128), f32),
            VMEM((8, 128), jnp.int32),
        ),
        (1 << 20, 1 << 19),
        scalars=[rank, delays, rec_cell],
        far=[field, past, rec_cell, emit_cell],
        scratch=[VMEM((128, 256), f32), VMEM((8, 128), jnp.bfloat16), DMA((6,))],
    )


def turn_kernel(green_any, right_ref, green_ref, sems):
    for copy in copies([(green_any, green_ref)], sems):
        copy.wait()
    for b in range(32):
        at = slice(b * 128, (b + 1) * 128)
        right_ref[:, at] = jnp.transpose(green_ref[at, :])


def turn(green):
    return call(
        turn_kernel,
        VMEM((128, 4096), jnp.bfloat16),
        (1 << 20, 1 << 20),
        far=[green],
        scratch=[VMEM((4096, 128), jnp.bfloat16), DMA((1,))],
    )


def match_kernel(first_ref, delay_ref, out_ref, old_ref):
    for s in range(8):
        rec = first_ref[s, 9:10, :]
        emit = first_ref[s, 10:11, :]
        same = sheet_of(emit, 128) == jnp.broadcast_to(rec, (128, 128))
        out_ref[s * 128 : (s + 1) * 128, :] = jnp.where(same, 1.0, 0.0).astype(jnp.bfloat16)
    for moment in (1, 2):
        old_ref[moment - 1] = old_samples(first_ref, 8 + moment - delay_ref[...])


def matches(first, delay):
    return call(
        match_kernel,
        (VMEM((1024, 128), jnp.bfloat16), VMEM((2, 8, 128), f32)),
        (1 << 20, 1 << 18),
        arrays=[first, delay],
    )


def multiply(chosen, right_ref, out_ref):
    product = jnp.dot(chosen.astype(jnp.bfloat16), right_ref[...], preferred_element_type=f32)
    for b in range(32):
        out_ref[b] = product[:, b * 128 : (b + 1) * 128]


def old_samples(first_ref, where):
    chosen = jnp.zeros((8, 128), f32)
    for k in range(9):
        series = jnp.concatenate([first_ref[s, k : k + 1, :] for s in range(8)], axis=0)
        chosen = jnp.where(where == k, series, chosen)
    return chosen


def start_kernel(first_ref, delay_ref, right_ref, out_ref):
    multiply(old_samples(first_ref, 8 - delay_ref[...]), right_ref, out_ref)


def emission_start(first, delay, right):
    out = VMEM((32, 8, 128), f32)
    return call(start_kernel, out, (8 << 20, 1 << 20), arrays=[first, delay, right])


def samples_kernel(moment, message_ref, match_ref, old_ref, delay_ref, own_ref, *refs):
    *newer_refs, right_ref, out_ref, mine_ref, sample_ref = refs
    total = message_ref[0, 0:8, :]
    for lag in range(1, 8):
        total = total + message_ref[lag, 0:8, :]
    values = jnp.concatenate([message_ref[s, 8:9, :] for s in range(8)], axis=0)
    wide = jnp.concatenate([total] * 8, axis=1)
    block = lax.broadcasted_iota(jnp.int32, (8, 1024), 1) >> 7
    wide = jnp.where(block == lax.broadcasted_iota(jnp.int32, (8, 1024), 0), wide, 0.0)
    high = wide.astype(jnp.bfloat16)
    rest = wide - high.astype(f32)
    middle = rest.astype(jnp.bfloat16)
    low = (rest - middle.astype(f32)).astype(jnp.bfloat16)
    parts = jnp.concatenate([high, middle, low], axis=0)
    added = jnp.dot(parts, match_ref[...], preferred_element_type=f32)
    values = values + ((added[16:24] + added[8:16]) + added[0:8])
    sample = values.astype(jnp.bfloat16).astype(f32)
    delay = delay_ref[...]
    chosen = old_ref[moment - 1]
    for k, newer_ref in enumerate(newer_refs):
        chosen = jnp.where(delay == moment - 1 - k, newer_ref[...], chosen)
    chosen = jnp.where(delay == 0, sample, chosen)
    multiply(chosen, right_ref, out_ref)
    sample_ref[...] = sample
    mine_ref[...] = jnp.sum(jnp.where(own_ref[...] > 0.5, total, 0.0), axis=0, keepdims=True)


def samples_and_emission(moment, message, match, old, delay, own, newer, right):
    return call(
        functools.partial(samples_kernel, moment),
        (VMEM((32, 8, 128), f32), VMEM((1, 128), f32), VMEM((8, 128), f32)),
        (8 << 20, 1 << 20),
        arrays=[message, match, old, delay, own, *newer, right],
    )


def stencil_kernel(take, cell_smem, cell_vec, field_ref, prev_any, diag_any, cross_any, low_any, high_any, *refs):
    *outs, prev_ref, diag_ref, cross_ref, low_ref, high_ref, sems, edge_sems = refs
    out_ref, *outs = outs
    order = (1, 2, 0, 3)
    started = {}
    for x in order:
        pairs = [(diag_any.at[k, x], diag_ref.at[k, x]) for k in range(3)]
        pairs += [(cross_any.at[k, x], cross_ref.at[k, x]) for k in range(3)]
        started[x] = copies([(prev_any.at[x], prev_ref.at[x])] + pairs, sems.at[x])
    edges = copies([(low_any, low_ref), (high_any, high_ref)], edge_sems)
    chunk = 32
    lane = lax.broadcasted_iota(jnp.int32, (chunk, 256), 1)
    sub = lax.broadcasted_iota(jnp.int32, (chunk, 256), 0)
    last = lane == 255
    first = lane == 0

    def right(a):
        return jnp.where(last, 0.0, pltpu.roll(a, 255, 1))

    def left(a):
        return jnp.where(first, 0.0, pltpu.roll(a, 1, 1))

    for x in order:
        if x == 0:
            for copy in edges:
                copy.wait()
        for copy in started[x]:
            copy.wait()

        def load(dx, a, b):
            if x + dx < 0:
                return low_ref[a:b, :]
            if x + dx > 3:
                return high_ref[a:b, :]
            return field_ref[x + dx, a:b, :]

        for k in range(256 // chunk):
            a = k * chunk
            b = a + chunk

            def up(dx):
                if b < 256:
                    return load(dx, a + 1, b + 1)
                whole = load(dx, a, b)
                return jnp.where(sub == chunk - 1, 0.0, pltpu.roll(whole, chunk - 1, 0))

            def down(dx):
                if a > 0:
                    return load(dx, a - 1, b - 1)
                whole = load(dx, a, b)
                return jnp.where(sub == 0, 0.0, pltpu.roll(whole, 1, 0))

            mid = load(0, a, b)
            ahead = load(1, a, b)
            behind = load(-1, a, b)
            mid_up, mid_down = up(0), down(0)
            twice = 2.0 * mid
            slope_x = ahead - behind
            slope_y = mid_up - mid_down
            mixed = cross_ref[0, x, a:b, :] * ((up(1) - up(-1)) - (down(1) - down(-1)))
            mixed = mixed + cross_ref[1, x, a:b, :] * (right(slope_x) - left(slope_x))
            mixed = mixed + cross_ref[2, x, a:b, :] * (right(slope_y) - left(slope_y))
            second = diag_ref[0, x, a:b, :] * (ahead - twice + behind)
            second = second + diag_ref[1, x, a:b, :] * (mid_up - twice + mid_down)
            second = second + diag_ref[2, x, a:b, :] * (right(mid) - twice + left(mid))
            out_ref[x, a:b, :] = (twice - prev_ref[x, a:b, :]) + (second + 0.5 * mixed)
    if take:
        value_ref, rows_ref = outs
        value_ref[...] = gather_row(out_ref, cell_smem, cell_vec[...], rows_ref)


def stencil(take, rec_cell, rec, field, prev, diag, cross, low, high):
    out_shape = [VMEM((4, 256, 256), f32)]
    scratch = []
    if take:
        out_shape.append(VMEM((1, 128), f32))
        scratch.append(VMEM((128, 256), f32))
    plane = VMEM((256, 256), f32)
    coef = VMEM((3, 4, 256, 256), f32)
    return call(
        functools.partial(stencil_kernel, take),
        tuple(out_shape),
        (16 << 20, 10 << 20),
        scalars=[rec_cell],
        arrays=[rec, field],
        far=[prev, diag, cross],
        free=[low, high],
        scratch=scratch + [VMEM((4, 256, 256), f32), coef, coef, plane, plane, DMA((4, 7)), DMA((2,))],
        room=10,
    )


def add_at(cell_smem, cell_vec, value, target_ref, rows_ref):
    rows_ref[...] = jnp.where(lanes_of(cell_vec[...]), sheet_of(value, 256), 0.0)
    for j in range(128):
        row = cell_smem[0, j] >> 8
        at = (row >> 8, pl.ds(row & 255, 1), slice(None))
        target_ref[at] = target_ref[at] + rows_ref[j : j + 1, :]


def scatter_kernel(cell_smem, cell_vec, mine_ref, field_ref, *refs):
    *refs, rows_ref = refs
    old = refs[: len(refs) - 4] if len(refs) > 3 else []
    out_ref, low_ref, high_ref = refs[len(old) : len(old) + 3]
    del field_ref
    add_at(cell_smem, cell_vec, mine_ref[...], out_ref, rows_ref)
    low_ref[...] = out_ref[0]
    high_ref[...] = out_ref[3]
    if old:
        own_ref, first_ref, *sample_refs = old
        own = own_ref[...] > 0.5
        start = jnp.concatenate([first_ref[s, 8:9, :] for s in range(8)], axis=0)
        series = [start] + [s[...] for s in sample_refs]
        series = [jnp.sum(jnp.where(own, s, 0.0), axis=0, keepdims=True) for s in series]
        refs[-1][...] = jnp.concatenate(series, axis=0).astype(jnp.bfloat16)


def scatter(emit_cell, emit, mine, field, old=()):
    plane = VMEM((256, 256), f32)
    outs = (VMEM((4, 256, 256), f32), plane, plane)
    if old:
        outs += (VMEM((3, 128), jnp.bfloat16),)
    return call(
        scatter_kernel,
        outs,
        (1 << 20, 1 << 19),
        scalars=[emit_cell],
        arrays=[emit, mine, field, *old],
        scratch=[VMEM((128, 256), f32)],
        aliases={3: 0},
    )


def last_kernel(cell_smem, cell_vec, parts_ref, field_ref, out_ref, rows_ref):
    out_ref[...] = field_ref[...]
    value = parts_ref[0]
    for lag in range(1, 8):
        value = value + parts_ref[lag]
    add_at(cell_smem, cell_vec, value, out_ref, rows_ref)


def last_scatter(emit_cell, emit, parts, field):
    return call(
        last_kernel,
        jax.ShapeDtypeStruct((4, 256, 256), f32),
        (1 << 20, 2 << 20),
        scalars=[emit_cell],
        arrays=[emit, parts, field],
        scratch=[VMEM((128, 256), f32)],
    )


def spread_kernel(parts_ref, *refs):
    *value_refs, out_ref = refs
    sums = [parts_ref[b] for b in range(4)]
    for b in range(4, 32):
        sums[b % 4] = sums[b % 4] + parts_ref[b]
    total = (sums[0] + sums[1]) + (sums[2] + sums[3])
    if not value_refs:
        for s in range(8):
            out_ref[s] = total[s : s + 1, :]
        return
    value = jnp.broadcast_to(value_refs[0][...], (8, 128))
    for s in range(8):
        out_ref[s, 0:8, :] = total
        out_ref[s, 8:16, :] = value


def spread(parts, *value):
    out = VMEM((8, 16 if value else 1, 128), f32)
    return call(spread_kernel, out, (1 << 15, 1 << 17), arrays=[parts, *value])


def exchange(array, axis):
    return lax.all_to_all(array, axis, 0, 0, tiled=True)


def halos(first_plane, last_plane):
    size = lax.axis_size("brick")
    up = [(i, i + 1) for i in range(size - 1)]
    down = [(i + 1, i) for i in range(size - 1)]
    low = lax.ppermute(last_plane, "brick", up)
    high = lax.ppermute(first_plane, "brick", down)
    return low, high


def steps(field_prev, field_now, diag, cross, green, delays, past, rec_cell, emit_cell):
    rank = lax.axis_index("shot").reshape(1)
    past = past[:, 0]

    message, current, *planes, rec, emit, own, delay = first_message(
        rank, delays, rec_cell, emit_cell, past, field_now[0]
    )
    first = exchange(message, "shot")
    low, high = halos(*planes)
    right = turn(green[0])
    following, value = stencil(True, rec_cell, rec, current, field_prev[0], diag, cross, low, high)
    partial = emission_start(first, delay, right)
    parts = exchange(partial, "brick")
    match, old = matches(first, delay)
    message = spread(parts, value)

    answer = exchange(message, "shot")
    partial, mine, sample1 = samples_and_emission(1, answer, match, old, delay, own, [], right)
    earlier = current
    current, *planes = scatter(emit_cell, emit, mine, following)
    low, high = halos(*planes)
    parts = exchange(partial, "brick")
    following, value = stencil(True, rec_cell, rec, current, earlier, diag, cross, low, high)
    message = spread(parts, value)

    answer = exchange(message, "shot")
    partial, mine, sample2 = samples_and_emission(2, answer, match, old, delay, own, [sample1], right)
    parts = exchange(partial, "brick")
    earlier = current
    current, *planes, recorded = scatter(emit_cell, emit, mine, following, (own, first, sample1, sample2))
    low, high = halos(*planes)
    (following,) = stencil(False, rec_cell, rec, current, earlier, diag, cross, low, high)
    message = spread(parts)
    parts = exchange(message, "shot")
    after = last_scatter(emit_cell, emit, parts, following)
    return current[None], after[None], recorded[:, None]


def solution(mesh):
    return jax.shard_map(
        steps,
        mesh=mesh,
        in_specs=(
            P("shot", "brick", None, None),
            P("shot", "brick", None, None),
            P(None, "brick", None, None),
            P(None, "brick", None, None),
            P("shot", None, "brick"),
            P(),
            P(None, "shot", "brick"),
            P("shot", "brick"),
            P("shot", "brick"),
        ),
        out_specs=(
            P("shot", "brick", None, None),
            P("shot", "brick", None, None),
            P(None, "shot", "brick"),
        ),
        check_vma=False,
    )
```

```python
import functools

import jax
import jax.numpy as jnp
from jax import lax
from jax.experimental import pallas as pl
from jax.experimental.pallas import tpu as pltpu
from jax.sharding import PartitionSpec as P


VMEM = pltpu.VMEM
SMEM = pltpu.SMEM
HBM = pltpu.HBM
DMA = pltpu.SemaphoreType.DMA
f32 = jnp.float32


def spec(space):
    return pl.BlockSpec(memory_space=space)


def near(array):
    return pltpu.with_memory_space_constraint(array, pltpu.MemorySpace.VMEM)


def distant(array):
    return pltpu.with_memory_space_constraint(array, pltpu.MemorySpace.HBM)


def call(kernel, out_shape, work, scalars=(), arrays=(), far=(), free=(), scratch=(), aliases=None, room=2, result=VMEM):
    flops, moved = work
    return pl.pallas_call(
        kernel,
        out_shape=out_shape,
        in_specs=[spec(SMEM)] * len(scalars) + [spec(VMEM)] * len(arrays) + [spec(HBM)] * len(far) + [spec(pl.ANY)] * len(free),
        out_specs=jax.tree.map(lambda _: spec(result), out_shape),
        scratch_shapes=list(scratch),
        input_output_aliases=aliases or {},
        cost_estimate=pl.CostEstimate(flops=flops, bytes_accessed=moved, transcendentals=0),
        compiler_params=pltpu.CompilerParams(vmem_limit_bytes=room << 20),
    )(*scalars, *[near(a) for a in arrays], *[distant(a) for a in far], *free)


def sheet_of(row, width):
    tall = jnp.transpose(jnp.broadcast_to(row, (128, 128)))
    return jnp.concatenate([tall] * (width // 128), axis=1)


def lanes_of(cells):
    column = sheet_of((cells & 255).astype(f32), 256).astype(jnp.int32)
    return lax.broadcasted_iota(jnp.int32, (128, 256), 1) == column


def gather_row(field_ref, cell_smem, cell_vec, rows_ref):
    for j in range(128):
        row = cell_smem[0, j] >> 8
        rows_ref[j : j + 1, :] = field_ref[row >> 8, pl.ds(row & 255, 1), :]
    picked = jnp.where(lanes_of(cell_vec), rows_ref[...], 0.0)
    return jnp.sum(jnp.transpose(picked[:, :128] + picked[:, 128:]), axis=0, keepdims=True)


def copies(pairs, sems):
    started = [pltpu.make_async_copy(a, b, sems.at[k]) for k, (a, b) in enumerate(pairs)]
    for copy in started:
        copy.start()
    return started


def first_kernel(
    rank,
    odd_brick,
    field_any,
    past_any,
    rec_any,
    emit_any,
    delays_any,
    out_ref,
    even_ref,
    odd_ref,
    rec_ref,
    emit_ref,
    own_ref,
    delay_ref,
    field_ref,
    rows_ref,
    past_ref,
    cell_smem,
    delays,
    sems,
):
    pairs = [(rec_any, cell_smem), (delays_any, delays), (field_any, field_ref), (past_any, past_ref)]
    started = copies(pairs + [(rec_any, rec_ref), (emit_any, emit_ref)], sems)
    own = lax.broadcasted_iota(jnp.int32, (8, 128), 0) == rank[0]
    own_ref[...] = jnp.where(own, 1.0, 0.0)
    for copy in started:
        copy.wait()
    delay_ref[...] = jnp.full((8, 128), delays[rank[0]], jnp.int32)
    sample = gather_row(field_ref, cell_smem, rec_ref[...], rows_ref)
    rows = [past_ref[...].astype(f32), sample.astype(jnp.bfloat16).astype(f32)]
    rows += [rec_ref[...].astype(f32), emit_ref[...].astype(f32), jnp.zeros((5, 128), f32)]
    message = jnp.concatenate(rows, axis=0)
    for s in range(8):
        out_ref[s] = message
    edges(odd_brick, field_ref, even_ref, odd_ref)


def edges(odd_brick, field_ref, even_ref, odd_ref):
    even_ref[...] = field_ref[3 - 3 * odd_brick[0]]
    odd_ref[...] = field_ref[3 * odd_brick[0]]


def first_message(rank, odd_brick, delays, rec_cell, emit_cell, past, field):
    plane = VMEM((256, 256), f32)
    row = VMEM((1, 128), jnp.int32)
    return call(
        first_kernel,
        (VMEM((8, 16, 128), f32), plane, plane, row, row, VMEM((8, 128), f32), VMEM((8, 128), jnp.int32)),
        (1 << 20, 1 << 19),
        scalars=[rank, odd_brick],
        far=[field, past, rec_cell, emit_cell, delays],
        scratch=[
            VMEM((4, 256, 256), f32),
            VMEM((128, 256), f32),
            VMEM((8, 128), jnp.bfloat16),
            SMEM((1, 128), jnp.int32),
            SMEM((8,), jnp.int32),
            DMA((6,)),
        ],
        room=3,
    )


def turn_kernel(green_any, right_ref, green_ref, sems):
    for copy in copies([(green_any, green_ref)], sems):
        copy.wait()
    for b in range(32):
        at = slice(b * 128, (b + 1) * 128)
        right_ref[:, at] = jnp.transpose(green_ref[at, :])


def turn(green):
    return call(
        turn_kernel,
        VMEM((128, 4096), jnp.bfloat16),
        (1 << 20, 1 << 20),
        far=[green],
        scratch=[VMEM((4096, 128), jnp.bfloat16), DMA((1,))],
    )


def older_kernel(first_ref, delay_ref, old_ref):
    for moment in (1, 2):
        old_ref[moment - 1] = old_samples(first_ref, 8 + moment - delay_ref[...])


def older(first, delay):
    out = VMEM((2, 8, 128), f32)
    return call(older_kernel, out, (1 << 20, 1 << 18), arrays=[first, delay])


def matches(first_ref):
    blocks = []
    for s in range(8):
        rec = first_ref[s, 9:10, :]
        emit = first_ref[s, 10:11, :]
        same = sheet_of(emit, 128) == jnp.broadcast_to(rec, (128, 128))
        blocks.append(jnp.where(same, 1.0, 0.0).astype(jnp.bfloat16))
    return jnp.concatenate(blocks, axis=0)


def multiply(chosen, right_ref, out_ref):
    product = jnp.dot(chosen.astype(jnp.bfloat16), right_ref[...], preferred_element_type=f32)
    for b in range(32):
        out_ref[b] = product[:, b * 128 : (b + 1) * 128]


def old_samples(first_ref, where):
    chosen = jnp.zeros((8, 128), f32)
    for k in range(9):
        series = jnp.concatenate([first_ref[s, k : k + 1, :] for s in range(8)], axis=0)
        chosen = jnp.where(where == k, series, chosen)
    return chosen


def start_kernel(first_ref, delay_ref, right_ref, out_ref):
    multiply(old_samples(first_ref, 8 - delay_ref[...]), right_ref, out_ref)


def emission_start(first, delay, right):
    out = VMEM((32, 8, 128), f32)
    return call(start_kernel, out, (8 << 20, 1 << 20), arrays=[first, delay, right])


def samples_kernel(moment, message_ref, first_ref, old_ref, delay_ref, own_ref, *refs):
    *newer_refs, right_ref, out_ref, mine_ref, sample_ref = refs
    total = message_ref[0, 0:8, :]
    for lag in range(1, 8):
        total = total + message_ref[lag, 0:8, :]
    values = jnp.concatenate([message_ref[s, 8:9, :] for s in range(8)], axis=0)
    wide = jnp.concatenate([total] * 8, axis=1)
    block = lax.broadcasted_iota(jnp.int32, (8, 1024), 1) >> 7
    wide = jnp.where(block == lax.broadcasted_iota(jnp.int32, (8, 1024), 0), wide, 0.0)
    high = wide.astype(jnp.bfloat16)
    rest = wide - high.astype(f32)
    middle = rest.astype(jnp.bfloat16)
    low = (rest - middle.astype(f32)).astype(jnp.bfloat16)
    parts = jnp.concatenate([high, middle, low], axis=0)
    added = jnp.dot(parts, matches(first_ref), preferred_element_type=f32)
    values = values + ((added[16:24] + added[8:16]) + added[0:8])
    sample = values.astype(jnp.bfloat16).astype(f32)
    delay = delay_ref[...]
    chosen = old_ref[moment - 1]
    for k, newer_ref in enumerate(newer_refs):
        chosen = jnp.where(delay == moment - 1 - k, newer_ref[...], chosen)
    chosen = jnp.where(delay == 0, sample, chosen)
    multiply(chosen, right_ref, out_ref)
    sample_ref[...] = sample
    mine_ref[...] = jnp.sum(jnp.where(own_ref[...] > 0.5, total, 0.0), axis=0, keepdims=True)


def samples_and_emission(moment, message, first, old, delay, own, newer, right):
    return call(
        functools.partial(samples_kernel, moment),
        (VMEM((32, 8, 128), f32), VMEM((1, 128), f32), VMEM((8, 128), f32)),
        (8 << 20, 1 << 20),
        arrays=[message, first, old, delay, own, *newer, right],
    )


def stencil_kernel(take, inside, odd_brick, cell_smem, cell_vec, *refs):
    field_in, prev_any, diag_any, cross_any, even_any, odd_any, *refs = refs
    *outs, field_ref, prev_ref, diag_ref, cross_ref, low_ref, high_ref, sems, edge_sems = refs
    out_ref, *outs = outs
    order = (1, 2, 0, 3)
    started = {}
    begun = {}
    if inside:
        field_ref = field_in
    else:
        begun = {x: copies([(field_in.at[x], field_ref.at[x])], sems.at[x, pl.ds(7, 1)]) for x in (0, 1, 2, 3)}
    for x in order:
        pairs = [(diag_any.at[k, x], diag_ref.at[k, x]) for k in range(3)]
        pairs += [(cross_any.at[k, x], cross_ref.at[k, x]) for k in range(3)]
        started[x] = copies([(prev_any.at[x], prev_ref.at[x])] + pairs, sems.at[x])

    @pl.when(odd_brick[0] == 0)
    def _():
        copies([(even_any, high_ref), (odd_any, low_ref)], edge_sems)

    @pl.when(odd_brick[0] == 1)
    def _():
        copies([(even_any, low_ref), (odd_any, high_ref)], edge_sems)

    lane = lax.broadcasted_iota(jnp.int32, (8, 128), 1)
    sub = lax.broadcasted_iota(jnp.int32, (8, 128), 0)
    zero = jnp.zeros((8, 128), f32)

    def after_z(pair):
        a, b = (pltpu.roll(v, 127, 1) for v in pair)
        return jnp.where(lane == 127, b, a), jnp.where(lane == 127, 0.0, b)

    def before_z(pair):
        a, b = (pltpu.roll(v, 1, 1) for v in pair)
        return jnp.where(lane == 0, 0.0, a), jnp.where(lane == 0, a, b)

    def at(ref, where, t):
        rows = slice(8 * t, 8 * t + 8)
        return ref[(*where, rows, slice(0, 128))], ref[(*where, rows, slice(128, 256))]

    def each(f, *pairs):
        return tuple(f(*vs) for vs in zip(*pairs))

    for x in order:
        need = {1: (0, 1, 2), 2: (3,)}.get(x, ())
        for k in need:
            for copy in begun.get(k, ()):
                copy.wait()
        if x == 0:
            for copy in [pltpu.make_async_copy(odd_any, low_ref, edge_sems.at[k]) for k in (0, 1)]:
                copy.wait()
        for copy in started[x]:
            copy.wait()

        def plane(dx):
            if x + dx < 0:
                return low_ref, ()
            if x + dx > 3:
                return high_ref, ()
            return field_ref, (x + dx,)

        def turned(pair):
            return tuple(pltpu.roll(v, 7, 0) for v in pair), tuple(pltpu.roll(v, 1, 0) for v in pair)

        edge = ((zero, zero), (zero, zero))
        tiles = {}
        turns = {-1: (edge, edge), 32: (edge, edge)}

        def fetch(t):
            mid = at(*plane(0), t)
            ahead = at(*plane(1), t)
            behind = at(*plane(-1), t)
            slope = each(lambda a, b: a - b, ahead, behind)
            tiles[t] = mid, each(lambda a, b: a + b, ahead, behind), slope
            turns[t] = turned(mid), turned(slope)

        def after_y(t, k):
            return each(lambda a, b: jnp.where(sub == 7, b, a), turns[t][k][0], turns[t + 1][k][0])

        def before_y(t, k):
            return each(lambda a, b: jnp.where(sub == 0, b, a), turns[t][k][1], turns[t - 1][k][1])

        fetch(0)
        for t in range(32):
            if t < 31:
                fetch(t + 1)
            mid, sum_x, slope_x = tiles.pop(t)
            up, down = after_y(t, 0), before_y(t, 0)
            twist = each(lambda a, b: a - b, after_y(t, 1), before_y(t, 1))
            slope_y = each(lambda a, b: a - b, up, down)
            sum_y = each(lambda a, b: a + b, up, down)
            sum_z = each(lambda a, b: a + b, after_z(mid), before_z(mid))
            twist_x = each(lambda a, b: a - b, after_z(slope_x), before_z(slope_x))
            twist_y = each(lambda a, b: a - b, after_z(slope_y), before_z(slope_y))
            diag = [at(diag_ref, (k, x), t) for k in range(3)]
            cross = [at(cross_ref, (k, x), t) for k in range(3)]
            prev = at(prev_ref, (x,), t)
            for h in range(2):
                d0, d1, d2 = (d[h] for d in diag)
                c0, c1, c2 = (c[h] for c in cross)
                twice = mid[h] + mid[h]
                second = d0 * (sum_x[h] - twice) + d1 * (sum_y[h] - twice) + d2 * (sum_z[h] - twice)
                mixed = c0 * twist[h] + c1 * twist_x[h] + c2 * twist_y[h]
                value = (twice - prev[h]) + (second + 0.5 * mixed)
                out_ref[x, 8 * t : 8 * t + 8, 128 * h : 128 * h + 128] = value
    if take:
        value_ref, rows_ref = outs
        value_ref[...] = gather_row(out_ref, cell_smem, cell_vec[...], rows_ref)


def stencil(take, inside, odd_brick, rec_cell, rec, field, prev, diag, cross, even, odd):
    out_shape = [VMEM((4, 256, 256), f32)]
    scratch = []
    if take:
        out_shape.append(VMEM((1, 128), f32))
        scratch.append(VMEM((128, 256), f32))
    plane = VMEM((256, 256), f32)
    coef = VMEM((3, 4, 256, 256), f32)
    whole = VMEM((4, 256, 256), f32)
    scratch += [VMEM((8, 128), f32) if inside else whole, whole, coef, coef, plane, plane, DMA((4, 8)), DMA((2,))]
    return call(
        functools.partial(stencil_kernel, take, inside),
        tuple(out_shape),
        (16 << 20, 10 << 20),
        scalars=[odd_brick, rec_cell],
        arrays=[rec] + [field] * inside,
        far=[field] * (not inside) + [prev, diag, cross],
        free=[even, odd],
        scratch=scratch,
        room=11,
    )


def add_at(cell_smem, cell_vec, value, target_ref, rows_ref):
    rows_ref[...] = jnp.where(lanes_of(cell_vec[...]), sheet_of(value, 256), 0.0)
    for j in range(128):
        row = cell_smem[0, j] >> 8
        at = (row >> 8, pl.ds(row & 255, 1), slice(None))
        target_ref[at] = target_ref[at] + rows_ref[j : j + 1, :]


def scatter_kernel(odd_brick, cell_smem, cell_vec, mine_ref, field_ref, *refs):
    *refs, rows_ref = refs
    old = refs[: len(refs) - 4] if len(refs) > 3 else []
    out_ref, even_ref, odd_ref = refs[len(old) : len(old) + 3]
    del field_ref
    add_at(cell_smem, cell_vec, mine_ref[...], out_ref, rows_ref)
    edges(odd_brick, out_ref, even_ref, odd_ref)
    if old:
        own_ref, first_ref, *sample_refs = old
        own = own_ref[...] > 0.5
        start = jnp.concatenate([first_ref[s, 8:9, :] for s in range(8)], axis=0)
        series = [start] + [s[...] for s in sample_refs]
        series = [jnp.sum(jnp.where(own, s, 0.0), axis=0, keepdims=True) for s in series]
        refs[-1][...] = jnp.concatenate(series, axis=0).astype(jnp.bfloat16)


def scatter(odd_brick, emit_cell, emit, mine, field, old=()):
    plane = VMEM((256, 256), f32)
    outs = (VMEM((4, 256, 256), f32), plane, plane)
    if old:
        outs += (VMEM((3, 128), jnp.bfloat16),)
    return call(
        scatter_kernel,
        outs,
        (1 << 20, 1 << 19),
        scalars=[odd_brick, emit_cell],
        arrays=[emit, mine, field, *old],
        scratch=[VMEM((128, 256), f32)],
        aliases={4: 0},
    )


def last_kernel(cell_smem, cell_vec, parts_ref, field_ref, out_any, rows_ref, sem):
    value = parts_ref[0]
    for lag in range(1, 8):
        value = value + parts_ref[lag]
    add_at(cell_smem, cell_vec, value, field_ref, rows_ref)
    copy = pltpu.make_async_copy(field_ref, out_any, sem)
    copy.start()
    copy.wait()


def last_scatter(emit_cell, emit, parts, field):
    return call(
        last_kernel,
        jax.ShapeDtypeStruct((4, 256, 256), f32),
        (1 << 20, 2 << 20),
        scalars=[emit_cell],
        arrays=[emit, parts, field],
        scratch=[VMEM((128, 256), f32), DMA],
        result=HBM,
    )


def spread_kernel(parts_ref, *refs):
    *value_refs, out_ref = refs
    sums = [parts_ref[b] for b in range(4)]
    for b in range(4, 32):
        sums[b % 4] = sums[b % 4] + parts_ref[b]
    total = (sums[0] + sums[1]) + (sums[2] + sums[3])
    if not value_refs:
        for s in range(8):
            out_ref[s] = total[s : s + 1, :]
        return
    value = jnp.broadcast_to(value_refs[0][...], (8, 128))
    for s in range(8):
        out_ref[s, 0:8, :] = total
        out_ref[s, 8:16, :] = value


def spread(parts, *value):
    out = VMEM((8, 16 if value else 1, 128), f32)
    return call(spread_kernel, out, (1 << 15, 1 << 17), arrays=[parts, *value])


def exchange(array, axis):
    return lax.all_to_all(array, axis, 0, 0, tiled=True)


def halos(even_plane, odd_plane):
    size = lax.axis_size("brick")
    even = lax.ppermute(even_plane, "brick", [(i, i ^ 1) for i in range(size)])
    odd = lax.ppermute(odd_plane, "brick", [(i, ((i + 1) ^ 1) - 1) for i in range(1, size - 1)])
    return even, odd


def steps(field_prev, field_now, diag, cross, green, delays, past, rec_cell, emit_cell):
    rank = lax.axis_index("shot").reshape(1)
    odd_brick = (lax.axis_index("brick") & 1).reshape(1)
    past = past[:, 0]

    current = field_now[0]
    message, *planes, rec, emit, own, delay = first_message(rank, odd_brick, delays, rec_cell, emit_cell, past, current)
    first = exchange(message, "shot")
    even, odd = halos(*planes)
    right = turn(green[0])
    following, value = stencil(True, False, odd_brick, rec_cell, rec, current, field_prev[0], diag, cross, even, odd)
    partial = emission_start(first, delay, right)
    parts = exchange(partial, "brick")
    old = older(first, delay)
    message = spread(parts, value)

    answer = exchange(message, "shot")
    partial, mine, sample1 = samples_and_emission(1, answer, first, old, delay, own, [], right)
    earlier = current
    current, *planes = scatter(odd_brick, emit_cell, emit, mine, following)
    even, odd = halos(*planes)
    parts = exchange(partial, "brick")
    following, value = stencil(True, True, odd_brick, rec_cell, rec, current, earlier, diag, cross, even, odd)
    message = spread(parts, value)

    answer = exchange(message, "shot")
    partial, mine, sample2 = samples_and_emission(2, answer, first, old, delay, own, [sample1], right)
    parts = exchange(partial, "brick")
    earlier = current
    current, *planes, recorded = scatter(odd_brick, emit_cell, emit, mine, following, (own, first, sample1, sample2))
    even, odd = halos(*planes)
    (following,) = stencil(False, True, odd_brick, rec_cell, rec, current, earlier, diag, cross, even, odd)
    message = spread(parts)
    parts = exchange(message, "shot")
    after = last_scatter(emit_cell, emit, parts, following)
    return current[None], after[None], recorded[:, None]


def solution(mesh):
    return jax.shard_map(
        steps,
        mesh=mesh,
        in_specs=(
            P("shot", "brick", None, None),
            P("shot", "brick", None, None),
            P(None, "brick", None, None),
            P(None, "brick", None, None),
            P("shot", None, "brick"),
            P(),
            P(None, "shot", "brick"),
            P("shot", "brick"),
            P("shot", "brick"),
        ),
        out_specs=(
            P("shot", "brick", None, None),
            P("shot", "brick", None, None),
            P(None, "shot", "brick"),
        ),
        check_vma=False,
    )
```

```python
import functools

import jax
import jax.numpy as jnp
from jax import lax
from jax.experimental import pallas as pl
from jax.experimental.pallas import tpu as pltpu
from jax.sharding import PartitionSpec as P


VMEM = pltpu.VMEM
SMEM = pltpu.SMEM
HBM = pltpu.HBM
FAR = True
DMA = pltpu.SemaphoreType.DMA
f32 = jnp.float32


def spec(space):
    return pl.BlockSpec(memory_space=space)


def near(array):
    return pltpu.with_memory_space_constraint(array, pltpu.MemorySpace.VMEM)


def distant(array):
    return pltpu.with_memory_space_constraint(array, pltpu.MemorySpace.HBM)


def call(kernel, out_shape, work, scalars=(), arrays=(), far=(), free=(), scratch=(), aliases=None, room=2, result=VMEM):
    flops, moved = work
    return pl.pallas_call(
        kernel,
        out_shape=out_shape,
        in_specs=[spec(SMEM)] * len(scalars) + [spec(VMEM)] * len(arrays) + [spec(HBM)] * len(far) + [spec(pl.ANY)] * len(free),
        out_specs=jax.tree.map(lambda _: spec(result), out_shape),
        scratch_shapes=list(scratch),
        input_output_aliases=aliases or {},
        cost_estimate=pl.CostEstimate(flops=flops, bytes_accessed=moved, transcendentals=0),
        compiler_params=pltpu.CompilerParams(vmem_limit_bytes=room << 20),
    )(*scalars, *[near(a) for a in arrays], *[distant(a) for a in far], *free)


def sheet_of(row, width):
    tall = jnp.transpose(jnp.broadcast_to(row, (128, 128)))
    return jnp.concatenate([tall] * (width // 128), axis=1)


def lanes_of(cells):
    column = sheet_of((cells & 255).astype(f32), 256).astype(jnp.int32)
    return lax.broadcasted_iota(jnp.int32, (128, 256), 1) == column


def gather_row(field_ref, cell_smem, cell_vec, rows_ref):
    for j in range(128):
        row = cell_smem[0, j] >> 8
        rows_ref[j : j + 1, :] = field_ref[pl.ds(row, 1), :]
    picked = jnp.where(lanes_of(cell_vec), rows_ref[...], 0.0)
    return jnp.sum(jnp.transpose(picked[:, :128] + picked[:, 128:]), axis=0, keepdims=True)


def copies(pairs, sems):
    started = [pltpu.make_async_copy(a, b, sems.at[k]) for k, (a, b) in enumerate(pairs)]
    for copy in started:
        copy.start()
    return started


def first_kernel(
    rank,
    odd_brick,
    field_any,
    past_any,
    rec_any,
    emit_any,
    delays_any,
    out_ref,
    even_ref,
    odd_ref,
    rec_ref,
    emit_ref,
    own_ref,
    delay_ref,
    field_ref,
    rows_ref,
    past_ref,
    cell_smem,
    delays,
    sems,
):
    pairs = [(rec_any, cell_smem), (delays_any, delays), (field_any, field_ref), (past_any, past_ref)]
    started = copies(pairs + [(rec_any, rec_ref), (emit_any, emit_ref)], sems)
    own = lax.broadcasted_iota(jnp.int32, (8, 128), 0) == rank[0]
    own_ref[...] = jnp.where(own, 1.0, 0.0)
    for copy in started:
        copy.wait()
    delay_ref[...] = jnp.full((8, 128), delays[rank[0]], jnp.int32)
    sample = gather_row(field_ref, cell_smem, rec_ref[...], rows_ref)
    rows = [past_ref[...].astype(f32), sample.astype(jnp.bfloat16).astype(f32)]
    rows += [rec_ref[...].astype(f32), emit_ref[...].astype(f32), jnp.zeros((5, 128), f32)]
    message = jnp.concatenate(rows, axis=0)
    for s in range(8):
        out_ref[s] = message
    edges(odd_brick, field_ref, even_ref, odd_ref)


def edges(odd_brick, field_ref, even_ref, odd_ref):
    even_ref[...] = field_ref[pl.ds(pl.multiple_of(768 - 768 * odd_brick[0], 256), 256), :]
    odd_ref[...] = field_ref[pl.ds(pl.multiple_of(768 * odd_brick[0], 256), 256), :]


def first_message(rank, odd_brick, delays, rec_cell, emit_cell, past, field):
    plane = VMEM((256, 256), f32)
    row = VMEM((1, 128), jnp.int32)
    return call(
        first_kernel,
        (VMEM((8, 16, 128), f32), plane, plane, row, row, VMEM((8, 128), f32), VMEM((8, 128), jnp.int32)),
        (1 << 20, 1 << 19),
        scalars=[rank, odd_brick],
        far=[field, past, rec_cell, emit_cell, delays],
        scratch=[
            VMEM((1024, 256), f32),
            VMEM((128, 256), f32),
            VMEM((8, 128), jnp.bfloat16),
            SMEM((1, 128), jnp.int32),
            SMEM((8,), jnp.int32),
            DMA((6,)),
        ],
        room=3,
    )


def turn_kernel(green_ref, right_ref):
    for b in range(32):
        at = slice(b * 128, (b + 1) * 128)
        right_ref[:, at] = jnp.transpose(green_ref[at, :])


def turn(green):
    return call(turn_kernel, VMEM((128, 4096), jnp.bfloat16), (1 << 20, 1 << 20), arrays=[green])


def older_kernel(first_ref, delay_ref, old_ref):
    for moment in (1, 2):
        old_ref[moment - 1] = old_samples(first_ref, 8 + moment - delay_ref[...])


def older(first, delay):
    out = VMEM((2, 8, 128), f32)
    return call(older_kernel, out, (1 << 20, 1 << 18), arrays=[first, delay])


def matches(first_ref):
    blocks = []
    for s in range(8):
        rec = first_ref[s, 9:10, :]
        emit = first_ref[s, 10:11, :]
        same = sheet_of(emit, 128) == jnp.broadcast_to(rec, (128, 128))
        blocks.append(jnp.where(same, 1.0, 0.0).astype(jnp.bfloat16))
    return jnp.concatenate(blocks, axis=0)


def multiply(chosen, right_ref, out_ref):
    product = jnp.dot(chosen.astype(jnp.bfloat16), right_ref[...], preferred_element_type=f32)
    for b in range(32):
        out_ref[b] = product[:, b * 128 : (b + 1) * 128]


def old_samples(first_ref, where):
    chosen = jnp.zeros((8, 128), f32)
    for k in range(9):
        series = jnp.concatenate([first_ref[s, k : k + 1, :] for s in range(8)], axis=0)
        chosen = jnp.where(where == k, series, chosen)
    return chosen


def start_kernel(first_ref, delay_ref, right_ref, out_ref):
    multiply(old_samples(first_ref, 8 - delay_ref[...]), right_ref, out_ref)


def emission_start(first, delay, right):
    out = VMEM((32, 8, 128), f32)
    return call(start_kernel, out, (8 << 20, 1 << 20), arrays=[first, delay, right])


def samples_kernel(moment, message_ref, first_ref, old_ref, delay_ref, own_ref, *refs):
    *newer_refs, right_ref, out_ref, mine_ref, sample_ref = refs
    total = message_ref[0, 0:8, :]
    for lag in range(1, 8):
        total = total + message_ref[lag, 0:8, :]
    values = jnp.concatenate([message_ref[s, 8:9, :] for s in range(8)], axis=0)
    wide = jnp.concatenate([total] * 8, axis=1)
    block = lax.broadcasted_iota(jnp.int32, (8, 1024), 1) >> 7
    wide = jnp.where(block == lax.broadcasted_iota(jnp.int32, (8, 1024), 0), wide, 0.0)
    high = wide.astype(jnp.bfloat16)
    rest = wide - high.astype(f32)
    middle = rest.astype(jnp.bfloat16)
    low = (rest - middle.astype(f32)).astype(jnp.bfloat16)
    parts = jnp.concatenate([high, middle, low], axis=0)
    added = jnp.dot(parts, matches(first_ref), preferred_element_type=f32)
    values = values + ((added[16:24] + added[8:16]) + added[0:8])
    sample = values.astype(jnp.bfloat16).astype(f32)
    delay = delay_ref[...]
    chosen = old_ref[moment - 1]
    for k, newer_ref in enumerate(newer_refs):
        chosen = jnp.where(delay == moment - 1 - k, newer_ref[...], chosen)
    chosen = jnp.where(delay == 0, sample, chosen)
    multiply(chosen, right_ref, out_ref)
    sample_ref[...] = sample
    mine_ref[...] = jnp.sum(jnp.where(own_ref[...] > 0.5, total, 0.0), axis=0, keepdims=True)


def samples_and_emission(moment, message, first, old, delay, own, newer, right):
    return call(
        functools.partial(samples_kernel, moment),
        (VMEM((32, 8, 128), f32), VMEM((1, 128), f32), VMEM((8, 128), f32)),
        (8 << 20, 1 << 20),
        arrays=[message, first, old, delay, own, *newer, right],
    )


def stencil_kernel(take, inside, odd_brick, cell_smem, cell_vec, *refs):
    field_in, prev_any, diag_any, cross_any, even_any, odd_any, *refs = refs
    *outs, field_ref, prev_ref, diag_ref, cross_ref, low_ref, high_ref, skew_ref, sum_ref, sems, edge_sems = refs
    out_ref, *outs = outs
    order = (1, 2, 0, 3)

    def part(x):
        return pl.ds(256 * x, 256)

    begun = {}
    if inside:
        field_ref = field_in
    else:
        for x in (0, 1, 2, 3):
            begun[x] = copies([(field_in.at[part(x)], field_ref.at[part(x)])], sems.at[x, pl.ds(7, 1)])
    started = {}
    for x in order:
        pairs = [(diag_any.at[k, x], diag_ref.at[k, x]) for k in range(3)]
        pairs += [(cross_any.at[k, x], cross_ref.at[k, x]) for k in range(3)]
        started[x] = copies([(prev_any.at[part(x)], prev_ref.at[part(x)])] + pairs, sems.at[x])

    @pl.when(odd_brick[0] == 0)
    def _():
        copies([(even_any, high_ref), (odd_any, low_ref)], edge_sems)

    @pl.when(odd_brick[0] == 1)
    def _():
        copies([(even_any, low_ref), (odd_any, high_ref)], edge_sems)

    lane = lax.broadcasted_iota(jnp.int32, (8, 128), 1)
    sub = lax.broadcasted_iota(jnp.int32, (8, 128), 0)
    zero = jnp.zeros((8, 128), f32)
    first_lane, last_lane = lane == 0, lane == 127
    first_sub, last_sub = sub == 0, sub == 7

    def at(ref, where, row):
        rows = slice(row, row + 8)
        return ref[(*where, rows, slice(0, 128))], ref[(*where, rows, slice(128, 256))]

    def put(ref, row, pair):
        for h in range(2):
            ref[row : row + 8, 128 * h : 128 * h + 128] = pair[h]

    def each(f, *pairs):
        return tuple(f(*vs) for vs in zip(*pairs))

    def plus(a, b):
        return each(lambda v, w: v + w, a, b)

    def minus(a, b):
        return each(lambda v, w: v - w, a, b)

    def source(x):
        if x < 0:
            return low_ref, 0
        if x > 3:
            return high_ref, 0
        return field_ref, 256 * x

    def along_z(x):
        ref, base = source(x)
        for t in range(32):
            a, b = at(ref, (), base + 8 * t)
            up_a, up_b = pltpu.roll(a, 127, 1), pltpu.roll(b, 127, 1)
            down_a, down_b = pltpu.roll(a, 1, 1), pltpu.roll(b, 1, 1)
            ahead = (jnp.where(last_lane, up_b, up_a), jnp.where(last_lane, 0.0, up_b))
            behind = (jnp.where(first_lane, 0.0, down_a), jnp.where(first_lane, down_a, down_b))
            put(skew_ref, 256 * (x + 1) + 8 * t, minus(ahead, behind))
            if 0 <= x < 4:
                put(sum_ref, 256 * x + 8 * t, plus(ahead, behind))

    ready = {1: (0, 1, 2), 2: (3,), 0: (-1,), 3: (4,)}
    for x in order:
        if x == 0:
            for k in (0, 1):
                pltpu.make_async_copy(odd_any, low_ref, edge_sems.at[k]).wait()
        for k in ready[x]:
            for copy in begun.get(k, ()):
                copy.wait()
            along_z(k)
        for copy in started[x]:
            copy.wait()

        def turned(pair):
            return tuple(pltpu.roll(v, 7, 0) for v in pair), tuple(pltpu.roll(v, 1, 0) for v in pair)

        edge = ((zero, zero), (zero, zero))
        tiles = {}
        turns = {-1: (edge, edge, edge), 32: (edge, edge, edge)}

        def fetch(t):
            mid, ahead, behind = (at(ref, (), base + 8 * t) for ref, base in map(source, (x, x + 1, x - 1)))
            slope = minus(ahead, behind)
            skew = at(skew_ref, (), 256 * (x + 1) + 8 * t)
            tiles[t] = mid, plus(ahead, behind)
            turns[t] = turned(mid), turned(slope), turned(skew)

        def after_y(t, k):
            return each(lambda a, b: jnp.where(last_sub, b, a), turns[t][k][0], turns[t + 1][k][0])

        def before_y(t, k):
            return each(lambda a, b: jnp.where(first_sub, b, a), turns[t][k][1], turns[t - 1][k][1])

        fetch(0)
        for t in range(32):
            if t < 31:
                fetch(t + 1)
            row = 8 * t
            mid, sum_x = tiles.pop(t)
            sum_y = plus(after_y(t, 0), before_y(t, 0))
            sum_z = at(sum_ref, (), 256 * x + row)
            skew_xy = minus(after_y(t, 1), before_y(t, 1))
            skew_xz = minus(at(skew_ref, (), 256 * (x + 2) + row), at(skew_ref, (), 256 * x + row))
            skew_yz = minus(after_y(t, 2), before_y(t, 2))
            diag = [at(diag_ref, (k, x), row) for k in range(3)]
            cross = [at(cross_ref, (k, x), row) for k in range(3)]
            prev = at(prev_ref, (), 256 * x + row)
            values = []
            for h in range(2):
                d0, d1, d2 = (d[h] for d in diag)
                c0, c1, c2 = (c[h] for c in cross)
                twice = mid[h] + mid[h]
                second = d0 * (sum_x[h] - twice) + d1 * (sum_y[h] - twice) + d2 * (sum_z[h] - twice)
                mixed = c0 * skew_xy[h] + c1 * skew_xz[h] + c2 * skew_yz[h]
                values.append((twice - prev[h]) + (second + 0.5 * mixed))
            put(out_ref, 256 * x + row, values)
    if take:
        value_ref, rows_ref = outs
        value_ref[...] = gather_row(out_ref, cell_smem, cell_vec[...], rows_ref)


def stencil(take, inside, odd_brick, rec_cell, rec, field, prev, diag, cross, even, odd):
    out_shape = [VMEM((1024, 256), f32)]
    scratch = []
    if take:
        out_shape.append(VMEM((1, 128), f32))
        scratch.append(VMEM((128, 256), f32))
    plane = VMEM((256, 256), f32)
    coef = VMEM((3, 4, 256, 256), f32)
    whole = VMEM((1024, 256), f32)
    scratch += [VMEM((8, 128), f32) if inside else whole, whole, coef, coef, plane, plane]
    scratch += [VMEM((1536, 256), f32), whole, DMA((4, 8)), DMA((2,))]
    return call(
        functools.partial(stencil_kernel, take, inside),
        tuple(out_shape),
        (16 << 20, 10 << 20),
        scalars=[odd_brick, rec_cell],
        arrays=[rec] + [field] * inside,
        far=[field] * (not inside) + [prev, diag, cross] + ([even, odd] if FAR and take and inside else []),
        free=[] if FAR and take and inside else [even, odd],
        scratch=scratch,
        room=14,
    )


def add_at(cell_smem, cell_vec, value, target_ref, rows_ref):
    rows_ref[...] = jnp.where(lanes_of(cell_vec[...]), sheet_of(value, 256), 0.0)
    for j in range(128):
        row = cell_smem[0, j] >> 8
        target_ref[pl.ds(row, 1), :] = target_ref[pl.ds(row, 1), :] + rows_ref[j : j + 1, :]


def scatter_kernel(odd_brick, cell_smem, cell_vec, mine_ref, field_ref, *refs):
    *refs, rows_ref = refs
    old = refs[: len(refs) - 4] if len(refs) > 3 else []
    out_ref, even_ref, odd_ref = refs[len(old) : len(old) + 3]
    del field_ref
    add_at(cell_smem, cell_vec, mine_ref[...], out_ref, rows_ref)
    edges(odd_brick, out_ref, even_ref, odd_ref)
    if old:
        own_ref, first_ref, *sample_refs = old
        own = own_ref[...] > 0.5
        start = jnp.concatenate([first_ref[s, 8:9, :] for s in range(8)], axis=0)
        series = [start] + [s[...] for s in sample_refs]
        series = [jnp.sum(jnp.where(own, s, 0.0), axis=0, keepdims=True) for s in series]
        refs[-1][...] = jnp.concatenate(series, axis=0).astype(jnp.bfloat16)


def scatter(odd_brick, emit_cell, emit, mine, field, old=()):
    plane = VMEM((256, 256), f32)
    outs = (VMEM((1024, 256), f32), plane, plane)
    if old:
        outs += (VMEM((3, 128), jnp.bfloat16),)
    return call(
        scatter_kernel,
        outs,
        (1 << 20, 1 << 19),
        scalars=[odd_brick, emit_cell],
        arrays=[emit, mine, field, *old],
        scratch=[VMEM((128, 256), f32)],
        aliases={4: 0},
    )


def last_kernel(cell_smem, cell_vec, parts_ref, field_ref, out_any, rows_ref, sem):
    value = parts_ref[0]
    for lag in range(1, 8):
        value = value + parts_ref[lag]
    add_at(cell_smem, cell_vec, value, field_ref, rows_ref)
    copy = pltpu.make_async_copy(field_ref, out_any, sem)
    copy.start()
    copy.wait()


def last_scatter(emit_cell, emit, parts, field):
    return call(
        last_kernel,
        jax.ShapeDtypeStruct((1024, 256), f32),
        (1 << 20, 2 << 20),
        scalars=[emit_cell],
        arrays=[emit, parts, field],
        scratch=[VMEM((128, 256), f32), DMA],
        result=HBM,
    )


def spread_kernel(parts_ref, *refs):
    *value_refs, out_ref = refs
    sums = [parts_ref[b] for b in range(4)]
    for b in range(4, 32):
        sums[b % 4] = sums[b % 4] + parts_ref[b]
    total = (sums[0] + sums[1]) + (sums[2] + sums[3])
    if not value_refs:
        for s in range(8):
            out_ref[s] = total[s : s + 1, :]
        return
    value = jnp.broadcast_to(value_refs[0][...], (8, 128))
    for s in range(8):
        out_ref[s, 0:8, :] = total
        out_ref[s, 8:16, :] = value


def spread(parts, *value):
    out = VMEM((8, 16 if value else 1, 128), f32)
    return call(spread_kernel, out, (1 << 15, 1 << 17), arrays=[parts, *value])


def exchange(array, axis):
    return lax.all_to_all(array, axis, 0, 0, tiled=True)


def halos(even_plane, odd_plane):
    size = lax.axis_size("brick")
    even = lax.ppermute(even_plane, "brick", [(i, i ^ 1) for i in range(size)])
    odd = lax.ppermute(odd_plane, "brick", [(i, ((i + 1) ^ 1) - 1) for i in range(1, size - 1)])
    return even, odd


def steps(field_prev, field_now, diag, cross, green, delays, past, rec_cell, emit_cell):
    rank = lax.axis_index("shot").reshape(1)
    odd_brick = (lax.axis_index("brick") & 1).reshape(1)
    past = past[:, 0]

    current = field_now.reshape(1024, 256)
    before = field_prev.reshape(1024, 256)
    message, *planes, rec, emit, own, delay = first_message(rank, odd_brick, delays, rec_cell, emit_cell, past, current)
    first = exchange(message, "shot")
    even, odd = halos(*planes)
    right = turn(green[0])
    following, value = stencil(True, False, odd_brick, rec_cell, rec, current, before, diag, cross, even, odd)
    partial = emission_start(first, delay, right)
    parts = exchange(partial, "brick")
    old = older(first, delay)
    message = spread(parts, value)

    answer = exchange(message, "shot")
    partial, mine, sample1 = samples_and_emission(1, answer, first, old, delay, own, [], right)
    earlier = current
    current, *planes = scatter(odd_brick, emit_cell, emit, mine, following)
    even, odd = halos(*planes)
    parts = exchange(partial, "brick")
    following, value = stencil(True, True, odd_brick, rec_cell, rec, current, earlier, diag, cross, even, odd)
    message = spread(parts, value)

    answer = exchange(message, "shot")
    partial, mine, sample2 = samples_and_emission(2, answer, first, old, delay, own, [sample1], right)
    parts = exchange(partial, "brick")
    earlier = current
    current, *planes, recorded = scatter(odd_brick, emit_cell, emit, mine, following, (own, first, sample1, sample2))
    even, odd = halos(*planes)
    (following,) = stencil(False, True, odd_brick, rec_cell, rec, current, earlier, diag, cross, even, odd)
    message = spread(parts)
    parts = exchange(message, "shot")
    after = last_scatter(emit_cell, emit, parts, following)
    shape = field_now.shape
    return current.reshape(shape), after.reshape(shape), recorded[:, None]


def solution(mesh):
    return jax.shard_map(
        steps,
        mesh=mesh,
        in_specs=(
            P("shot", "brick", None, None),
            P("shot", "brick", None, None),
            P(None, "brick", None, None),
            P(None, "brick", None, None),
            P("shot", None, "brick"),
            P(),
            P(None, "shot", "brick"),
            P("shot", "brick"),
            P("shot", "brick"),
        ),
        out_specs=(
            P("shot", "brick", None, None),
            P("shot", "brick", None, None),
            P(None, "shot", "brick"),
        ),
        check_vma=False,
    )
```

```python
import functools

import jax
import jax.numpy as jnp
from jax import lax
from jax.experimental import pallas as pl
from jax.experimental.pallas import tpu as pltpu
from jax.sharding import PartitionSpec as P


VMEM = pltpu.VMEM
SMEM = pltpu.SMEM
HBM = pltpu.HBM
DMA = pltpu.SemaphoreType.DMA
f32 = jnp.float32


def spec(space):
    return pl.BlockSpec(memory_space=space)


def near(array):
    return pltpu.with_memory_space_constraint(array, pltpu.MemorySpace.VMEM)


def distant(array):
    return pltpu.with_memory_space_constraint(array, pltpu.MemorySpace.HBM)


def call(kernel, out_shape, work, scalars=(), arrays=(), far=(), free=(), scratch=(), aliases=None, room=2, result=VMEM):
    flops, moved = work
    return pl.pallas_call(
        kernel,
        out_shape=out_shape,
        in_specs=[spec(SMEM)] * len(scalars) + [spec(VMEM)] * len(arrays) + [spec(HBM)] * len(far) + [spec(pl.ANY)] * len(free),
        out_specs=jax.tree.map(lambda _: spec(result), out_shape),
        scratch_shapes=list(scratch),
        input_output_aliases=aliases or {},
        cost_estimate=pl.CostEstimate(flops=flops, bytes_accessed=moved, transcendentals=0),
        compiler_params=pltpu.CompilerParams(vmem_limit_bytes=room << 20),
    )(*scalars, *[near(a) for a in arrays], *[distant(a) for a in far], *free)


def sheet_of(row, width):
    tall = jnp.transpose(jnp.broadcast_to(row, (128, 128)))
    return jnp.concatenate([tall] * (width // 128), axis=1)


def lanes_of(cells):
    column = sheet_of((cells & 255).astype(f32), 256).astype(jnp.int32)
    return lax.broadcasted_iota(jnp.int32, (128, 256), 1) == column


def gather_row(field_ref, cell_smem, cell_vec, rows_ref):
    for j in range(128):
        row = cell_smem[0, j] >> 8
        rows_ref[j : j + 1, :] = field_ref[pl.ds(row, 1), :]
    picked = jnp.where(lanes_of(cell_vec), rows_ref[...], 0.0)
    return jnp.sum(jnp.transpose(picked[:, :128] + picked[:, 128:]), axis=0, keepdims=True)


def copies(pairs, sems):
    started = [pltpu.make_async_copy(a, b, sems.at[k]) for k, (a, b) in enumerate(pairs)]
    for copy in started:
        copy.start()
    return started


def first_kernel(
    rank,
    odd_brick,
    field_any,
    past_any,
    rec_any,
    emit_any,
    delays_any,
    out_ref,
    even_ref,
    odd_ref,
    rec_ref,
    emit_ref,
    own_ref,
    delay_ref,
    field_ref,
    rows_ref,
    past_ref,
    cell_smem,
    delays,
    sems,
):
    pairs = [(rec_any, cell_smem), (delays_any, delays), (field_any, field_ref), (past_any, past_ref)]
    started = copies(pairs + [(rec_any, rec_ref), (emit_any, emit_ref)], sems)
    own = lax.broadcasted_iota(jnp.int32, (8, 128), 0) == rank[0]
    own_ref[...] = jnp.where(own, 1.0, 0.0)
    for copy in started:
        copy.wait()
    delay_ref[...] = jnp.full((8, 128), delays[rank[0]], jnp.int32)
    sample = gather_row(field_ref, cell_smem, rec_ref[...], rows_ref)
    rows = [past_ref[...].astype(f32), sample.astype(jnp.bfloat16).astype(f32)]
    rows += [rec_ref[...].astype(f32), emit_ref[...].astype(f32), jnp.zeros((5, 128), f32)]
    message = jnp.concatenate(rows, axis=0)
    for s in range(8):
        out_ref[s] = message
    edges(odd_brick, field_ref, even_ref, odd_ref)
    cells = jnp.broadcast_to(emit_ref[...].astype(f32), (8, 128))
    for ref in (even_ref, odd_ref):
        ref[256:264, 0:128] = cells
        ref[256:264, 128:256] = cells


def edges(odd_brick, field_ref, even_ref, odd_ref):
    even_ref[0:256, :] = field_ref[pl.ds(pl.multiple_of(768 - 768 * odd_brick[0], 256), 256), :]
    odd_ref[0:256, :] = field_ref[pl.ds(pl.multiple_of(768 * odd_brick[0], 256), 256), :]


def first_message(rank, odd_brick, delays, rec_cell, emit_cell, past, field):
    plane = VMEM((264, 256), f32)
    row = VMEM((1, 128), jnp.int32)
    return call(
        first_kernel,
        (VMEM((8, 16, 128), f32), plane, plane, row, row, VMEM((8, 128), f32), VMEM((8, 128), jnp.int32)),
        (1 << 20, 1 << 19),
        scalars=[rank, odd_brick],
        far=[field, past, rec_cell, emit_cell, delays],
        scratch=[
            VMEM((1024, 256), f32),
            VMEM((128, 256), f32),
            VMEM((8, 128), jnp.bfloat16),
            SMEM((1, 128), jnp.int32),
            SMEM((8,), jnp.int32),
            DMA((6,)),
        ],
        room=3,
    )


def turn_kernel(green_ref, right_ref):
    for b in range(32):
        at = slice(b * 128, (b + 1) * 128)
        right_ref[:, at] = jnp.transpose(green_ref[at, :])


def turn(green):
    return call(turn_kernel, VMEM((128, 4096), jnp.bfloat16), (1 << 20, 1 << 20), arrays=[green])


def older_kernel(first_ref, delay_ref, old_ref):
    for moment in (1, 2):
        old_ref[moment - 1] = old_samples(first_ref, 8 + moment - delay_ref[...])


def older(first, delay):
    out = VMEM((2, 8, 128), f32)
    return call(older_kernel, out, (1 << 20, 1 << 18), arrays=[first, delay])


def matches(first_ref):
    blocks = []
    for s in range(8):
        rec = first_ref[s, 9:10, :]
        emit = first_ref[s, 10:11, :]
        same = sheet_of(emit, 128) == jnp.broadcast_to(rec, (128, 128))
        blocks.append(jnp.where(same, 1.0, 0.0).astype(jnp.bfloat16))
    return jnp.concatenate(blocks, axis=0)


def multiply(chosen, right_ref, out_ref):
    product = jnp.dot(chosen.astype(jnp.bfloat16), right_ref[...], preferred_element_type=f32)
    wide = out_ref.shape[1] == 24
    for b in range(32):
        block = product[:, b * 128 : (b + 1) * 128]
        if not wide:
            out_ref[b] = block
            continue
        out_ref[b, 8:16, :] = block
        if b < 31:
            out_ref[b + 1, 0:8, :] = block
        if b > 0:
            out_ref[b - 1, 16:24, :] = block
    if wide:
        out_ref[0, 0:8, :] = jnp.zeros((8, 128), f32)
        out_ref[31, 16:24, :] = jnp.zeros((8, 128), f32)


def old_samples(first_ref, where):
    chosen = jnp.zeros((8, 128), f32)
    for k in range(9):
        series = jnp.concatenate([first_ref[s, k : k + 1, :] for s in range(8)], axis=0)
        chosen = jnp.where(where == k, series, chosen)
    return chosen


def start_kernel(first_ref, delay_ref, right_ref, out_ref):
    multiply(old_samples(first_ref, 8 - delay_ref[...]), right_ref, out_ref)


def emission_start(first, delay, right):
    out = VMEM((32, 24, 128), f32)
    return call(start_kernel, out, (8 << 20, 1 << 20), arrays=[first, delay, right])


def samples_kernel(moment, message_ref, first_ref, old_ref, delay_ref, own_ref, *refs):
    *newer_refs, right_ref, out_ref, mine_ref, near_ref, sample_ref = refs
    total = message_ref[0, 0:8, :]
    for lag in range(1, 8):
        total = total + message_ref[lag, 0:8, :]
    near = message_ref[0, 8:16, :]
    for lag in range(1, 8):
        near = near + message_ref[lag, 8:16, :]
    near_ref[...] = near
    values = jnp.concatenate([message_ref[s, 8:9, :] for s in range(8)], axis=0)
    wide = jnp.concatenate([total] * 8, axis=1)
    block = lax.broadcasted_iota(jnp.int32, (8, 1024), 1) >> 7
    wide = jnp.where(block == lax.broadcasted_iota(jnp.int32, (8, 1024), 0), wide, 0.0)
    high = wide.astype(jnp.bfloat16)
    rest = wide - high.astype(f32)
    middle = rest.astype(jnp.bfloat16)
    low = (rest - middle.astype(f32)).astype(jnp.bfloat16)
    parts = jnp.concatenate([high, middle, low], axis=0)
    added = jnp.dot(parts, matches(first_ref), preferred_element_type=f32)
    values = values + ((added[16:24] + added[8:16]) + added[0:8])
    sample = values.astype(jnp.bfloat16).astype(f32)
    delay = delay_ref[...]
    chosen = old_ref[moment - 1]
    for k, newer_ref in enumerate(newer_refs):
        chosen = jnp.where(delay == moment - 1 - k, newer_ref[...], chosen)
    chosen = jnp.where(delay == 0, sample, chosen)
    multiply(chosen, right_ref, out_ref)
    sample_ref[...] = sample
    mine_ref[...] = jnp.sum(jnp.where(own_ref[...] > 0.5, total, 0.0), axis=0, keepdims=True)


def samples_and_emission(moment, message, first, old, delay, own, newer, right):
    return call(
        functools.partial(samples_kernel, moment),
        (VMEM((32, 24 if moment == 1 else 8, 128), f32), VMEM((1, 128), f32), VMEM((8, 128), f32), VMEM((8, 128), f32)),
        (8 << 20, 1 << 20),
        arrays=[message, first, old, delay, own, *newer, right],
    )


def spots(values, cells, plane):
    cells = cells.astype(jnp.int32)
    values = jnp.where((cells >> 16) == plane, values, 0.0)
    column = sheet_of(((cells >> 8) & 255).astype(f32), 256).astype(jnp.int32)
    rows = jnp.where(lax.broadcasted_iota(jnp.int32, (128, 256), 1) == column, 1.0, 0.0).astype(jnp.bfloat16)
    rest = jnp.where(lanes_of(cells), sheet_of(values, 256), 0.0)
    terms = []
    for _ in range(3):
        term = rest.astype(jnp.bfloat16)
        rest = rest - term.astype(f32)
        terms.append(lax.dot_general(rows, term, (((0,), (0,)), ((), ())), preferred_element_type=f32))
    return (terms[2] + terms[1]) + terms[0]


def stencil_kernel(take, inside, odd_brick, cell_smem, cell_vec, *refs):
    if inside:
        near_ref, near_cells_ref, *refs = refs
    field_in, prev_any, diag_any, cross_any, even_any, odd_any, *refs = refs
    *outs, rows_ref, field_ref, prev_ref, diag_ref, cross_ref, low_ref, high_ref, skew_ref, sum_ref, sems, edge_sems = refs
    out_ref, *outs = outs
    order = (1, 2, 0, 3)

    def part(x):
        return pl.ds(256 * x, 256)

    begun = {}
    if inside:
        field_ref = field_in
    else:
        for x in (0, 1, 2, 3):
            begun[x] = copies([(field_in.at[part(x)], field_ref.at[part(x)])], sems.at[x, pl.ds(7, 1)])
    started = {}
    for x in order:
        pairs = [(diag_any.at[k, x], diag_ref.at[k, x]) for k in range(3)]
        pairs += [(cross_any.at[k, x], cross_ref.at[k, x]) for k in range(3)]
        started[x] = copies([(prev_any.at[part(x)], prev_ref.at[part(x)])] + pairs, sems.at[x])

    @pl.when(odd_brick[0] == 0)
    def _():
        copies([(even_any, high_ref), (odd_any, low_ref)], edge_sems)

    @pl.when(odd_brick[0] == 1)
    def _():
        copies([(even_any, low_ref), (odd_any, high_ref)], edge_sems)

    lane = lax.broadcasted_iota(jnp.int32, (8, 128), 1)
    sub = lax.broadcasted_iota(jnp.int32, (8, 128), 0)
    zero = jnp.zeros((8, 128), f32)
    first_lane, last_lane = lane == 0, lane == 127
    first_sub, last_sub = sub == 0, sub == 7

    def at(ref, where, row):
        rows = slice(row, row + 8)
        return ref[(*where, rows, slice(0, 128))], ref[(*where, rows, slice(128, 256))]

    def put(ref, row, pair):
        for h in range(2):
            ref[row : row + 8, 128 * h : 128 * h + 128] = pair[h]

    def each(f, *pairs):
        return tuple(f(*vs) for vs in zip(*pairs))

    def plus(a, b):
        return each(lambda v, w: v + w, a, b)

    def minus(a, b):
        return each(lambda v, w: v - w, a, b)

    def source(x):
        if x < 0:
            return low_ref, 0
        if x > 3:
            return high_ref, 0
        return field_ref, 256 * x

    def along_z(x):
        ref, base = source(x)
        for t in range(32):
            a, b = at(ref, (), base + 8 * t)
            up_a, up_b = pltpu.roll(a, 127, 1), pltpu.roll(b, 127, 1)
            down_a, down_b = pltpu.roll(a, 1, 1), pltpu.roll(b, 1, 1)
            ahead = (jnp.where(last_lane, up_b, up_a), jnp.where(last_lane, 0.0, up_b))
            behind = (jnp.where(first_lane, 0.0, down_a), jnp.where(first_lane, down_a, down_b))
            put(skew_ref, 256 * (x + 1) + 8 * t, minus(ahead, behind))
            if 0 <= x < 4:
                put(sum_ref, 256 * x + 8 * t, plus(ahead, behind))

    ready = {1: (0, 1, 2), 2: (3,), 0: (-1,), 3: (4,)}
    for x in order:
        if x == 0:
            for k in (0, 1):
                pltpu.make_async_copy(odd_any, low_ref, edge_sems.at[k]).wait()
            if inside:
                low_ref[...] = low_ref[...] + spots(near_ref[1:2, :], near_cells_ref[0:1, :], 3)
                high_ref[...] = high_ref[...] + spots(near_ref[2:3, :], near_cells_ref[1:2, :], 0)
            else:
                outs[-1][0:1, :] = low_ref[256:257, 0:128]
                outs[-1][1:2, :] = high_ref[256:257, 0:128]
        for k in ready[x]:
            for copy in begun.get(k, ()):
                copy.wait()
            along_z(k)
        for copy in started[x]:
            copy.wait()

        def turned(pair):
            return tuple(pltpu.roll(v, 7, 0) for v in pair), tuple(pltpu.roll(v, 1, 0) for v in pair)

        edge = ((zero, zero), (zero, zero))
        tiles = {}
        turns = {-1: (edge, edge, edge), 32: (edge, edge, edge)}

        def fetch(t):
            mid, ahead, behind = (at(ref, (), base + 8 * t) for ref, base in map(source, (x, x + 1, x - 1)))
            slope = minus(ahead, behind)
            skew = at(skew_ref, (), 256 * (x + 1) + 8 * t)
            tiles[t] = mid, plus(ahead, behind)
            turns[t] = turned(mid), turned(slope), turned(skew)

        def after_y(t, k):
            return each(lambda a, b: jnp.where(last_sub, b, a), turns[t][k][0], turns[t + 1][k][0])

        def before_y(t, k):
            return each(lambda a, b: jnp.where(first_sub, b, a), turns[t][k][1], turns[t - 1][k][1])

        fetch(0)
        for t in range(32):
            if t < 31:
                fetch(t + 1)
            row = 8 * t
            mid, sum_x = tiles.pop(t)
            sum_y = plus(after_y(t, 0), before_y(t, 0))
            sum_z = at(sum_ref, (), 256 * x + row)
            skew_xy = minus(after_y(t, 1), before_y(t, 1))
            skew_xz = minus(at(skew_ref, (), 256 * (x + 2) + row), at(skew_ref, (), 256 * x + row))
            skew_yz = minus(after_y(t, 2), before_y(t, 2))
            diag = [at(diag_ref, (k, x), row) for k in range(3)]
            cross = [at(cross_ref, (k, x), row) for k in range(3)]
            prev = at(prev_ref, (), 256 * x + row)
            values = []
            for h in range(2):
                d0, d1, d2 = (d[h] for d in diag)
                c0, c1, c2 = (c[h] for c in cross)
                twice = mid[h] + mid[h]
                second = d0 * (sum_x[h] - twice) + d1 * (sum_y[h] - twice) + d2 * (sum_z[h] - twice)
                mixed = c0 * skew_xy[h] + c1 * skew_xz[h] + c2 * skew_yz[h]
                values.append((twice - prev[h]) + (second + 0.5 * mixed))
            put(out_ref, 256 * x + row, values)
    if take:
        edges(odd_brick, out_ref, outs[1], outs[2])
        outs[0][...] = gather_row(out_ref, cell_smem, cell_vec[...], rows_ref)


def stencil(take, odd_brick, rec_cell, rec, field, prev, diag, cross, even, odd, near=()):
    plane = VMEM((256, 256), f32)
    inside = bool(near)
    out_shape = [VMEM((1024, 256), f32)]
    if take:
        out_shape += [VMEM((1, 128), f32), plane, plane]
    if not inside:
        out_shape.append(VMEM((8, 128), f32))
    coef = VMEM((3, 4, 256, 256), f32)
    whole = VMEM((1024, 256), f32)
    edge = VMEM(even.shape, f32)
    scratch = [VMEM((128, 256), f32), VMEM((8, 128), f32) if inside else whole, whole, coef, coef, edge, edge]
    scratch += [VMEM((1536, 256), f32), whole, DMA((4, 8)), DMA((2,))]
    return call(
        functools.partial(stencil_kernel, take, inside),
        tuple(out_shape),
        (16 << 20, 10 << 20),
        scalars=[odd_brick, rec_cell],
        arrays=[rec, *near] + [field] * inside,
        far=[field] * (not inside) + [prev, diag, cross] + [even, odd] * (inside and take),
        free=[even, odd] * (not inside or not take),
        scratch=scratch,
        room=14,
    )


def add_at(cell_smem, cell_vec, value, target_ref, rows_ref):
    rows_ref[...] = jnp.where(lanes_of(cell_vec[...]), sheet_of(value, 256), 0.0)
    for j in range(128):
        row = cell_smem[0, j] >> 8
        target_ref[pl.ds(row, 1), :] = target_ref[pl.ds(row, 1), :] + rows_ref[j : j + 1, :]


def scatter_kernel(cell_smem, cell_vec, mine_ref, field_ref, *refs):
    *refs, rows_ref = refs
    del field_ref
    old = refs[:-2]
    add_at(cell_smem, cell_vec, mine_ref[...], refs[-2] if old else refs[-1], rows_ref)
    if old:
        own_ref, first_ref, *sample_refs = old
        own = own_ref[...] > 0.5
        start = jnp.concatenate([first_ref[s, 8:9, :] for s in range(8)], axis=0)
        series = [start] + [s[...] for s in sample_refs]
        series = [jnp.sum(jnp.where(own, s, 0.0), axis=0, keepdims=True) for s in series]
        refs[-1][...] = jnp.concatenate(series, axis=0).astype(jnp.bfloat16)


def scatter(emit_cell, emit, mine, field, old=()):
    outs = [VMEM((1024, 256), f32)]
    if old:
        outs.append(VMEM((3, 128), jnp.bfloat16))
    return call(
        scatter_kernel,
        tuple(outs),
        (1 << 20, 1 << 19),
        scalars=[emit_cell],
        arrays=[emit, mine, field, *old],
        scratch=[VMEM((128, 256), f32)],
        aliases={3: 0},
    )


def last_kernel(cell_smem, cell_vec, parts_ref, field_ref, out_any, rows_ref, sem):
    value = parts_ref[0]
    for lag in range(1, 8):
        value = value + parts_ref[lag]
    add_at(cell_smem, cell_vec, value, field_ref, rows_ref)
    copy = pltpu.make_async_copy(field_ref, out_any, sem)
    copy.start()
    copy.wait()


def last_scatter(emit_cell, emit, parts, field):
    return call(
        last_kernel,
        jax.ShapeDtypeStruct((1024, 256), f32),
        (1 << 20, 2 << 20),
        scalars=[emit_cell],
        arrays=[emit, parts, field],
        scratch=[VMEM((128, 256), f32), DMA],
        result=HBM,
    )


def spread_kernel(parts_ref, *refs):
    *value_refs, out_ref = refs
    sums = [parts_ref[b] for b in range(4)]
    for b in range(4, 32):
        sums[b % 4] = sums[b % 4] + parts_ref[b]
    total = (sums[0] + sums[1]) + (sums[2] + sums[3])
    for s in range(8):
        if not value_refs:
            out_ref[s] = total[s : s + 1, :]
            continue
        out_ref[s, 0:8, :] = total[8:16]
        rows = [value_refs[0][...], total[s : s + 1], total[16 + s : 17 + s], jnp.zeros((5, 128), f32)]
        out_ref[s, 8:16, :] = jnp.concatenate(rows, axis=0)


def spread(parts, *value):
    out = VMEM((8, 16 if value else 1, 128), f32)
    return call(spread_kernel, out, (1 << 15, 1 << 17), arrays=[parts, *value])


def exchange(array, axis):
    return lax.all_to_all(array, axis, 0, 0, tiled=True)


def halos(even_plane, odd_plane):
    size = lax.axis_size("brick")
    even = lax.ppermute(even_plane, "brick", [(i, i ^ 1) for i in range(size)])
    odd = lax.ppermute(odd_plane, "brick", [(i, ((i + 1) ^ 1) - 1) for i in range(1, size - 1)])
    return even, odd


def steps(field_prev, field_now, diag, cross, green, delays, past, rec_cell, emit_cell):
    rank = lax.axis_index("shot").reshape(1)
    odd_brick = (lax.axis_index("brick") & 1).reshape(1)
    past = past[:, 0]

    current = field_now.reshape(1024, 256)
    before = field_prev.reshape(1024, 256)
    message, *planes, rec, emit, own, delay = first_message(rank, odd_brick, delays, rec_cell, emit_cell, past, current)
    first = exchange(message, "shot")
    even, odd = halos(*planes)
    right = turn(green[0])
    following, value, *planes, cells = stencil(True, odd_brick, rec_cell, rec, current, before, diag, cross, even, odd)
    partial = emission_start(first, delay, right)
    parts = exchange(partial, "brick")
    old = older(first, delay)
    message = spread(parts, value)

    answer = exchange(message, "shot")
    even, odd = halos(*planes)
    partial, mine, near, sample1 = samples_and_emission(1, answer, first, old, delay, own, [], right)
    parts = exchange(partial, "brick")
    earlier = current
    (current,) = scatter(emit_cell, emit, mine, following)
    following, value, *planes = stencil(
        True, odd_brick, rec_cell, rec, current, earlier, diag, cross, even, odd, (near, cells)
    )
    message = spread(parts, value)

    answer = exchange(message, "shot")
    even, odd = halos(*planes)
    partial, mine, near, sample2 = samples_and_emission(2, answer, first, old, delay, own, [sample1], right)
    parts = exchange(partial, "brick")
    earlier = current
    current, recorded = scatter(emit_cell, emit, mine, following, (own, first, sample1, sample2))
    message = spread(parts)
    parts = exchange(message, "shot")
    (following,) = stencil(
        False, odd_brick, rec_cell, rec, current, earlier, diag, cross, even, odd, (near, cells)
    )
    after = last_scatter(emit_cell, emit, parts, following)
    shape = field_now.shape
    return current.reshape(shape), after.reshape(shape), recorded[:, None]


def solution(mesh):
    return jax.shard_map(
        steps,
        mesh=mesh,
        in_specs=(
            P("shot", "brick", None, None),
            P("shot", "brick", None, None),
            P(None, "brick", None, None),
            P(None, "brick", None, None),
            P("shot", None, "brick"),
            P(),
            P(None, "shot", "brick"),
            P("shot", "brick"),
            P("shot", "brick"),
        ),
        out_specs=(
            P("shot", "brick", None, None),
            P("shot", "brick", None, None),
            P(None, "shot", "brick"),
        ),
        check_vma=False,
    )
```

```python
import functools

import jax
import jax.numpy as jnp
from jax import lax
from jax.experimental import pallas as pl
from jax.experimental.pallas import tpu as pltpu
from jax.sharding import PartitionSpec as P


VMEM = pltpu.VMEM
SMEM = pltpu.SMEM
HBM = pltpu.HBM
DMA = pltpu.SemaphoreType.DMA
f32 = jnp.float32


def spec(space):
    return pl.BlockSpec(memory_space=space)


def near(array):
    return pltpu.with_memory_space_constraint(array, pltpu.MemorySpace.VMEM)


def distant(array):
    return pltpu.with_memory_space_constraint(array, pltpu.MemorySpace.HBM)


def call(kernel, out_shape, work, scalars=(), arrays=(), far=(), free=(), scratch=(), aliases=None, room=2):
    flops, moved = work
    return pl.pallas_call(
        kernel,
        out_shape=out_shape,
        in_specs=[spec(SMEM)] * len(scalars) + [spec(VMEM)] * len(arrays) + [spec(HBM)] * len(far) + [spec(pl.ANY)] * len(free),
        out_specs=jax.tree.map(lambda o: spec(HBM if o.memory_space == HBM else VMEM), out_shape),
        scratch_shapes=list(scratch),
        input_output_aliases=aliases or {},
        cost_estimate=pl.CostEstimate(flops=flops, bytes_accessed=moved, transcendentals=0),
        compiler_params=pltpu.CompilerParams(vmem_limit_bytes=room << 20),
    )(*scalars, *[near(a) for a in arrays], *[distant(a) for a in far], *free)


def sheet_of(row, width):
    tall = jnp.transpose(jnp.broadcast_to(row, (128, 128)))
    return jnp.concatenate([tall] * (width // 128), axis=1)


def lanes_of(cells):
    column = sheet_of((cells & 255).astype(f32), 256).astype(jnp.int32)
    return lax.broadcasted_iota(jnp.int32, (128, 256), 1) == column


def gather_row(field_ref, cell_smem, cell_vec, rows_ref):
    for j in range(128):
        row = cell_smem[0, j] >> 8
        rows_ref[j : j + 1, :] = field_ref[pl.ds(row, 1), :]
    picked = jnp.where(lanes_of(cell_vec), rows_ref[...], 0.0)
    return jnp.sum(jnp.transpose(picked[:, :128] + picked[:, 128:]), axis=0, keepdims=True)


def copies(pairs, sems):
    started = [pltpu.make_async_copy(a, b, sems.at[k]) for k, (a, b) in enumerate(pairs)]
    for copy in started:
        copy.start()
    return started


def first_kernel(
    rank,
    odd_brick,
    field_any,
    past_any,
    rec_any,
    emit_any,
    delays_any,
    green_any,
    out_ref,
    even_ref,
    odd_ref,
    rec_ref,
    emit_ref,
    own_ref,
    delay_ref,
    green_ref,
    field_ref,
    rows_ref,
    past_ref,
    cell_smem,
    delays,
    sems,
):
    pairs = [(rec_any, cell_smem), (delays_any, delays), (field_any, field_ref), (past_any, past_ref)]
    started = copies(pairs + [(rec_any, rec_ref), (emit_any, emit_ref), (green_any, green_ref)], sems)
    own = lax.broadcasted_iota(jnp.int32, (8, 128), 0) == rank[0]
    own_ref[...] = jnp.where(own, 1.0, 0.0)
    for copy in started[:-1]:
        copy.wait()
    delay_ref[...] = jnp.full((8, 128), delays[rank[0]], jnp.int32)
    sample = gather_row(field_ref, cell_smem, rec_ref[...], rows_ref)
    rows = [past_ref[...].astype(f32), sample.astype(jnp.bfloat16).astype(f32)]
    rows += [rec_ref[...].astype(f32), emit_ref[...].astype(f32), jnp.zeros((5, 128), f32)]
    message = jnp.concatenate(rows, axis=0)
    for s in range(8):
        out_ref[s] = message
    edges(odd_brick, field_ref, even_ref, odd_ref)
    cells = jnp.broadcast_to(emit_ref[...].astype(f32), (8, 128))
    for ref in (even_ref, odd_ref):
        ref[256:264, 0:128] = cells
        ref[256:264, 128:256] = cells
    started[-1].wait()


def edges(odd_brick, field_ref, even_ref, odd_ref):
    even_ref[0:256, :] = field_ref[pl.ds(pl.multiple_of(768 - 768 * odd_brick[0], 256), 256), :]
    odd_ref[0:256, :] = field_ref[pl.ds(pl.multiple_of(768 * odd_brick[0], 256), 256), :]


def first_message(rank, odd_brick, delays, rec_cell, emit_cell, past, field, green):
    plane = VMEM((264, 256), f32)
    row = VMEM((1, 128), jnp.int32)
    return call(
        first_kernel,
        (
            VMEM((8, 16, 128), f32),
            plane,
            plane,
            row,
            row,
            VMEM((8, 128), f32),
            VMEM((8, 128), jnp.int32),
            VMEM((4096, 128), jnp.bfloat16),
        ),
        (1 << 20, 1 << 19),
        scalars=[rank, odd_brick],
        far=[field, past, rec_cell, emit_cell, delays, green],
        scratch=[
            VMEM((1024, 256), f32),
            VMEM((128, 256), f32),
            VMEM((8, 128), jnp.bfloat16),
            SMEM((1, 128), jnp.int32),
            SMEM((8,), jnp.int32),
            DMA((7,)),
        ],
        room=3,
    )


def turn_kernel(green_ref, right_ref):
    for b in range(32):
        at = slice(b * 128, (b + 1) * 128)
        right_ref[:, at] = jnp.transpose(green_ref[at, :])


def turn(green):
    return call(turn_kernel, VMEM((128, 4096), jnp.bfloat16), (1 << 20, 1 << 20), arrays=[green])


def older_kernel(first_ref, delay_ref, old_ref):
    for moment in (1, 2):
        old_ref[moment - 1] = old_samples(first_ref, 8 + moment - delay_ref[...])


def older(first, delay):
    out = VMEM((2, 8, 128), f32)
    return call(older_kernel, out, (1 << 20, 1 << 18), arrays=[first, delay])


def matches(first_ref):
    blocks = []
    for s in range(8):
        rec = first_ref[s, 9:10, :]
        emit = first_ref[s, 10:11, :]
        same = sheet_of(emit, 128) == jnp.broadcast_to(rec, (128, 128))
        blocks.append(jnp.where(same, 1.0, 0.0).astype(jnp.bfloat16))
    return jnp.concatenate(blocks, axis=0)


def multiply(chosen, right_ref, out_ref):
    product = jnp.dot(chosen.astype(jnp.bfloat16), right_ref[...], preferred_element_type=f32)
    if out_ref.shape[0] == 256:
        for b in range(32):
            out_ref[pl.ds(b, 8, stride=32), :] = product[:, b * 128 : (b + 1) * 128]
        return
    for b in range(32):
        block = product[:, b * 128 : (b + 1) * 128]
        out_ref[b, 8:16, :] = block
        if b < 31:
            out_ref[b + 1, 0:8, :] = block
        if b > 0:
            out_ref[b - 1, 16:24, :] = block
    out_ref[0, 0:8, :] = jnp.zeros((8, 128), f32)
    out_ref[31, 16:24, :] = jnp.zeros((8, 128), f32)


def old_samples(first_ref, where):
    chosen = jnp.zeros((8, 128), f32)
    for k in range(9):
        series = jnp.concatenate([first_ref[s, k : k + 1, :] for s in range(8)], axis=0)
        chosen = jnp.where(where == k, series, chosen)
    return chosen


def start_kernel(first_ref, delay_ref, right_ref, out_ref):
    multiply(old_samples(first_ref, 8 - delay_ref[...]), right_ref, out_ref)


def emission_start(first, delay, right):
    out = VMEM((32, 24, 128), f32)
    return call(start_kernel, out, (8 << 20, 1 << 20), arrays=[first, delay, right])


def samples_kernel(moment, message_ref, first_ref, old_ref, delay_ref, own_ref, *refs):
    *newer_refs, right_ref, out_ref, mine_ref, near_ref, sample_ref = refs
    total = message_ref[0, 0:8, :]
    for lag in range(1, 8):
        total = total + message_ref[lag, 0:8, :]
    near = message_ref[0, 8:16, :]
    for lag in range(1, 8):
        near = near + message_ref[lag, 8:16, :]
    near_ref[...] = near
    values = jnp.concatenate([message_ref[s, 8:9, :] for s in range(8)], axis=0)
    wide = jnp.concatenate([total] * 8, axis=1)
    block = lax.broadcasted_iota(jnp.int32, (8, 1024), 1) >> 7
    wide = jnp.where(block == lax.broadcasted_iota(jnp.int32, (8, 1024), 0), wide, 0.0)
    high = wide.astype(jnp.bfloat16)
    rest = wide - high.astype(f32)
    middle = rest.astype(jnp.bfloat16)
    low = (rest - middle.astype(f32)).astype(jnp.bfloat16)
    parts = jnp.concatenate([high, middle, low], axis=0)
    added = jnp.dot(parts, matches(first_ref), preferred_element_type=f32)
    values = values + ((added[16:24] + added[8:16]) + added[0:8])
    sample = values.astype(jnp.bfloat16).astype(f32)
    delay = delay_ref[...]
    chosen = old_ref[moment - 1]
    for k, newer_ref in enumerate(newer_refs):
        chosen = jnp.where(delay == moment - 1 - k, newer_ref[...], chosen)
    chosen = jnp.where(delay == 0, sample, chosen)
    multiply(chosen, right_ref, out_ref)
    sample_ref[...] = sample
    mine_ref[...] = jnp.sum(jnp.where(own_ref[...] > 0.5, total, 0.0), axis=0, keepdims=True)


def samples_and_emission(moment, message, first, old, delay, own, newer, right):
    return call(
        functools.partial(samples_kernel, moment),
        (VMEM((32, 24, 128) if moment == 1 else (256, 128), f32), VMEM((1, 128), f32), VMEM((8, 128), f32), VMEM((8, 128), f32)),
        (8 << 20, 1 << 20),
        arrays=[message, first, old, delay, own, *newer, right],
    )


def spots(values, cells, plane):
    cells = cells.astype(jnp.int32)
    values = jnp.where((cells >> 16) == plane, values, 0.0)
    column = sheet_of(((cells >> 8) & 255).astype(f32), 256).astype(jnp.int32)
    rows = jnp.where(lax.broadcasted_iota(jnp.int32, (128, 256), 1) == column, 1.0, 0.0).astype(jnp.bfloat16)
    rest = jnp.where(lanes_of(cells), sheet_of(values, 256), 0.0)
    terms = []
    for _ in range(3):
        term = rest.astype(jnp.bfloat16)
        rest = rest - term.astype(f32)
        terms.append(lax.dot_general(rows, term, (((0,), (0,)), ((), ())), preferred_element_type=f32))
    return (terms[2] + terms[1]) + terms[0]


def wave_kernel(step, odd_brick, rec_ref, *refs):
    refs = list(refs)

    def take(count):
        taken = refs[:count]
        del refs[:count]
        return taken

    emit_ref, mine_ref, near_ref, near_cells_ref = take(4) if step else [None] * 4
    own_ref, start_ref, *sample_refs = take(4) if step == 2 else [None] * 4
    rec_any, emit_any, field_any, prev_any, diag_any, cross_any, even_any, odd_any = take(8)
    out_any, *outs = take(5 if step < 2 else 3)
    field_ref, prev_ref, diag_ref, cross_ref, low_ref, high_ref, skew_ref, sum_ref = take(8)
    rows_ref, rec_smem, emit_smem, sems, edge_sems, cell_sems, end_sems = take(7)
    (out_ref,) = take(1) if step < 2 else [out_any]
    order = (1, 2, 0, 3)

    def part(x):
        return pl.ds(256 * x, 256)

    listed = copies([(rec_any, rec_smem), (emit_any, emit_smem)], cell_sems)
    begun = {}
    for x in (0, 1, 2, 3):
        begun[x] = copies([(field_any.at[part(x)], field_ref.at[part(x)])], sems.at[x, pl.ds(7, 1)])
    started = {}
    for x in order:
        pairs = [(diag_any.at[k, x], diag_ref.at[k, x]) for k in range(3)]
        pairs += [(cross_any.at[k, x], cross_ref.at[k, x]) for k in range(3)]
        started[x] = copies([(prev_any.at[part(x)], prev_ref.at[part(x)])] + pairs, sems.at[x])

    @pl.when(odd_brick[0] == 0)
    def _():
        copies([(even_any, high_ref), (odd_any, low_ref)], edge_sems)

    @pl.when(odd_brick[0] == 1)
    def _():
        copies([(even_any, low_ref), (odd_any, high_ref)], edge_sems)

    ending = []
    for copy in listed:
        copy.wait()
    if step:
        for x in (0, 1, 2, 3):
            begun.pop(x)[0].wait()
        add_at(emit_smem, emit_ref, mine_ref[...], field_ref, rows_ref)
        ending += copies([(field_ref, outs[-1])], end_sems.at[pl.ds(4, 1)])
    if step == 2:
        own = own_ref[...] > 0.5
        start = jnp.concatenate([start_ref[s, 8:9, :] for s in range(8)], axis=0)
        series = [start] + [s[...] for s in sample_refs]
        series = [jnp.sum(jnp.where(own, s, 0.0), axis=0, keepdims=True) for s in series]
        outs[0][...] = jnp.concatenate(series, axis=0).astype(jnp.bfloat16)

    lane = lax.broadcasted_iota(jnp.int32, (8, 128), 1)
    sub = lax.broadcasted_iota(jnp.int32, (8, 128), 0)
    zero = jnp.zeros((8, 128), f32)
    first_lane, last_lane = lane == 0, lane == 127
    first_sub, last_sub = sub == 0, sub == 7

    def at(ref, where, row):
        rows = slice(row, row + 8)
        return ref[(*where, rows, slice(0, 128))], ref[(*where, rows, slice(128, 256))]

    def put(ref, row, pair):
        for h in range(2):
            ref[row : row + 8, 128 * h : 128 * h + 128] = pair[h]

    def each(f, *pairs):
        return tuple(f(*vs) for vs in zip(*pairs))

    def plus(a, b):
        return each(lambda v, w: v + w, a, b)

    def minus(a, b):
        return each(lambda v, w: v - w, a, b)

    def source(x):
        if x < 0:
            return low_ref, 0
        if x > 3:
            return high_ref, 0
        return field_ref, 256 * x

    def along_z(x):
        ref, base = source(x)
        for t in range(32):
            a, b = at(ref, (), base + 8 * t)
            up_a, up_b = pltpu.roll(a, 127, 1), pltpu.roll(b, 127, 1)
            down_a, down_b = pltpu.roll(a, 1, 1), pltpu.roll(b, 1, 1)
            ahead = (jnp.where(last_lane, up_b, up_a), jnp.where(last_lane, 0.0, up_b))
            behind = (jnp.where(first_lane, 0.0, down_a), jnp.where(first_lane, down_a, down_b))
            put(skew_ref, 256 * (x + 1) + 8 * t, minus(ahead, behind))
            if 0 <= x < 4:
                put(sum_ref, 256 * x + 8 * t, plus(ahead, behind))

    ready = {1: (0, 1, 2), 2: (3,), 0: (-1,), 3: (4,)}
    for x in order:
        if x == 0:
            for k in (0, 1):
                pltpu.make_async_copy(odd_any, low_ref, edge_sems.at[k]).wait()
            if step:
                low_ref[...] = low_ref[...] + spots(near_ref[1:2, :], near_cells_ref[0:1, :], 3)
                high_ref[...] = high_ref[...] + spots(near_ref[2:3, :], near_cells_ref[1:2, :], 0)
            else:
                outs[3][0:1, :] = low_ref[256:257, 0:128]
                outs[3][1:2, :] = high_ref[256:257, 0:128]
        for k in ready[x]:
            for copy in begun.get(k, ()):
                copy.wait()
            along_z(k)
        for copy in started[x]:
            copy.wait()

        def turned(pair):
            return tuple(pltpu.roll(v, 7, 0) for v in pair), tuple(pltpu.roll(v, 1, 0) for v in pair)

        edge = ((zero, zero), (zero, zero))
        tiles = {}
        turns = {-1: (edge, edge, edge), 32: (edge, edge, edge)}

        def fetch(t):
            mid, ahead, behind = (at(ref, (), base + 8 * t) for ref, base in map(source, (x, x + 1, x - 1)))
            slope = minus(ahead, behind)
            skew = at(skew_ref, (), 256 * (x + 1) + 8 * t)
            tiles[t] = mid, plus(ahead, behind)
            turns[t] = turned(mid), turned(slope), turned(skew)

        def after_y(t, k):
            return each(lambda a, b: jnp.where(last_sub, b, a), turns[t][k][0], turns[t + 1][k][0])

        def before_y(t, k):
            return each(lambda a, b: jnp.where(first_sub, b, a), turns[t][k][1], turns[t - 1][k][1])

        fetch(0)
        for t in range(32):
            if t < 31:
                fetch(t + 1)
            row = 8 * t
            mid, sum_x = tiles.pop(t)
            sum_y = plus(after_y(t, 0), before_y(t, 0))
            sum_z = at(sum_ref, (), 256 * x + row)
            skew_xy = minus(after_y(t, 1), before_y(t, 1))
            skew_xz = minus(at(skew_ref, (), 256 * (x + 2) + row), at(skew_ref, (), 256 * x + row))
            skew_yz = minus(after_y(t, 2), before_y(t, 2))
            diag = [at(diag_ref, (k, x), row) for k in range(3)]
            cross = [at(cross_ref, (k, x), row) for k in range(3)]
            prev = at(prev_ref, (), 256 * x + row)
            values = []
            for h in range(2):
                d0, d1, d2 = (d[h] for d in diag)
                c0, c1, c2 = (c[h] for c in cross)
                twice = mid[h] + mid[h]
                second = d0 * (sum_x[h] - twice) + d1 * (sum_y[h] - twice) + d2 * (sum_z[h] - twice)
                mixed = c0 * skew_xy[h] + c1 * skew_xz[h] + c2 * skew_yz[h]
                values.append((twice - prev[h]) + (second + 0.5 * mixed))
            put(out_ref, 256 * x + row, values)
        if step < 2:
            ending += copies([(out_ref.at[part(x)], out_any.at[part(x)])], end_sems.at[pl.ds(x, 1)])
    if step < 2:
        value_ref, even_out, odd_out = outs[:3]
        even = out_ref.at[pl.ds(pl.multiple_of(768 - 768 * odd_brick[0], 256), 256)]
        odd = out_ref.at[pl.ds(pl.multiple_of(768 * odd_brick[0], 256), 256)]
        ending += copies([(even, even_out), (odd, odd_out)], end_sems.at[pl.ds(5, 2)])
        value_ref[...] = gather_row(out_ref, rec_smem, rec_ref[...], rows_ref)
    for copy in ending:
        copy.wait()


def wave(step, odd_brick, rec, cells, field, prev, diag, cross, edge_planes, added=(), record=()):
    whole = (1024, 256)
    out_shape = [HBM(whole, f32), VMEM((1, 128), f32), HBM((256, 256), f32), HBM((256, 256), f32)]
    if step == 0:
        out_shape += [VMEM((8, 128), f32)]
    elif step == 1:
        out_shape += [HBM(whole, f32)]
    else:
        out_shape = [VMEM(whole, f32), VMEM((3, 128), jnp.bfloat16), HBM(whole, f32)]
    coef = VMEM((3, 4, 256, 256), f32)
    edge = VMEM(edge_planes[0].shape, f32)
    listed = SMEM((1, 128), jnp.int32)
    scratch = [VMEM(whole, f32), VMEM(whole, f32), coef, coef, edge, edge, VMEM((1536, 256), f32), VMEM(whole, f32)]
    scratch += [VMEM((128, 256), f32), listed, listed, DMA((4, 8)), DMA((2,)), DMA((2,)), DMA((7,))]
    if step < 2:
        scratch.append(VMEM(whole, f32))
    return call(
        functools.partial(wave_kernel, step),
        tuple(out_shape),
        (16 << 20, 10 << 20),
        scalars=[odd_brick],
        arrays=[rec, *added, *record],
        far=[*cells, field, prev, diag, cross],
        free=edge_planes,
        scratch=scratch,
        room=16,
    )


def add_at(cell_smem, cell_vec, value, target_ref, rows_ref):
    rows_ref[...] = jnp.where(lanes_of(cell_vec[...]), sheet_of(value, 256), 0.0)
    for j in range(128):
        row = cell_smem[0, j] >> 8
        target_ref[pl.ds(row, 1), :] = target_ref[pl.ds(row, 1), :] + rows_ref[j : j + 1, :]


def last_kernel(cell_smem, cell_vec, parts_ref, field_ref, out_any, rows_ref, sem):
    sums = [parts_ref[8 * k : 8 * k + 8, :] for k in range(4)]
    for k in range(4, 32):
        sums[k % 4] = sums[k % 4] + parts_ref[8 * k : 8 * k + 8, :]
    value = jnp.sum((sums[0] + sums[1]) + (sums[2] + sums[3]), axis=0, keepdims=True)
    add_at(cell_smem, cell_vec, value, field_ref, rows_ref)
    copy = pltpu.make_async_copy(field_ref, out_any, sem)
    copy.start()
    copy.wait()


def last_scatter(emit_cell, emit, parts, field):
    return call(
        last_kernel,
        HBM((1024, 256), f32),
        (1 << 20, 2 << 20),
        scalars=[emit_cell],
        arrays=[emit, parts, field],
        scratch=[VMEM((128, 256), f32), DMA],
    )


def spread_kernel(parts_ref, value_ref, out_ref):
    sums = [parts_ref[b] for b in range(4)]
    for b in range(4, 32):
        sums[b % 4] = sums[b % 4] + parts_ref[b]
    total = (sums[0] + sums[1]) + (sums[2] + sums[3])
    for s in range(8):
        out_ref[s, 0:8, :] = total[8:16]
        rows = [value_ref[...], total[s : s + 1], total[16 + s : 17 + s], jnp.zeros((5, 128), f32)]
        out_ref[s, 8:16, :] = jnp.concatenate(rows, axis=0)


def spread(parts, value):
    out = VMEM((8, 16, 128), f32)
    return call(spread_kernel, out, (1 << 15, 1 << 17), arrays=[parts, value])


def exchange(array, axis):
    return lax.all_to_all(array, axis, 0, 0, tiled=True)


def halos(even_plane, odd_plane):
    size = lax.axis_size("brick")
    even = lax.ppermute(even_plane, "brick", [(i, i ^ 1) for i in range(size)])
    odd = lax.ppermute(odd_plane, "brick", [(i, ((i + 1) ^ 1) - 1) for i in range(1, size - 1)])
    return even, odd


def steps(field_prev, field_now, diag, cross, green, delays, past, rec_cell, emit_cell):
    rank = lax.axis_index("shot").reshape(1)
    odd_brick = (lax.axis_index("brick") & 1).reshape(1)
    past = past[:, 0]

    current = field_now.reshape(1024, 256)
    before = field_prev.reshape(1024, 256)
    message, *planes, rec, emit, own, delay, green = first_message(
        rank, odd_brick, delays, rec_cell, emit_cell, past, current, green[0]
    )
    first = exchange(message, "shot")
    even, odd = halos(*planes)
    right = turn(green)
    cells = (rec_cell, emit_cell)
    following, value, *planes, near_cells = wave(0, odd_brick, rec, cells, current, before, diag, cross, (even, odd))
    partial = emission_start(first, delay, right)
    parts = exchange(partial, "brick")
    old = older(first, delay)
    message = spread(parts, value)

    answer = exchange(message, "shot")
    even, odd = halos(*planes)
    partial, mine, near, sample1 = samples_and_emission(1, answer, first, old, delay, own, [], right)
    parts = exchange(partial, "brick")
    added = (emit, mine, near, near_cells)
    earlier = current
    following, value, *planes, current = wave(
        1, odd_brick, rec, cells, following, earlier, diag, cross, (even, odd), added
    )
    message = spread(parts, value)

    answer = exchange(message, "shot")
    even, odd = halos(*planes)
    partial, mine, near, sample2 = samples_and_emission(2, answer, first, old, delay, own, [sample1], right)
    parts = exchange(partial.reshape(256, 1, 128), ("shot", "brick")).reshape(256, 128)
    added = (emit, mine, near, near_cells)
    record = (own, first, sample1, sample2)
    earlier = current
    following, recorded, current = wave(
        2, odd_brick, rec, cells, following, earlier, diag, cross, (even, odd), added, record
    )
    after = last_scatter(emit_cell, emit, parts, following)
    shape = field_now.shape
    return current.reshape(shape), after.reshape(shape), recorded[:, None]


def solution(mesh):
    return jax.shard_map(
        steps,
        mesh=mesh,
        in_specs=(
            P("shot", "brick", None, None),
            P("shot", "brick", None, None),
            P(None, "brick", None, None),
            P(None, "brick", None, None),
            P("shot", None, "brick"),
            P(),
            P(None, "shot", "brick"),
            P("shot", "brick"),
            P("shot", "brick"),
        ),
        out_specs=(
            P("shot", "brick", None, None),
            P("shot", "brick", None, None),
            P(None, "shot", "brick"),
        ),
        check_vma=False,
    )
```

```python
import functools

import jax
import jax.numpy as jnp
from jax import lax
from jax.experimental import pallas as pl
from jax.experimental.pallas import tpu as pltpu
from jax.sharding import PartitionSpec as P


VMEM = pltpu.VMEM
SMEM = pltpu.SMEM
HBM = pltpu.HBM
DMA = pltpu.SemaphoreType.DMA
f32 = jnp.float32


def spec(space):
    return pl.BlockSpec(memory_space=space)


def near(array):
    return pltpu.with_memory_space_constraint(array, pltpu.MemorySpace.VMEM)


def distant(array):
    return pltpu.with_memory_space_constraint(array, pltpu.MemorySpace.HBM)


def call(kernel, out_shape, work, scalars=(), arrays=(), far=(), free=(), scratch=(), aliases=None, room=2):
    flops, moved = work
    return pl.pallas_call(
        kernel,
        out_shape=out_shape,
        in_specs=[spec(SMEM)] * len(scalars) + [spec(VMEM)] * len(arrays) + [spec(HBM)] * len(far) + [spec(pl.ANY)] * len(free),
        out_specs=jax.tree.map(lambda o: spec(HBM if o.memory_space == HBM else VMEM), out_shape),
        scratch_shapes=list(scratch),
        input_output_aliases=aliases or {},
        cost_estimate=pl.CostEstimate(flops=flops, bytes_accessed=moved, transcendentals=0),
        compiler_params=pltpu.CompilerParams(vmem_limit_bytes=room << 20),
    )(*scalars, *[near(a) for a in arrays], *[distant(a) for a in far], *free)


def sheet_of(row, width):
    tall = jnp.transpose(jnp.broadcast_to(row, (128, 128)))
    return jnp.concatenate([tall] * (width // 128), axis=1)


def lanes_of(cells):
    column = sheet_of((cells & 255).astype(f32), 256).astype(jnp.int32)
    return lax.broadcasted_iota(jnp.int32, (128, 256), 1) == column


def gather_row(field_ref, cell_smem, cell_vec, rows_ref):
    for j in range(128):
        row = cell_smem[0, j] >> 8
        rows_ref[j : j + 1, :] = field_ref[pl.ds(row, 1), :]
    picked = jnp.where(lanes_of(cell_vec), rows_ref[...], 0.0)
    return jnp.sum(jnp.transpose(picked[:, :128] + picked[:, 128:]), axis=0, keepdims=True)


def copies(pairs, sems):
    started = [pltpu.make_async_copy(a, b, sems.at[k]) for k, (a, b) in enumerate(pairs)]
    for copy in started:
        copy.start()
    return started


def first_kernel(
    rank,
    odd_brick,
    field_any,
    past_any,
    rec_any,
    emit_any,
    delays_any,
    green_any,
    out_ref,
    even_ref,
    odd_ref,
    rec_ref,
    emit_ref,
    own_ref,
    delay_ref,
    green_ref,
    field_ref,
    rows_ref,
    past_ref,
    cell_smem,
    delays,
    sems,
):
    pairs = [(rec_any, cell_smem), (delays_any, delays), (field_any, field_ref), (past_any, past_ref)]
    started = copies(pairs + [(rec_any, rec_ref), (emit_any, emit_ref), (green_any, green_ref)], sems)
    own = lax.broadcasted_iota(jnp.int32, (8, 128), 0) == rank[0]
    own_ref[...] = jnp.where(own, 1.0, 0.0)
    for copy in started[:-1]:
        copy.wait()
    delay_ref[...] = jnp.full((8, 128), delays[rank[0]], jnp.int32)
    sample = gather_row(field_ref, cell_smem, rec_ref[...], rows_ref)
    rows = [past_ref[...].astype(f32), sample.astype(jnp.bfloat16).astype(f32)]
    rows += [rec_ref[...].astype(f32), emit_ref[...].astype(f32), jnp.zeros((5, 128), f32)]
    message = jnp.concatenate(rows, axis=0)
    for s in range(8):
        out_ref[s] = message
    edges(odd_brick, field_ref, even_ref, odd_ref)
    cells = jnp.broadcast_to(emit_ref[...].astype(f32), (8, 128))
    for ref in (even_ref, odd_ref):
        ref[256:264, 0:128] = cells
        ref[256:264, 128:256] = cells
    started[-1].wait()


def edges(odd_brick, field_ref, even_ref, odd_ref):
    even_ref[0:256, :] = field_ref[pl.ds(pl.multiple_of(768 - 768 * odd_brick[0], 256), 256), :]
    odd_ref[0:256, :] = field_ref[pl.ds(pl.multiple_of(768 * odd_brick[0], 256), 256), :]


def first_message(rank, odd_brick, delays, rec_cell, emit_cell, past, field, green):
    plane = VMEM((264, 256), f32)
    row = VMEM((1, 128), jnp.int32)
    return call(
        first_kernel,
        (
            VMEM((8, 16, 128), f32),
            plane,
            plane,
            row,
            row,
            VMEM((8, 128), f32),
            VMEM((8, 128), jnp.int32),
            VMEM((4096, 128), jnp.bfloat16),
        ),
        (1 << 20, 1 << 19),
        scalars=[rank, odd_brick],
        far=[field, past, rec_cell, emit_cell, delays, green],
        scratch=[
            VMEM((1024, 256), f32),
            VMEM((128, 256), f32),
            VMEM((8, 128), jnp.bfloat16),
            SMEM((1, 128), jnp.int32),
            SMEM((8,), jnp.int32),
            DMA((7,)),
        ],
        room=3,
    )


def turn_kernel(green_ref, right_ref):
    for b in range(32):
        at = slice(b * 128, (b + 1) * 128)
        right_ref[:, at] = jnp.transpose(green_ref[at, :])


def turn(green):
    return call(turn_kernel, VMEM((128, 4096), jnp.bfloat16), (1 << 20, 1 << 20), arrays=[green])


def older_kernel(first_ref, delay_ref, old_ref):
    for moment in (1, 2):
        old_ref[moment - 1] = old_samples(first_ref, 8 + moment - delay_ref[...])


def older(first, delay):
    out = VMEM((2, 8, 128), f32)
    return call(older_kernel, out, (1 << 20, 1 << 18), arrays=[first, delay])


def matches(first_ref):
    blocks = []
    for s in range(8):
        rec = first_ref[s, 9:10, :]
        emit = first_ref[s, 10:11, :]
        same = sheet_of(emit, 128) == jnp.broadcast_to(rec, (128, 128))
        blocks.append(jnp.where(same, 1.0, 0.0).astype(jnp.bfloat16))
    return jnp.concatenate(blocks, axis=0)


def multiply(chosen, right_ref, out_ref):
    product = jnp.dot(chosen.astype(jnp.bfloat16), right_ref[...], preferred_element_type=f32)
    if out_ref.shape[0] == 256:
        for b in range(32):
            out_ref[pl.ds(b, 8, stride=32), :] = product[:, b * 128 : (b + 1) * 128]
        return
    for b in range(32):
        block = product[:, b * 128 : (b + 1) * 128]
        out_ref[b, 8:16, :] = block
        if b < 31:
            out_ref[b + 1, 0:8, :] = block
        if b > 0:
            out_ref[b - 1, 16:24, :] = block
    out_ref[0, 0:8, :] = jnp.zeros((8, 128), f32)
    out_ref[31, 16:24, :] = jnp.zeros((8, 128), f32)


def old_samples(first_ref, where):
    chosen = jnp.zeros((8, 128), f32)
    for k in range(9):
        series = jnp.concatenate([first_ref[s, k : k + 1, :] for s in range(8)], axis=0)
        chosen = jnp.where(where == k, series, chosen)
    return chosen


def start_kernel(first_ref, delay_ref, right_ref, out_ref):
    multiply(old_samples(first_ref, 8 - delay_ref[...]), right_ref, out_ref)


def emission_start(first, delay, right):
    out = VMEM((32, 24, 128), f32)
    return call(start_kernel, out, (8 << 20, 1 << 20), arrays=[first, delay, right])


def samples_kernel(moment, message_ref, first_ref, old_ref, delay_ref, own_ref, *refs):
    *newer_refs, right_ref, out_ref, mine_ref, near_ref, sample_ref = refs
    total = message_ref[0, 0:8, :]
    for lag in range(1, 8):
        total = total + message_ref[lag, 0:8, :]
    near = message_ref[0, 8:16, :]
    for lag in range(1, 8):
        near = near + message_ref[lag, 8:16, :]
    near_ref[...] = near
    values = jnp.concatenate([message_ref[s, 8:9, :] for s in range(8)], axis=0)
    wide = jnp.concatenate([total] * 8, axis=1)
    block = lax.broadcasted_iota(jnp.int32, (8, 1024), 1) >> 7
    wide = jnp.where(block == lax.broadcasted_iota(jnp.int32, (8, 1024), 0), wide, 0.0)
    high = wide.astype(jnp.bfloat16)
    rest = wide - high.astype(f32)
    middle = rest.astype(jnp.bfloat16)
    low = (rest - middle.astype(f32)).astype(jnp.bfloat16)
    parts = jnp.concatenate([high, middle, low], axis=0)
    added = jnp.dot(parts, matches(first_ref), preferred_element_type=f32)
    values = values + ((added[16:24] + added[8:16]) + added[0:8])
    sample = values.astype(jnp.bfloat16).astype(f32)
    delay = delay_ref[...]
    chosen = old_ref[moment - 1]
    for k, newer_ref in enumerate(newer_refs):
        chosen = jnp.where(delay == moment - 1 - k, newer_ref[...], chosen)
    chosen = jnp.where(delay == 0, sample, chosen)
    multiply(chosen, right_ref, out_ref)
    sample_ref[...] = sample
    mine_ref[...] = jnp.sum(jnp.where(own_ref[...] > 0.5, total, 0.0), axis=0, keepdims=True)


def samples_and_emission(moment, message, first, old, delay, own, newer, right):
    return call(
        functools.partial(samples_kernel, moment),
        (VMEM((32, 24, 128) if moment == 1 else (256, 128), f32), VMEM((1, 128), f32), VMEM((8, 128), f32), VMEM((8, 128), f32)),
        (8 << 20, 1 << 20),
        arrays=[message, first, old, delay, own, *newer, right],
    )


def spots(values, cells, plane):
    cells = cells.astype(jnp.int32)
    values = jnp.where((cells >> 16) == plane, values, 0.0)
    column = sheet_of(((cells >> 8) & 255).astype(f32), 256).astype(jnp.int32)
    rows = jnp.where(lax.broadcasted_iota(jnp.int32, (128, 256), 1) == column, 1.0, 0.0).astype(jnp.bfloat16)
    rest = jnp.where(lanes_of(cells), sheet_of(values, 256), 0.0)
    terms = []
    for _ in range(3):
        term = rest.astype(jnp.bfloat16)
        rest = rest - term.astype(f32)
        terms.append(lax.dot_general(rows, term, (((0,), (0,)), ((), ())), preferred_element_type=f32))
    return (terms[2] + terms[1]) + terms[0]


def base(x):
    return 8 + 264 * (x + 1)


def wave_kernel(step, odd_brick, rec_ref, *refs):
    refs = list(refs)

    def take(count):
        taken = refs[:count]
        del refs[:count]
        return taken

    emit_ref, mine_ref, near_ref, near_cells_ref = take(4) if step else [None] * 4
    own_ref, start_ref, *sample_refs = take(4) if step == 2 else [None] * 4
    rec_any, emit_any, field_any, prev_any, diag_any, cross_any, even_any, odd_any = take(8)
    out_any, *outs = take(5 if step < 2 else 3)
    left_ref, right_ref, prev_ref, diag_ref, cross_ref, left_skew, right_skew, left_sum, right_sum = take(9)
    rows_ref, cells_ref, rec_smem, emit_smem, sems, edge_sems, cell_sems, end_sems = take(8)
    (out_ref,) = take(1) if step < 2 else [out_any]
    order = (1, 2, 0, 3)
    fields, skews, sums = (left_ref, right_ref), (left_skew, right_skew), (left_sum, right_sum)

    def part(x):
        return pl.ds(256 * x, 256)

    def lanes(h):
        return pl.ds(128 * h, 128)

    def plane(h, x):
        return fields[h].at[pl.ds(base(x), 256)]

    listed = copies([(rec_any, rec_smem), (emit_any, emit_smem)], cell_sems)
    begun = {}
    for x in (0, 1, 2, 3):
        begun[x] = copies([(field_any.at[part(x), lanes(h)], plane(h, x)) for h in (0, 1)], sems.at[x, pl.ds(7, 2)])
    started = {}
    for x in order:
        pairs = [(diag_any.at[k, x], diag_ref.at[k, x]) for k in range(3)]
        pairs += [(cross_any.at[k, x], cross_ref.at[k, x]) for k in range(3)]
        started[x] = copies([(prev_any.at[part(x)], prev_ref.at[part(x)])] + pairs, sems.at[x])

    def bring(low, high):
        pairs = [(low.at[pl.ds(0, 256), lanes(h)], plane(h, -1)) for h in (0, 1)]
        pairs += [(high.at[pl.ds(0, 256), lanes(h)], plane(h, 4)) for h in (0, 1)]
        if step == 0:
            pairs += [(low.at[pl.ds(256, 8), lanes(0)], cells_ref.at[pl.ds(0, 8)])]
            pairs += [(high.at[pl.ds(256, 8), lanes(0)], cells_ref.at[pl.ds(8, 8)])]
        return [pltpu.make_async_copy(a, b, edge_sems.at[k]) for k, (a, b) in enumerate(pairs)]

    @pl.when(odd_brick[0] == 0)
    def _():
        for copy in bring(odd_any, even_any):
            copy.start()

    @pl.when(odd_brick[0] == 1)
    def _():
        for copy in bring(even_any, odd_any):
            copy.start()

    for ref in fields + skews:
        for x in range(-2, 5):
            ref[base(x) + 256 : base(x) + 264, :] = jnp.zeros((8, 128), f32)
    ending = []
    for copy in listed:
        copy.wait()
    if step:
        for x in (0, 1, 2, 3):
            for copy in begun.pop(x):
                copy.wait()
        rows_ref[...] = jnp.where(lanes_of(emit_ref[...]), sheet_of(mine_ref[...], 256), 0.0)
        for j in range(128):
            cell = emit_smem[0, j]
            row = (cell >> 8) + 8 * (cell >> 16) + base(0)
            for h in (0, 1):
                spot = (pl.ds(row, 1), slice(None))
                fields[h][spot] = fields[h][spot] + rows_ref[j : j + 1, 128 * h : 128 * h + 128]
        pairs = [(plane(h, x), outs[-1].at[part(x), lanes(h)]) for x in (0, 1, 2, 3) for h in (0, 1)]
        ending += copies(pairs, end_sems.at[pl.ds(6, 8)])
    if step == 2:
        own = own_ref[...] > 0.5
        start = jnp.concatenate([start_ref[s, 8:9, :] for s in range(8)], axis=0)
        series = [start] + [s[...] for s in sample_refs]
        series = [jnp.sum(jnp.where(own, s, 0.0), axis=0, keepdims=True) for s in series]
        outs[0][...] = jnp.concatenate(series, axis=0).astype(jnp.bfloat16)

    lane = lax.broadcasted_iota(jnp.int32, (8, 128), 1)
    first_lane, last_lane = lane == 0, lane == 127

    def along_z(x):
        for t in range(32):
            rows = slice(base(x) + 8 * t, base(x) + 8 * t + 8)
            a, b = left_ref[rows, :], right_ref[rows, :]
            up_a, up_b = pltpu.roll(a, 127, 1), pltpu.roll(b, 127, 1)
            down_a, down_b = pltpu.roll(a, 1, 1), pltpu.roll(b, 1, 1)
            ahead = (jnp.where(last_lane, up_b, up_a), jnp.where(last_lane, 0.0, up_b))
            behind = (jnp.where(first_lane, 0.0, down_a), jnp.where(first_lane, down_a, down_b))
            for h in (0, 1):
                skews[h][rows, :] = ahead[h] - behind[h]
                if 0 <= x < 4:
                    sums[h][256 * x + 8 * t : 256 * x + 8 * t + 8, :] = ahead[h] + behind[h]

    ready = {1: (0, 1, 2), 2: (3,), 0: (-1,), 3: (4,)}
    for x in order:
        if x == 0:
            for copy in bring(odd_any, even_any):
                copy.wait()
            if step:
                for side, plane_of, row in ((-1, 3, 0), (4, 0, 1)):
                    extra = spots(near_ref[1 + row : 2 + row, :], near_cells_ref[row : row + 1, :], plane_of)
                    rows = slice(base(side), base(side) + 256)
                    for h in (0, 1):
                        fields[h][rows, :] = fields[h][rows, :] + extra[:, 128 * h : 128 * h + 128]
            else:
                outs[3][0:1, :] = cells_ref[0:1, :]
                outs[3][1:2, :] = cells_ref[8:9, :]
        for k in ready[x]:
            for copy in begun.get(k, ()):
                copy.wait()
            along_z(k)
        for copy in started[x]:
            copy.wait()
        for t in range(32):
            near, up, down = (base(k) + 8 * t for k in (x, x + 1, x - 1))
            row = 256 * x + 8 * t
            rows = slice(row, row + 8)
            for h in (0, 1):
                field, skew = fields[h], skews[h]

                def at(ref, first):
                    return ref[first : first + 8, :]

                def across(ref, first):
                    return at(ref, first + 1) - at(ref, first - 1)

                columns = slice(128 * h, 128 * h + 128)
                d0, d1, d2 = (diag_ref[k, x, 8 * t : 8 * t + 8, columns] for k in range(3))
                c0, c1, c2 = (cross_ref[k, x, 8 * t : 8 * t + 8, columns] for k in range(3))
                mid = at(field, near)
                twice = mid + mid
                second = d0 * ((at(field, up) + at(field, down)) - twice)
                second = second + d1 * ((at(field, near + 1) + at(field, near - 1)) - twice)
                second = second + d2 * (sums[h][rows, :] - twice)
                mixed = c0 * (across(field, up) - across(field, down))
                mixed = mixed + c1 * (at(skew, up) - at(skew, down)) + c2 * across(skew, near)
                out_ref[rows, columns] = (twice - prev_ref[rows, columns]) + (second + 0.5 * mixed)
        if step < 2:
            ending += copies([(out_ref.at[part(x)], out_any.at[part(x)])], end_sems.at[pl.ds(x, 1)])
    if step < 2:
        value_ref, even_out, odd_out = outs[:3]
        even = out_ref.at[pl.ds(pl.multiple_of(768 - 768 * odd_brick[0], 256), 256)]
        odd = out_ref.at[pl.ds(pl.multiple_of(768 * odd_brick[0], 256), 256)]
        ending += copies([(even, even_out), (odd, odd_out)], end_sems.at[pl.ds(4, 2)])
        value_ref[...] = gather_row(out_ref, rec_smem, rec_ref[...], rows_ref)
    for copy in ending:
        copy.wait()


def wave(step, odd_brick, rec, cells, field, prev, diag, cross, edge_planes, added=(), record=()):
    whole = (1024, 256)
    out_shape = [HBM(whole, f32), VMEM((1, 128), f32), HBM((256, 256), f32), HBM((256, 256), f32)]
    if step == 0:
        out_shape += [VMEM((8, 128), f32)]
    elif step == 1:
        out_shape += [HBM(whole, f32)]
    else:
        out_shape = [VMEM(whole, f32), VMEM((3, 128), jnp.bfloat16), HBM(whole, f32)]
    coef = VMEM((3, 4, 256, 256), f32)
    half = VMEM((1592, 128), f32)
    inner = VMEM((1024, 128), f32)
    listed = SMEM((1, 128), jnp.int32)
    scratch = [half, half, VMEM(whole, f32), coef, coef, half, half, inner, inner]
    scratch += [VMEM((128, 256), f32), VMEM((16, 128), f32), listed, listed]
    scratch += [DMA((4, 9)), DMA((6,)), DMA((2,)), DMA((14,))]
    if step < 2:
        scratch.append(VMEM(whole, f32))
    return call(
        functools.partial(wave_kernel, step),
        tuple(out_shape),
        (16 << 20, 10 << 20),
        scalars=[odd_brick],
        arrays=[rec, *added, *record],
        far=[*cells, field, prev, diag, cross],
        free=edge_planes,
        scratch=scratch,
        room=16,
    )


def add_at(cell_smem, cell_vec, value, target_ref, rows_ref):
    rows_ref[...] = jnp.where(lanes_of(cell_vec[...]), sheet_of(value, 256), 0.0)
    for j in range(128):
        row = cell_smem[0, j] >> 8
        target_ref[pl.ds(row, 1), :] = target_ref[pl.ds(row, 1), :] + rows_ref[j : j + 1, :]


def last_kernel(cell_smem, cell_vec, parts_ref, field_ref, out_any, rows_ref, sem):
    sums = [parts_ref[8 * k : 8 * k + 8, :] for k in range(4)]
    for k in range(4, 32):
        sums[k % 4] = sums[k % 4] + parts_ref[8 * k : 8 * k + 8, :]
    value = jnp.sum((sums[0] + sums[1]) + (sums[2] + sums[3]), axis=0, keepdims=True)
    add_at(cell_smem, cell_vec, value, field_ref, rows_ref)
    copy = pltpu.make_async_copy(field_ref, out_any, sem)
    copy.start()
    copy.wait()


def last_scatter(emit_cell, emit, parts, field):
    return call(
        last_kernel,
        HBM((1024, 256), f32),
        (1 << 20, 2 << 20),
        scalars=[emit_cell],
        arrays=[emit, parts, field],
        scratch=[VMEM((128, 256), f32), DMA],
    )


def spread_kernel(parts_ref, value_ref, out_ref):
    sums = [parts_ref[b] for b in range(4)]
    for b in range(4, 32):
        sums[b % 4] = sums[b % 4] + parts_ref[b]
    total = (sums[0] + sums[1]) + (sums[2] + sums[3])
    for s in range(8):
        out_ref[s, 0:8, :] = total[8:16]
        rows = [value_ref[...], total[s : s + 1], total[16 + s : 17 + s], jnp.zeros((5, 128), f32)]
        out_ref[s, 8:16, :] = jnp.concatenate(rows, axis=0)


def spread(parts, value):
    out = VMEM((8, 16, 128), f32)
    return call(spread_kernel, out, (1 << 15, 1 << 17), arrays=[parts, value])


def exchange(array, axis):
    return lax.all_to_all(array, axis, 0, 0, tiled=True)


def halos(even_plane, odd_plane):
    size = lax.axis_size("brick")
    even = lax.ppermute(even_plane, "brick", [(i, i ^ 1) for i in range(size)])
    odd = lax.ppermute(odd_plane, "brick", [(i, ((i + 1) ^ 1) - 1) for i in range(1, size - 1)])
    return even, odd


def steps(field_prev, field_now, diag, cross, green, delays, past, rec_cell, emit_cell):
    rank = lax.axis_index("shot").reshape(1)
    odd_brick = (lax.axis_index("brick") & 1).reshape(1)
    past = past[:, 0]

    current = field_now.reshape(1024, 256)
    before = field_prev.reshape(1024, 256)
    message, *planes, rec, emit, own, delay, green = first_message(
        rank, odd_brick, delays, rec_cell, emit_cell, past, current, green[0]
    )
    first = exchange(message, "shot")
    even, odd = halos(*planes)
    right = turn(green)
    cells = (rec_cell, emit_cell)
    following, value, *planes, near_cells = wave(0, odd_brick, rec, cells, current, before, diag, cross, (even, odd))
    partial = emission_start(first, delay, right)
    parts = exchange(partial, "brick")
    old = older(first, delay)
    message = spread(parts, value)

    answer = exchange(message, "shot")
    even, odd = halos(*planes)
    partial, mine, near, sample1 = samples_and_emission(1, answer, first, old, delay, own, [], right)
    parts = exchange(partial, "brick")
    added = (emit, mine, near, near_cells)
    earlier = current
    following, value, *planes, current = wave(
        1, odd_brick, rec, cells, following, earlier, diag, cross, (even, odd), added
    )
    message = spread(parts, value)

    answer = exchange(message, "shot")
    even, odd = halos(*planes)
    partial, mine, near, sample2 = samples_and_emission(2, answer, first, old, delay, own, [sample1], right)
    parts = exchange(partial.reshape(256, 1, 128), ("shot", "brick")).reshape(256, 128)
    added = (emit, mine, near, near_cells)
    record = (own, first, sample1, sample2)
    earlier = current
    following, recorded, current = wave(
        2, odd_brick, rec, cells, following, earlier, diag, cross, (even, odd), added, record
    )
    after = last_scatter(emit_cell, emit, parts, following)
    shape = field_now.shape
    return current.reshape(shape), after.reshape(shape), recorded[:, None]


def solution(mesh):
    return jax.shard_map(
        steps,
        mesh=mesh,
        in_specs=(
            P("shot", "brick", None, None),
            P("shot", "brick", None, None),
            P(None, "brick", None, None),
            P(None, "brick", None, None),
            P("shot", None, "brick"),
            P(),
            P(None, "shot", "brick"),
            P("shot", "brick"),
            P("shot", "brick"),
        ),
        out_specs=(
            P("shot", "brick", None, None),
            P("shot", "brick", None, None),
            P(None, "shot", "brick"),
        ),
        check_vma=False,
    )
```

```python
import functools

import jax
import jax.numpy as jnp
from jax import lax
from jax.experimental import pallas as pl
from jax.experimental.pallas import tpu as pltpu
from jax.sharding import PartitionSpec as P


VMEM = pltpu.VMEM
SMEM = pltpu.SMEM
HBM = pltpu.HBM
DMA = pltpu.SemaphoreType.DMA
f32 = jnp.float32


def spec(space):
    return pl.BlockSpec(memory_space=space)


def near(array):
    return pltpu.with_memory_space_constraint(array, pltpu.MemorySpace.VMEM)


def distant(array):
    return pltpu.with_memory_space_constraint(array, pltpu.MemorySpace.HBM)


def call(kernel, out_shape, work, scalars=(), arrays=(), far=(), free=(), scratch=(), aliases=None, room=2):
    flops, moved = work
    return pl.pallas_call(
        kernel,
        out_shape=out_shape,
        in_specs=[spec(SMEM)] * len(scalars) + [spec(VMEM)] * len(arrays) + [spec(HBM)] * len(far) + [spec(pl.ANY)] * len(free),
        out_specs=jax.tree.map(lambda o: spec(HBM if o.memory_space == HBM else VMEM), out_shape),
        scratch_shapes=list(scratch),
        input_output_aliases=aliases or {},
        cost_estimate=pl.CostEstimate(flops=flops, bytes_accessed=moved, transcendentals=0),
        compiler_params=pltpu.CompilerParams(vmem_limit_bytes=room << 20),
    )(*scalars, *[near(a) for a in arrays], *[distant(a) for a in far], *free)


def sheet_of(row, width):
    tall = jnp.transpose(jnp.broadcast_to(row, (128, 128)))
    return jnp.concatenate([tall] * (width // 128), axis=1)


def lanes_of(cells):
    column = sheet_of((cells & 255).astype(f32), 256).astype(jnp.int32)
    return lax.broadcasted_iota(jnp.int32, (128, 256), 1) == column


def gather_row(field_ref, cell_smem, cell_vec, rows_ref):
    for j in range(128):
        row = cell_smem[0, j] >> 8
        rows_ref[j : j + 1, :] = field_ref[pl.ds(row, 1), :]
    picked = jnp.where(lanes_of(cell_vec), rows_ref[...], 0.0)
    return jnp.sum(jnp.transpose(picked[:, :128] + picked[:, 128:]), axis=0, keepdims=True)


def copies(pairs, sems):
    started = [pltpu.make_async_copy(a, b, sems.at[k]) for k, (a, b) in enumerate(pairs)]
    for copy in started:
        copy.start()
    return started


def first_kernel(
    rank,
    odd_brick,
    field_any,
    past_any,
    rec_any,
    emit_any,
    delays_any,
    green_any,
    out_ref,
    even_ref,
    odd_ref,
    rec_ref,
    emit_ref,
    own_ref,
    delay_ref,
    green_ref,
    field_ref,
    rows_ref,
    past_ref,
    cell_smem,
    delays,
    sems,
):
    pairs = [(rec_any, cell_smem), (delays_any, delays), (field_any, field_ref), (past_any, past_ref)]
    started = copies(pairs + [(rec_any, rec_ref), (emit_any, emit_ref), (green_any, green_ref)], sems)
    own = lax.broadcasted_iota(jnp.int32, (8, 128), 0) == rank[0]
    own_ref[...] = jnp.where(own, 1.0, 0.0)
    for copy in started[:-1]:
        copy.wait()
    delay_ref[...] = jnp.full((8, 128), delays[rank[0]], jnp.int32)
    sample = gather_row(field_ref, cell_smem, rec_ref[...], rows_ref)
    rows = [past_ref[...].astype(f32), sample.astype(jnp.bfloat16).astype(f32)]
    rows += [rec_ref[...].astype(f32), emit_ref[...].astype(f32), jnp.zeros((5, 128), f32)]
    message = jnp.concatenate(rows, axis=0)
    for s in range(8):
        out_ref[s] = message
    edges(odd_brick, field_ref, even_ref, odd_ref)
    cells = jnp.broadcast_to(emit_ref[...].astype(f32), (8, 128))
    for ref in (even_ref, odd_ref):
        ref[256:264, 0:128] = cells
        ref[256:264, 128:256] = cells
    started[-1].wait()


def edges(odd_brick, field_ref, even_ref, odd_ref):
    even_ref[0:256, :] = field_ref[pl.ds(pl.multiple_of(768 - 768 * odd_brick[0], 256), 256), :]
    odd_ref[0:256, :] = field_ref[pl.ds(pl.multiple_of(768 * odd_brick[0], 256), 256), :]


def first_message(rank, odd_brick, delays, rec_cell, emit_cell, past, field, green):
    plane = VMEM((264, 256), f32)
    row = VMEM((1, 128), jnp.int32)
    return call(
        first_kernel,
        (
            VMEM((8, 16, 128), f32),
            plane,
            plane,
            row,
            row,
            VMEM((8, 128), f32),
            VMEM((8, 128), jnp.int32),
            VMEM((4096, 128), jnp.bfloat16),
        ),
        (1 << 20, 1 << 19),
        scalars=[rank, odd_brick],
        far=[field, past, rec_cell, emit_cell, delays, green],
        scratch=[
            VMEM((1024, 256), f32),
            VMEM((128, 256), f32),
            VMEM((8, 128), jnp.bfloat16),
            SMEM((1, 128), jnp.int32),
            SMEM((8,), jnp.int32),
            DMA((7,)),
        ],
        room=3,
    )


def turn_kernel(green_ref, right_ref):
    for b in range(32):
        at = slice(b * 128, (b + 1) * 128)
        right_ref[:, at] = jnp.transpose(green_ref[at, :])


def turn(green):
    return call(turn_kernel, VMEM((128, 4096), jnp.bfloat16), (1 << 20, 1 << 20), arrays=[green])


def older_kernel(first_ref, delay_ref, old_ref):
    for moment in (1, 2):
        old_ref[moment - 1] = old_samples(first_ref, 8 + moment - delay_ref[...])


def older(first, delay):
    out = VMEM((2, 8, 128), f32)
    return call(older_kernel, out, (1 << 20, 1 << 18), arrays=[first, delay])


def matches(first_ref):
    blocks = []
    for s in range(8):
        rec = first_ref[s, 9:10, :]
        emit = first_ref[s, 10:11, :]
        same = sheet_of(emit, 128) == jnp.broadcast_to(rec, (128, 128))
        blocks.append(jnp.where(same, 1.0, 0.0).astype(jnp.bfloat16))
    return jnp.concatenate(blocks, axis=0)


def multiply(chosen, right_ref, out_ref):
    product = jnp.dot(chosen.astype(jnp.bfloat16), right_ref[...], preferred_element_type=f32)
    if out_ref.shape[0] == 256:
        for b in range(32):
            out_ref[pl.ds(b, 8, stride=32), :] = product[:, b * 128 : (b + 1) * 128]
        return
    for b in range(32):
        block = product[:, b * 128 : (b + 1) * 128]
        out_ref[b, 8:16, :] = block
        if b < 31:
            out_ref[b + 1, 0:8, :] = block
        if b > 0:
            out_ref[b - 1, 16:24, :] = block
    out_ref[0, 0:8, :] = jnp.zeros((8, 128), f32)
    out_ref[31, 16:24, :] = jnp.zeros((8, 128), f32)


def old_samples(first_ref, where):
    chosen = jnp.zeros((8, 128), f32)
    for k in range(9):
        series = jnp.concatenate([first_ref[s, k : k + 1, :] for s in range(8)], axis=0)
        chosen = jnp.where(where == k, series, chosen)
    return chosen


def start_kernel(first_ref, delay_ref, right_ref, out_ref):
    multiply(old_samples(first_ref, 8 - delay_ref[...]), right_ref, out_ref)


def emission_start(first, delay, right):
    out = VMEM((32, 24, 128), f32)
    return call(start_kernel, out, (8 << 20, 1 << 20), arrays=[first, delay, right])


def samples_kernel(moment, message_ref, first_ref, old_ref, delay_ref, own_ref, *refs):
    *newer_refs, right_ref, out_ref, mine_ref, near_ref, sample_ref = refs
    total = message_ref[0, 0:8, :]
    for lag in range(1, 8):
        total = total + message_ref[lag, 0:8, :]
    near = message_ref[0, 8:16, :]
    for lag in range(1, 8):
        near = near + message_ref[lag, 8:16, :]
    near_ref[...] = near
    values = jnp.concatenate([message_ref[s, 8:9, :] for s in range(8)], axis=0)
    wide = jnp.concatenate([total] * 8, axis=1)
    block = lax.broadcasted_iota(jnp.int32, (8, 1024), 1) >> 7
    wide = jnp.where(block == lax.broadcasted_iota(jnp.int32, (8, 1024), 0), wide, 0.0)
    high = wide.astype(jnp.bfloat16)
    rest = wide - high.astype(f32)
    middle = rest.astype(jnp.bfloat16)
    low = (rest - middle.astype(f32)).astype(jnp.bfloat16)
    parts = jnp.concatenate([high, middle, low], axis=0)
    added = jnp.dot(parts, matches(first_ref), preferred_element_type=f32)
    values = values + ((added[16:24] + added[8:16]) + added[0:8])
    sample = values.astype(jnp.bfloat16).astype(f32)
    delay = delay_ref[...]
    chosen = old_ref[moment - 1]
    for k, newer_ref in enumerate(newer_refs):
        chosen = jnp.where(delay == moment - 1 - k, newer_ref[...], chosen)
    chosen = jnp.where(delay == 0, sample, chosen)
    multiply(chosen, right_ref, out_ref)
    sample_ref[...] = sample
    mine_ref[...] = jnp.sum(jnp.where(own_ref[...] > 0.5, total, 0.0), axis=0, keepdims=True)


def samples_and_emission(moment, message, first, old, delay, own, newer, right):
    return call(
        functools.partial(samples_kernel, moment),
        (VMEM((32, 24, 128) if moment == 1 else (256, 128), f32), VMEM((1, 128), f32), VMEM((8, 128), f32), VMEM((8, 128), f32)),
        (8 << 20, 1 << 20),
        arrays=[message, first, old, delay, own, *newer, right],
    )


def spots(values, cells, plane):
    cells = cells.astype(jnp.int32)
    values = jnp.where((cells >> 16) == plane, values, 0.0)
    column = sheet_of(((cells >> 8) & 255).astype(f32), 256).astype(jnp.int32)
    rows = jnp.where(lax.broadcasted_iota(jnp.int32, (128, 256), 1) == column, 1.0, 0.0).astype(jnp.bfloat16)
    rest = jnp.where(lanes_of(cells), sheet_of(values, 256), 0.0)
    terms = []
    for _ in range(3):
        term = rest.astype(jnp.bfloat16)
        rest = rest - term.astype(f32)
        terms.append(lax.dot_general(rows, term, (((0,), (0,)), ((), ())), preferred_element_type=f32))
    return (terms[2] + terms[1]) + terms[0]


def base(x):
    return 8 + 264 * (x + 1)


def wave_kernel(step, planes, odd_brick, rec_ref, *refs):
    refs = list(refs)

    def take(count):
        taken = refs[:count]
        del refs[:count]
        return taken

    emit_ref, mine_ref, near_ref, near_cells_ref = take(4) if step else [None] * 4
    own_ref, start_ref, *sample_refs = take(4) if step == 2 else [None] * 4
    inner, outer = planes == (1, 2), planes == (0, 3)
    rec_any, emit_any, field_any, prev_any, diag_any, cross_any = take(6)
    (done_any,) = take(1) if outer else [None]
    even_any, odd_any = take(2) if not inner else [None] * 2
    out_any, *outs = take(1 if inner else 5 if step < 2 else 3)
    left_ref, right_ref, prev_ref, diag_ref, cross_ref, left_skew, right_skew, left_sum, right_sum = take(9)
    rows_ref, cells_ref, rec_smem, emit_smem, sems, edge_sems, cell_sems, end_sems = take(8)
    (out_ref,) = take(1) if step < 2 else [out_any]
    order = planes
    fields, skews, sums = (left_ref, right_ref), (left_skew, right_skew), (left_sum, right_sum)

    def part(x):
        return pl.ds(256 * x, 256)

    def lanes(h):
        return pl.ds(128 * h, 128)

    def plane(h, x):
        return fields[h].at[pl.ds(base(x), 256)]

    listed = copies([(rec_any, rec_smem), (emit_any, emit_smem)], cell_sems)
    begun = {}
    for x in (0, 1, 2, 3):
        begun[x] = copies([(field_any.at[part(x), lanes(h)], plane(h, x)) for h in (0, 1)], sems.at[x, pl.ds(7, 2)])
    started = {}
    for x in order:
        pairs = [(diag_any.at[k, x], diag_ref.at[k, x]) for k in range(3)]
        pairs += [(cross_any.at[k, x], cross_ref.at[k, x]) for k in range(3)]
        started[x] = copies([(prev_any.at[part(x)], prev_ref.at[part(x)])] + pairs, sems.at[x])

    def bring(low, high):
        pairs = [(low.at[pl.ds(0, 256), lanes(h)], plane(h, -1)) for h in (0, 1)]
        pairs += [(high.at[pl.ds(0, 256), lanes(h)], plane(h, 4)) for h in (0, 1)]
        if step == 0:
            pairs += [(low.at[pl.ds(256, 8), lanes(0)], cells_ref.at[pl.ds(0, 8)])]
            pairs += [(high.at[pl.ds(256, 8), lanes(0)], cells_ref.at[pl.ds(8, 8)])]
        return [pltpu.make_async_copy(a, b, edge_sems.at[k]) for k, (a, b) in enumerate(pairs)]

    if not inner:

        @pl.when(odd_brick[0] == 0)
        def _():
            for copy in bring(odd_any, even_any):
                copy.start()

        @pl.when(odd_brick[0] == 1)
        def _():
            for copy in bring(even_any, odd_any):
                copy.start()

    if outer:
        brought = copies([(done_any.at[part(x)], out_ref.at[part(x)]) for x in (1, 2)], end_sems.at[pl.ds(6, 2)])
    for ref in fields + skews:
        for x in range(-2, 5):
            ref[base(x) + 256 : base(x) + 264, :] = jnp.zeros((8, 128), f32)
    ending = []
    for copy in listed:
        copy.wait()
    if step:
        for x in (0, 1, 2, 3):
            for copy in begun.pop(x):
                copy.wait()
        rows_ref[...] = jnp.where(lanes_of(emit_ref[...]), sheet_of(mine_ref[...], 256), 0.0)
        for j in range(128):
            cell = emit_smem[0, j]
            row = (cell >> 8) + 8 * (cell >> 16) + base(0)
            for h in (0, 1):
                spot = (pl.ds(row, 1), slice(None))
                fields[h][spot] = fields[h][spot] + rows_ref[j : j + 1, 128 * h : 128 * h + 128]
        pairs = [(plane(h, x), outs[-1].at[part(x), lanes(h)]) for x in (0, 1, 2, 3) for h in (0, 1)]
        ending += copies(pairs, end_sems.at[pl.ds(6, 8)])
    if step == 2:
        own = own_ref[...] > 0.5
        start = jnp.concatenate([start_ref[s, 8:9, :] for s in range(8)], axis=0)
        series = [start] + [s[...] for s in sample_refs]
        series = [jnp.sum(jnp.where(own, s, 0.0), axis=0, keepdims=True) for s in series]
        outs[0][...] = jnp.concatenate(series, axis=0).astype(jnp.bfloat16)

    lane = lax.broadcasted_iota(jnp.int32, (8, 128), 1)
    first_lane, last_lane = lane == 0, lane == 127

    def along_z(x):
        for t in range(32):
            rows = slice(base(x) + 8 * t, base(x) + 8 * t + 8)
            a, b = left_ref[rows, :], right_ref[rows, :]
            up_a, up_b = pltpu.roll(a, 127, 1), pltpu.roll(b, 127, 1)
            down_a, down_b = pltpu.roll(a, 1, 1), pltpu.roll(b, 1, 1)
            ahead = (jnp.where(last_lane, up_b, up_a), jnp.where(last_lane, 0.0, up_b))
            behind = (jnp.where(first_lane, 0.0, down_a), jnp.where(first_lane, down_a, down_b))
            for h in (0, 1):
                skews[h][rows, :] = ahead[h] - behind[h]
                if 0 <= x < 4:
                    sums[h][256 * x + 8 * t : 256 * x + 8 * t + 8, :] = ahead[h] + behind[h]

    ready = {1: (0, 1, 2), 2: (3,), 0: (0, 1, 2, 3, -1) if outer else (-1,), 3: (4,)}
    for x in order:
        if x == 0:
            for copy in bring(odd_any, even_any):
                copy.wait()
            if step:
                for side, plane_of, row in ((-1, 3, 0), (4, 0, 1)):
                    extra = spots(near_ref[1 + row : 2 + row, :], near_cells_ref[row : row + 1, :], plane_of)
                    rows = slice(base(side), base(side) + 256)
                    for h in (0, 1):
                        fields[h][rows, :] = fields[h][rows, :] + extra[:, 128 * h : 128 * h + 128]
            else:
                outs[3][0:1, :] = cells_ref[0:1, :]
                outs[3][1:2, :] = cells_ref[8:9, :]
        for k in ready[x]:
            for copy in begun.get(k, ()):
                copy.wait()
            along_z(k)
        for copy in started[x]:
            copy.wait()
        for t in range(32):
            near, up, down = (base(k) + 8 * t for k in (x, x + 1, x - 1))
            row = 256 * x + 8 * t
            rows = slice(row, row + 8)
            for h in (0, 1):
                field, skew = fields[h], skews[h]

                def at(ref, first):
                    return ref[first : first + 8, :]

                def across(ref, first):
                    return at(ref, first + 1) - at(ref, first - 1)

                columns = slice(128 * h, 128 * h + 128)
                d0, d1, d2 = (diag_ref[k, x, 8 * t : 8 * t + 8, columns] for k in range(3))
                c0, c1, c2 = (cross_ref[k, x, 8 * t : 8 * t + 8, columns] for k in range(3))
                mid = at(field, near)
                twice = mid + mid
                second = d0 * ((at(field, up) + at(field, down)) - twice)
                second = second + d1 * ((at(field, near + 1) + at(field, near - 1)) - twice)
                second = second + d2 * (sums[h][rows, :] - twice)
                mixed = c0 * (across(field, up) - across(field, down))
                mixed = mixed + c1 * (at(skew, up) - at(skew, down)) + c2 * across(skew, near)
                out_ref[rows, columns] = (twice - prev_ref[rows, columns]) + (second + 0.5 * mixed)
        if step < 2:
            ending += copies([(out_ref.at[part(x)], out_any.at[part(x)])], end_sems.at[pl.ds(x, 1)])
    if outer:
        for copy in brought:
            copy.wait()
    if step < 2 and not inner:
        value_ref, even_out, odd_out = outs[:3]
        even = out_ref.at[pl.ds(pl.multiple_of(768 - 768 * odd_brick[0], 256), 256)]
        odd = out_ref.at[pl.ds(pl.multiple_of(768 * odd_brick[0], 256), 256)]
        ending += copies([(even, even_out), (odd, odd_out)], end_sems.at[pl.ds(4, 2)])
        value_ref[...] = gather_row(out_ref, rec_smem, rec_ref[...], rows_ref)
    for copy in ending:
        copy.wait()


def wave(step, odd_brick, rec, cells, field, prev, diag, cross, edge_planes, added=(), record=(), done=(), planes=None):
    whole = (1024, 256)
    out_shape = [HBM(whole, f32), VMEM((1, 128), f32), HBM((256, 256), f32), HBM((256, 256), f32)]
    if step == 0:
        out_shape += [VMEM((8, 128), f32)]
    elif step == 1:
        out_shape += [HBM(whole, f32)]
    else:
        out_shape = [VMEM(whole, f32), VMEM((3, 128), jnp.bfloat16), HBM(whole, f32)]
    if not edge_planes:
        out_shape = out_shape[:1]
    coef = VMEM((3, 4, 256, 256), f32)
    half = VMEM((1592, 128), f32)
    inner = VMEM((1024, 128), f32)
    listed = SMEM((1, 128), jnp.int32)
    scratch = [half, half, VMEM(whole, f32), coef, coef, half, half, inner, inner]
    scratch += [VMEM((128, 256), f32), VMEM((16, 128), f32), listed, listed]
    scratch += [DMA((4, 9)), DMA((6,)), DMA((2,)), DMA((14,))]
    if step < 2:
        scratch.append(VMEM(whole, f32))
    return call(
        functools.partial(wave_kernel, step, planes or (1, 2, 0, 3)),
        tuple(out_shape),
        (16 << 20, 10 << 20),
        scalars=[odd_brick],
        arrays=[rec, *added, *record],
        far=[*cells, field, prev, diag, cross, *done],
        free=edge_planes,
        scratch=scratch,
        aliases={2 + len(added) + len(record) + 6: 0} if done else None,
        room=16,
    )


def add_at(cell_smem, cell_vec, value, target_ref, rows_ref):
    rows_ref[...] = jnp.where(lanes_of(cell_vec[...]), sheet_of(value, 256), 0.0)
    for j in range(128):
        row = cell_smem[0, j] >> 8
        target_ref[pl.ds(row, 1), :] = target_ref[pl.ds(row, 1), :] + rows_ref[j : j + 1, :]


def last_kernel(cell_smem, cell_vec, parts_ref, field_ref, out_any, rows_ref, sem):
    sums = [parts_ref[8 * k : 8 * k + 8, :] for k in range(4)]
    for k in range(4, 32):
        sums[k % 4] = sums[k % 4] + parts_ref[8 * k : 8 * k + 8, :]
    value = jnp.sum((sums[0] + sums[1]) + (sums[2] + sums[3]), axis=0, keepdims=True)
    add_at(cell_smem, cell_vec, value, field_ref, rows_ref)
    copy = pltpu.make_async_copy(field_ref, out_any, sem)
    copy.start()
    copy.wait()


def last_scatter(emit_cell, emit, parts, field):
    return call(
        last_kernel,
        HBM((1024, 256), f32),
        (1 << 20, 2 << 20),
        scalars=[emit_cell],
        arrays=[emit, parts, field],
        scratch=[VMEM((128, 256), f32), DMA],
    )


def spread_kernel(parts_ref, value_ref, out_ref):
    sums = [parts_ref[b] for b in range(4)]
    for b in range(4, 32):
        sums[b % 4] = sums[b % 4] + parts_ref[b]
    total = (sums[0] + sums[1]) + (sums[2] + sums[3])
    for s in range(8):
        out_ref[s, 0:8, :] = total[8:16]
        rows = [value_ref[...], total[s : s + 1], total[16 + s : 17 + s], jnp.zeros((5, 128), f32)]
        out_ref[s, 8:16, :] = jnp.concatenate(rows, axis=0)


def spread(parts, value):
    out = VMEM((8, 16, 128), f32)
    return call(spread_kernel, out, (1 << 15, 1 << 17), arrays=[parts, value])


def exchange(array, axis):
    return lax.all_to_all(array, axis, 0, 0, tiled=True)


def halos(even_plane, odd_plane):
    size = lax.axis_size("brick")
    even = lax.ppermute(even_plane, "brick", [(i, i ^ 1) for i in range(size)])
    odd = lax.ppermute(odd_plane, "brick", [(i, ((i + 1) ^ 1) - 1) for i in range(1, size - 1)])
    return even, odd


def steps(field_prev, field_now, diag, cross, green, delays, past, rec_cell, emit_cell):
    rank = lax.axis_index("shot").reshape(1)
    odd_brick = (lax.axis_index("brick") & 1).reshape(1)
    past = past[:, 0]

    current = field_now.reshape(1024, 256)
    before = field_prev.reshape(1024, 256)
    message, *planes, rec, emit, own, delay, green = first_message(
        rank, odd_brick, delays, rec_cell, emit_cell, past, current, green[0]
    )
    first = exchange(message, "shot")
    even, odd = halos(*planes)
    right = turn(green)
    cells = (rec_cell, emit_cell)
    inner = wave(0, odd_brick, rec, cells, current, before, diag, cross, (), planes=(1, 2))
    following, value, *planes, near_cells = wave(
        0, odd_brick, rec, cells, current, before, diag, cross, (even, odd), done=inner, planes=(0, 3)
    )
    partial = emission_start(first, delay, right)
    parts = exchange(partial, "brick")
    old = older(first, delay)
    message = spread(parts, value)

    answer = exchange(message, "shot")
    even, odd = halos(*planes)
    partial, mine, near, sample1 = samples_and_emission(1, answer, first, old, delay, own, [], right)
    parts = exchange(partial, "brick")
    added = (emit, mine, near, near_cells)
    earlier = current
    following, value, *planes, current = wave(
        1, odd_brick, rec, cells, following, earlier, diag, cross, (even, odd), added
    )
    message = spread(parts, value)

    answer = exchange(message, "shot")
    even, odd = halos(*planes)
    partial, mine, near, sample2 = samples_and_emission(2, answer, first, old, delay, own, [sample1], right)
    parts = exchange(partial.reshape(256, 1, 128), ("shot", "brick")).reshape(256, 128)
    added = (emit, mine, near, near_cells)
    record = (own, first, sample1, sample2)
    earlier = current
    following, recorded, current = wave(
        2, odd_brick, rec, cells, following, earlier, diag, cross, (even, odd), added, record
    )
    after = last_scatter(emit_cell, emit, parts, following)
    shape = field_now.shape
    return current.reshape(shape), after.reshape(shape), recorded[:, None]


def solution(mesh):
    return jax.shard_map(
        steps,
        mesh=mesh,
        in_specs=(
            P("shot", "brick", None, None),
            P("shot", "brick", None, None),
            P(None, "brick", None, None),
            P(None, "brick", None, None),
            P("shot", None, "brick"),
            P(),
            P(None, "shot", "brick"),
            P("shot", "brick"),
            P("shot", "brick"),
        ),
        out_specs=(
            P("shot", "brick", None, None),
            P("shot", "brick", None, None),
            P(None, "shot", "brick"),
        ),
        check_vma=False,
    )
```

```python
import functools

import jax
import jax.numpy as jnp
from jax import lax
from jax.experimental import pallas as pl
from jax.experimental.pallas import tpu as pltpu
from jax.sharding import PartitionSpec as P


VMEM = pltpu.VMEM
SMEM = pltpu.SMEM
HBM = pltpu.HBM
DMA = pltpu.SemaphoreType.DMA
f32 = jnp.float32


def spec(space):
    return pl.BlockSpec(memory_space=space)


def near(array):
    return pltpu.with_memory_space_constraint(array, pltpu.MemorySpace.VMEM)


def distant(array):
    return pltpu.with_memory_space_constraint(array, pltpu.MemorySpace.HBM)


def call(kernel, out_shape, work, scalars=(), arrays=(), far=(), free=(), scratch=(), aliases=None, room=2):
    flops, moved = work
    return pl.pallas_call(
        kernel,
        out_shape=out_shape,
        in_specs=[spec(SMEM)] * len(scalars) + [spec(VMEM)] * len(arrays) + [spec(HBM)] * len(far) + [spec(pl.ANY)] * len(free),
        out_specs=jax.tree.map(lambda o: spec(HBM if o.memory_space == HBM else VMEM), out_shape),
        scratch_shapes=list(scratch),
        input_output_aliases=aliases or {},
        cost_estimate=pl.CostEstimate(flops=flops, bytes_accessed=moved, transcendentals=0),
        compiler_params=pltpu.CompilerParams(vmem_limit_bytes=room << 20),
    )(*scalars, *[near(a) for a in arrays], *[distant(a) for a in far], *free)


def sheet_of(row, width):
    tall = jnp.transpose(jnp.broadcast_to(row, (128, 128)))
    return jnp.concatenate([tall] * (width // 128), axis=1)


def lanes_of(cells):
    column = sheet_of((cells & 255).astype(f32), 256).astype(jnp.int32)
    return lax.broadcasted_iota(jnp.int32, (128, 256), 1) == column


def gather_row(field_ref, cell_smem, cell_vec, rows_ref):
    for j in range(128):
        row = cell_smem[0, j] >> 8
        rows_ref[j : j + 1, :] = field_ref[pl.ds(row, 1), :]
    picked = jnp.where(lanes_of(cell_vec), rows_ref[...], 0.0)
    return jnp.sum(jnp.transpose(picked[:, :128] + picked[:, 128:]), axis=0, keepdims=True)


def copies(pairs, sems):
    started = [pltpu.make_async_copy(a, b, sems.at[k]) for k, (a, b) in enumerate(pairs)]
    for copy in started:
        copy.start()
    return started


def first_kernel(
    rank,
    odd_brick,
    field_any,
    past_any,
    rec_any,
    emit_any,
    delays_any,
    green_any,
    out_ref,
    even_ref,
    odd_ref,
    rec_ref,
    emit_ref,
    own_ref,
    delay_ref,
    green_ref,
    field_ref,
    rows_ref,
    past_ref,
    cell_smem,
    delays,
    sems,
):
    pairs = [(rec_any, cell_smem), (delays_any, delays), (field_any, field_ref), (past_any, past_ref)]
    started = copies(pairs + [(rec_any, rec_ref), (emit_any, emit_ref), (green_any, green_ref)], sems)
    own = lax.broadcasted_iota(jnp.int32, (8, 128), 0) == rank[0]
    own_ref[...] = jnp.where(own, 1.0, 0.0)
    for copy in started[:-1]:
        copy.wait()
    delay_ref[...] = jnp.full((8, 128), delays[rank[0]], jnp.int32)
    sample = gather_row(field_ref, cell_smem, rec_ref[...], rows_ref)
    rows = [past_ref[...].astype(f32), sample.astype(jnp.bfloat16).astype(f32)]
    rows += [rec_ref[...].astype(f32), emit_ref[...].astype(f32), jnp.zeros((5, 128), f32)]
    message = jnp.concatenate(rows, axis=0)
    for s in range(8):
        out_ref[s] = message
    edges(odd_brick, field_ref, even_ref, odd_ref)
    cells = jnp.broadcast_to(emit_ref[...].astype(f32), (8, 128))
    for ref in (even_ref, odd_ref):
        ref[256:264, 0:128] = cells
        ref[256:264, 128:256] = cells
    started[-1].wait()


def edges(odd_brick, field_ref, even_ref, odd_ref):
    even_ref[0:256, :] = field_ref[pl.ds(pl.multiple_of(768 - 768 * odd_brick[0], 256), 256), :]
    odd_ref[0:256, :] = field_ref[pl.ds(pl.multiple_of(768 * odd_brick[0], 256), 256), :]


def first_message(rank, odd_brick, delays, rec_cell, emit_cell, past, field, green):
    plane = VMEM((264, 256), f32)
    row = VMEM((1, 128), jnp.int32)
    return call(
        first_kernel,
        (
            VMEM((8, 16, 128), f32),
            plane,
            plane,
            row,
            row,
            VMEM((8, 128), f32),
            VMEM((8, 128), jnp.int32),
            VMEM((4096, 128), jnp.bfloat16),
        ),
        (1 << 20, 1 << 19),
        scalars=[rank, odd_brick],
        far=[field, past, rec_cell, emit_cell, delays, green],
        scratch=[
            VMEM((1024, 256), f32),
            VMEM((128, 256), f32),
            VMEM((8, 128), jnp.bfloat16),
            SMEM((1, 128), jnp.int32),
            SMEM((8,), jnp.int32),
            DMA((7,)),
        ],
        room=3,
    )


def turn_kernel(green_ref, right_ref):
    for b in range(32):
        at = slice(b * 128, (b + 1) * 128)
        right_ref[:, at] = jnp.transpose(green_ref[at, :])


def turn(green):
    return call(turn_kernel, VMEM((128, 4096), jnp.bfloat16), (1 << 20, 1 << 20), arrays=[green])


def older_kernel(first_ref, delay_ref, old_ref):
    for moment in (1, 2):
        old_ref[moment - 1] = old_samples(first_ref, 8 + moment - delay_ref[...])


def older(first, delay):
    out = VMEM((2, 8, 128), f32)
    return call(older_kernel, out, (1 << 20, 1 << 18), arrays=[first, delay])


def matches(first_ref):
    blocks = []
    for s in range(8):
        rec = first_ref[s, 9:10, :]
        emit = first_ref[s, 10:11, :]
        same = sheet_of(emit, 128) == jnp.broadcast_to(rec, (128, 128))
        blocks.append(jnp.where(same, 1.0, 0.0).astype(jnp.bfloat16))
    return jnp.concatenate(blocks, axis=0)


def multiply(chosen, right_ref, out_ref):
    product = jnp.dot(chosen.astype(jnp.bfloat16), right_ref[...], preferred_element_type=f32)
    if out_ref.shape[0] == 256:
        for b in range(32):
            out_ref[pl.ds(b, 8, stride=32), :] = product[:, b * 128 : (b + 1) * 128]
        return
    for b in range(32):
        block = product[:, b * 128 : (b + 1) * 128]
        out_ref[b, 8:16, :] = block
        if b < 31:
            out_ref[b + 1, 0:8, :] = block
        if b > 0:
            out_ref[b - 1, 16:24, :] = block
    out_ref[0, 0:8, :] = jnp.zeros((8, 128), f32)
    out_ref[31, 16:24, :] = jnp.zeros((8, 128), f32)


def old_samples(first_ref, where):
    chosen = jnp.zeros((8, 128), f32)
    for k in range(9):
        series = jnp.concatenate([first_ref[s, k : k + 1, :] for s in range(8)], axis=0)
        chosen = jnp.where(where == k, series, chosen)
    return chosen


def start_kernel(first_ref, delay_ref, right_ref, out_ref):
    multiply(old_samples(first_ref, 8 - delay_ref[...]), right_ref, out_ref)


def emission_start(first, delay, right):
    out = VMEM((32, 24, 128), f32)
    return call(start_kernel, out, (8 << 20, 1 << 20), arrays=[first, delay, right])


def samples_kernel(moment, message_ref, first_ref, old_ref, delay_ref, own_ref, *refs):
    *newer_refs, right_ref, out_ref, mine_ref, near_ref, sample_ref = refs
    total = message_ref[0, 0:8, :]
    for lag in range(1, 8):
        total = total + message_ref[lag, 0:8, :]
    near = message_ref[0, 8:16, :]
    for lag in range(1, 8):
        near = near + message_ref[lag, 8:16, :]
    near_ref[...] = near
    values = jnp.concatenate([message_ref[s, 8:9, :] for s in range(8)], axis=0)
    wide = jnp.concatenate([total] * 8, axis=1)
    block = lax.broadcasted_iota(jnp.int32, (8, 1024), 1) >> 7
    wide = jnp.where(block == lax.broadcasted_iota(jnp.int32, (8, 1024), 0), wide, 0.0)
    high = wide.astype(jnp.bfloat16)
    rest = wide - high.astype(f32)
    middle = rest.astype(jnp.bfloat16)
    low = (rest - middle.astype(f32)).astype(jnp.bfloat16)
    parts = jnp.concatenate([high, middle, low], axis=0)
    added = jnp.dot(parts, matches(first_ref), preferred_element_type=f32)
    values = values + ((added[16:24] + added[8:16]) + added[0:8])
    sample = values.astype(jnp.bfloat16).astype(f32)
    delay = delay_ref[...]
    chosen = old_ref[moment - 1]
    for k, newer_ref in enumerate(newer_refs):
        chosen = jnp.where(delay == moment - 1 - k, newer_ref[...], chosen)
    chosen = jnp.where(delay == 0, sample, chosen)
    multiply(chosen, right_ref, out_ref)
    sample_ref[...] = sample
    mine_ref[...] = jnp.sum(jnp.where(own_ref[...] > 0.5, total, 0.0), axis=0, keepdims=True)


def samples_and_emission(moment, message, first, old, delay, own, newer, right):
    return call(
        functools.partial(samples_kernel, moment),
        (VMEM((32, 24, 128) if moment == 1 else (256, 128), f32), VMEM((1, 128), f32), VMEM((8, 128), f32), VMEM((8, 128), f32)),
        (8 << 20, 1 << 20),
        arrays=[message, first, old, delay, own, *newer, right],
    )


def spots(values, cells, plane):
    cells = cells.astype(jnp.int32)
    values = jnp.where((cells >> 16) == plane, values, 0.0)
    column = sheet_of(((cells >> 8) & 255).astype(f32), 256).astype(jnp.int32)
    rows = jnp.where(lax.broadcasted_iota(jnp.int32, (128, 256), 1) == column, 1.0, 0.0).astype(jnp.bfloat16)
    rest = jnp.where(lanes_of(cells), sheet_of(values, 256), 0.0)
    terms = []
    for _ in range(3):
        term = rest.astype(jnp.bfloat16)
        rest = rest - term.astype(f32)
        terms.append(lax.dot_general(rows, term, (((0,), (0,)), ((), ())), preferred_element_type=f32))
    return (terms[2] + terms[1]) + terms[0]


def base(x):
    return 8 + 264 * (x + 1)


def wave_kernel(step, planes, odd_brick, rec_ref, *refs):
    refs = list(refs)

    def take(count):
        taken = refs[:count]
        del refs[:count]
        return taken

    emit_ref, mine_ref, near_ref, near_cells_ref = take(4) if step else [None] * 4
    own_ref, start_ref, *sample_refs = take(4) if step == 2 else [None] * 4
    inner, outer = planes == (1, 2), planes == (0, 3)
    rec_any, emit_any, field_any, prev_any, diag_any, cross_any = take(6)
    (done_any,) = take(1) if outer else [None]
    even_any, odd_any = take(2) if not inner else [None] * 2
    out_any, *outs = take(1 + step if inner else 5 - step if outer else 5 if step < 2 else 3)
    left_ref, right_ref, prev_ref, diag_ref, cross_ref, left_skew, right_skew, left_sum, right_sum = take(9)
    rows_ref, cells_ref, rec_smem, emit_smem, sems, edge_sems, cell_sems, end_sems = take(8)
    (out_ref,) = take(1) if step < 2 else [out_any]
    order = planes
    fields, skews, sums = (left_ref, right_ref), (left_skew, right_skew), (left_sum, right_sum)

    def part(x):
        return pl.ds(256 * x, 256)

    def lanes(h):
        return pl.ds(128 * h, 128)

    def plane(h, x):
        return fields[h].at[pl.ds(base(x), 256)]

    listed = copies([(rec_any, rec_smem), (emit_any, emit_smem)], cell_sems)
    begun = {}
    for x in (0, 1, 2, 3):
        begun[x] = copies([(field_any.at[part(x), lanes(h)], plane(h, x)) for h in (0, 1)], sems.at[x, pl.ds(7, 2)])
    started = {}
    for x in order:
        pairs = [(diag_any.at[k, x], diag_ref.at[k, x]) for k in range(3)]
        pairs += [(cross_any.at[k, x], cross_ref.at[k, x]) for k in range(3)]
        started[x] = copies([(prev_any.at[part(x)], prev_ref.at[part(x)])] + pairs, sems.at[x])

    def bring(low, high):
        pairs = [(low.at[pl.ds(0, 256), lanes(h)], plane(h, -1)) for h in (0, 1)]
        pairs += [(high.at[pl.ds(0, 256), lanes(h)], plane(h, 4)) for h in (0, 1)]
        if step == 0:
            pairs += [(low.at[pl.ds(256, 8), lanes(0)], cells_ref.at[pl.ds(0, 8)])]
            pairs += [(high.at[pl.ds(256, 8), lanes(0)], cells_ref.at[pl.ds(8, 8)])]
        return [pltpu.make_async_copy(a, b, edge_sems.at[k]) for k, (a, b) in enumerate(pairs)]

    if not inner:

        @pl.when(odd_brick[0] == 0)
        def _():
            for copy in bring(odd_any, even_any):
                copy.start()

        @pl.when(odd_brick[0] == 1)
        def _():
            for copy in bring(even_any, odd_any):
                copy.start()

    if outer:
        brought = copies([(done_any.at[part(x)], out_ref.at[part(x)]) for x in (1, 2)], end_sems.at[pl.ds(6, 2)])
    for ref in fields + skews:
        for x in range(-2, 5):
            ref[base(x) + 256 : base(x) + 264, :] = jnp.zeros((8, 128), f32)
    ending = []
    for copy in listed:
        copy.wait()
    if step and not outer:
        for x in (0, 1, 2, 3):
            for copy in begun.pop(x):
                copy.wait()
        rows_ref[...] = jnp.where(lanes_of(emit_ref[...]), sheet_of(mine_ref[...], 256), 0.0)
        for j in range(128):
            cell = emit_smem[0, j]
            row = (cell >> 8) + 8 * (cell >> 16) + base(0)
            for h in (0, 1):
                spot = (pl.ds(row, 1), slice(None))
                fields[h][spot] = fields[h][spot] + rows_ref[j : j + 1, 128 * h : 128 * h + 128]
        pairs = [(plane(h, x), outs[-1].at[part(x), lanes(h)]) for x in (0, 1, 2, 3) for h in (0, 1)]
        ending += copies(pairs, end_sems.at[pl.ds(6, 8)])
    if step == 2:
        own = own_ref[...] > 0.5
        start = jnp.concatenate([start_ref[s, 8:9, :] for s in range(8)], axis=0)
        series = [start] + [s[...] for s in sample_refs]
        series = [jnp.sum(jnp.where(own, s, 0.0), axis=0, keepdims=True) for s in series]
        outs[0][...] = jnp.concatenate(series, axis=0).astype(jnp.bfloat16)

    lane = lax.broadcasted_iota(jnp.int32, (8, 128), 1)
    first_lane, last_lane = lane == 0, lane == 127

    def along_z(x):
        for t in range(32):
            rows = slice(base(x) + 8 * t, base(x) + 8 * t + 8)
            a, b = left_ref[rows, :], right_ref[rows, :]
            up_a, up_b = pltpu.roll(a, 127, 1), pltpu.roll(b, 127, 1)
            down_a, down_b = pltpu.roll(a, 1, 1), pltpu.roll(b, 1, 1)
            ahead = (jnp.where(last_lane, up_b, up_a), jnp.where(last_lane, 0.0, up_b))
            behind = (jnp.where(first_lane, 0.0, down_a), jnp.where(first_lane, down_a, down_b))
            for h in (0, 1):
                skews[h][rows, :] = ahead[h] - behind[h]
                if 0 <= x < 4:
                    sums[h][256 * x + 8 * t : 256 * x + 8 * t + 8, :] = ahead[h] + behind[h]

    ready = {1: (0, 1, 2), 2: (3,), 0: (0, 1, 2, 3, -1) if outer else (-1,), 3: (4,)}
    for x in order:
        if x == 0:
            for copy in bring(odd_any, even_any):
                copy.wait()
            if step:
                for side, plane_of, row in ((-1, 3, 0), (4, 0, 1)):
                    extra = spots(near_ref[1 + row : 2 + row, :], near_cells_ref[row : row + 1, :], plane_of)
                    rows = slice(base(side), base(side) + 256)
                    for h in (0, 1):
                        fields[h][rows, :] = fields[h][rows, :] + extra[:, 128 * h : 128 * h + 128]
            else:
                outs[3][0:1, :] = cells_ref[0:1, :]
                outs[3][1:2, :] = cells_ref[8:9, :]
        for k in ready[x]:
            for copy in begun.get(k, ()):
                copy.wait()
            along_z(k)
        for copy in started[x]:
            copy.wait()
        for t in range(32):
            near, up, down = (base(k) + 8 * t for k in (x, x + 1, x - 1))
            row = 256 * x + 8 * t
            rows = slice(row, row + 8)
            for h in (0, 1):
                field, skew = fields[h], skews[h]

                def at(ref, first):
                    return ref[first : first + 8, :]

                def across(ref, first):
                    return at(ref, first + 1) - at(ref, first - 1)

                columns = slice(128 * h, 128 * h + 128)
                d0, d1, d2 = (diag_ref[k, x, 8 * t : 8 * t + 8, columns] for k in range(3))
                c0, c1, c2 = (cross_ref[k, x, 8 * t : 8 * t + 8, columns] for k in range(3))
                mid = at(field, near)
                twice = mid + mid
                second = d0 * ((at(field, up) + at(field, down)) - twice)
                second = second + d1 * ((at(field, near + 1) + at(field, near - 1)) - twice)
                second = second + d2 * (sums[h][rows, :] - twice)
                mixed = c0 * (across(field, up) - across(field, down))
                mixed = mixed + c1 * (at(skew, up) - at(skew, down)) + c2 * across(skew, near)
                out_ref[rows, columns] = (twice - prev_ref[rows, columns]) + (second + 0.5 * mixed)
        if step < 2:
            ending += copies([(out_ref.at[part(x)], out_any.at[part(x)])], end_sems.at[pl.ds(x, 1)])
    if outer:
        for copy in brought:
            copy.wait()
    if step < 2 and not inner:
        value_ref, even_out, odd_out = outs[:3]
        even = out_ref.at[pl.ds(pl.multiple_of(768 - 768 * odd_brick[0], 256), 256)]
        odd = out_ref.at[pl.ds(pl.multiple_of(768 * odd_brick[0], 256), 256)]
        ending += copies([(even, even_out), (odd, odd_out)], end_sems.at[pl.ds(4, 2)])
        value_ref[...] = gather_row(out_ref, rec_smem, rec_ref[...], rows_ref)
    for copy in ending:
        copy.wait()


def wave(step, odd_brick, rec, cells, field, prev, diag, cross, edge_planes, added=(), record=(), done=(), planes=None):
    whole = (1024, 256)
    out_shape = [HBM(whole, f32), VMEM((1, 128), f32), HBM((256, 256), f32), HBM((256, 256), f32)]
    if step == 0:
        out_shape += [VMEM((8, 128), f32)]
    elif step == 1:
        out_shape += [HBM(whole, f32)]
    else:
        out_shape = [VMEM(whole, f32), VMEM((3, 128), jnp.bfloat16), HBM(whole, f32)]
    if step == 1 and planes:
        out_shape = out_shape[:4] if edge_planes else out_shape[:1] + out_shape[4:]
    elif not edge_planes:
        out_shape = out_shape[:1]
    coef = VMEM((3, 4, 256, 256), f32)
    half = VMEM((1592, 128), f32)
    inner = VMEM((1024, 128), f32)
    listed = SMEM((1, 128), jnp.int32)
    scratch = [half, half, VMEM(whole, f32), coef, coef, half, half, inner, inner]
    scratch += [VMEM((128, 256), f32), VMEM((16, 128), f32), listed, listed]
    scratch += [DMA((4, 9)), DMA((6,)), DMA((2,)), DMA((14,))]
    if step < 2:
        scratch.append(VMEM(whole, f32))
    return call(
        functools.partial(wave_kernel, step, planes or (1, 2, 0, 3)),
        tuple(out_shape),
        (16 << 20, 10 << 20),
        scalars=[odd_brick],
        arrays=[rec, *added, *record],
        far=[*cells, field, prev, diag, cross, *done],
        free=edge_planes,
        scratch=scratch,
        aliases={2 + len(added) + len(record) + 6: 0} if done else None,
        room=16,
    )


def add_at(cell_smem, cell_vec, value, target_ref, rows_ref):
    rows_ref[...] = jnp.where(lanes_of(cell_vec[...]), sheet_of(value, 256), 0.0)
    for j in range(128):
        row = cell_smem[0, j] >> 8
        target_ref[pl.ds(row, 1), :] = target_ref[pl.ds(row, 1), :] + rows_ref[j : j + 1, :]


def last_kernel(cell_smem, cell_vec, parts_ref, field_ref, out_any, rows_ref, sem):
    sums = [parts_ref[8 * k : 8 * k + 8, :] for k in range(4)]
    for k in range(4, 32):
        sums[k % 4] = sums[k % 4] + parts_ref[8 * k : 8 * k + 8, :]
    value = jnp.sum((sums[0] + sums[1]) + (sums[2] + sums[3]), axis=0, keepdims=True)
    add_at(cell_smem, cell_vec, value, field_ref, rows_ref)
    copy = pltpu.make_async_copy(field_ref, out_any, sem)
    copy.start()
    copy.wait()


def last_scatter(emit_cell, emit, parts, field):
    return call(
        last_kernel,
        HBM((1024, 256), f32),
        (1 << 20, 2 << 20),
        scalars=[emit_cell],
        arrays=[emit, parts, field],
        scratch=[VMEM((128, 256), f32), DMA],
    )


def spread_kernel(parts_ref, value_ref, out_ref):
    sums = [parts_ref[b] for b in range(4)]
    for b in range(4, 32):
        sums[b % 4] = sums[b % 4] + parts_ref[b]
    total = (sums[0] + sums[1]) + (sums[2] + sums[3])
    for s in range(8):
        out_ref[s, 0:8, :] = total[8:16]
        rows = [value_ref[...], total[s : s + 1], total[16 + s : 17 + s], jnp.zeros((5, 128), f32)]
        out_ref[s, 8:16, :] = jnp.concatenate(rows, axis=0)


def spread(parts, value):
    out = VMEM((8, 16, 128), f32)
    return call(spread_kernel, out, (1 << 15, 1 << 17), arrays=[parts, value])


def exchange(array, axis):
    return lax.all_to_all(array, axis, 0, 0, tiled=True)


def halos(even_plane, odd_plane):
    size = lax.axis_size("brick")
    even = lax.ppermute(even_plane, "brick", [(i, i ^ 1) for i in range(size)])
    odd = lax.ppermute(odd_plane, "brick", [(i, ((i + 1) ^ 1) - 1) for i in range(1, size - 1)])
    return even, odd


def steps(field_prev, field_now, diag, cross, green, delays, past, rec_cell, emit_cell):
    rank = lax.axis_index("shot").reshape(1)
    odd_brick = (lax.axis_index("brick") & 1).reshape(1)
    past = past[:, 0]

    current = field_now.reshape(1024, 256)
    before = field_prev.reshape(1024, 256)
    message, *planes, rec, emit, own, delay, green = first_message(
        rank, odd_brick, delays, rec_cell, emit_cell, past, current, green[0]
    )
    first = exchange(message, "shot")
    even, odd = halos(*planes)
    right = turn(green)
    cells = (rec_cell, emit_cell)
    inner = wave(0, odd_brick, rec, cells, current, before, diag, cross, (), planes=(1, 2))
    following, value, *planes, near_cells = wave(
        0, odd_brick, rec, cells, current, before, diag, cross, (even, odd), done=inner, planes=(0, 3)
    )
    partial = emission_start(first, delay, right)
    parts = exchange(partial, "brick")
    old = older(first, delay)
    message = spread(parts, value)

    answer = exchange(message, "shot")
    even, odd = halos(*planes)
    partial, mine, near, sample1 = samples_and_emission(1, answer, first, old, delay, own, [], right)
    parts = exchange(partial, "brick")
    added = (emit, mine, near, near_cells)
    earlier = current
    inner, current = wave(1, odd_brick, rec, cells, following, earlier, diag, cross, (), added, planes=(1, 2))
    following, value, *planes = wave(
        1, odd_brick, rec, cells, current, earlier, diag, cross, (even, odd), added, done=(inner,), planes=(0, 3)
    )
    message = spread(parts, value)

    answer = exchange(message, "shot")
    even, odd = halos(*planes)
    partial, mine, near, sample2 = samples_and_emission(2, answer, first, old, delay, own, [sample1], right)
    parts = exchange(partial.reshape(256, 1, 128), ("shot", "brick")).reshape(256, 128)
    added = (emit, mine, near, near_cells)
    record = (own, first, sample1, sample2)
    earlier = current
    following, recorded, current = wave(
        2, odd_brick, rec, cells, following, earlier, diag, cross, (even, odd), added, record
    )
    after = last_scatter(emit_cell, emit, parts, following)
    shape = field_now.shape
    return current.reshape(shape), after.reshape(shape), recorded[:, None]


def solution(mesh):
    return jax.shard_map(
        steps,
        mesh=mesh,
        in_specs=(
            P("shot", "brick", None, None),
            P("shot", "brick", None, None),
            P(None, "brick", None, None),
            P(None, "brick", None, None),
            P("shot", None, "brick"),
            P(),
            P(None, "shot", "brick"),
            P("shot", "brick"),
            P("shot", "brick"),
        ),
        out_specs=(
            P("shot", "brick", None, None),
            P("shot", "brick", None, None),
            P(None, "shot", "brick"),
        ),
        check_vma=False,
    )
```
